256 devices in a mesh: gx: 16 (over z, x_hi), gy: 16 (over x_lo, y, core).
Axes of the slice: x: 4 (x_hi: 2, x_lo: 2; x = x_hi * 2 + x_lo), y: 4, z: 8, core: 2. Of those that a mesh axis runs over, the one named last changes fastest.
Arguments:
- electric: float32 [2, 3, 512, 32768], P(None, None, 'gx', 'gy'), may hold values from -6 to 6
- magnetic: float32 [2, 3, 512, 32768], P(None, None, 'gx', 'gy'), may hold values from -6 to 6
- permittivity: float32 [512, 32768], P('gx', 'gy'), may hold values from 1 to 12
- source_profile: float32 [2, 512, 1024], P(None, 'gx', 'gy'), may hold values from -6 to 6
- source_plane: int32 [2, 512], P(None, 'gx'), may hold values from 0 to 31
- block_owner: int32 [16, 16, 16, 1], P('gx', 'gy'), may hold values from 0 to 15; in each aligned block of 16 rows (0 to 15, 16 to 31, ..., all dimensions but the last counted through in order) at most 2 rows name the same one
- design_slot: int32 [16, 16, 16], P('gx', 'gy'), may hold values from 0 to 3
- filter_matrix: float32 [128, 128], replicated, may hold values from -0.5 to 0.5
Outputs:
- electric_out: float32 [2, 3, 512, 32768], P(None, None, 'gx', 'gy')
- magnetic_out: float32 [2, 3, 512, 32768], P(None, None, 'gx', 'gy')
- design_grad: float32 [16, 64, 128], P('gx', 'gy')
The draws below stay inside these ranges and needn't reach their ends.
Inputs may be any that keep to these rules, and one draw needn't show every extreme that they name: `block_owner`: among the 16 blocks of one device no owner appears more than 2 times, and some owner appears exactly 2 times on some device.
All inputs are finite; a program needn't handle non-finite values.
Results may differ from the reference program's by a relative error of at most 0.00016.
Values sent between devices are 32-bit elements; how exact they have to be, the bound alone decides.
No kernel may reach another device: no remote copies, remote signals or barrier semaphores. Data moves between devices by JAX's collectives and lax.ppermute only.
A program may use at most 192 MiB of HBM per device.

```python
import math
import jax
import jax.numpy as jnp
import numpy as np
from jax import lax

CY = 64
NZ = 32
STEPS = 12
BROWS = 2
DB_DEV = 4
NX = 512
NY = 1024
NB_DEV = 16
CAP = 2
BCELLS = 128
DESIGN = 64
N_GX = 16
N_GY = 16


def touch_ends(values, rng, least, top_value):
    index_at = [jax.random.randint(jax.random.fold_in(rng, axis), (), 0, length) for axis, length in enumerate(values.shape)]
    longest = values.shape.index(max(values.shape))
    neighbour = index_at[:longest] + [(index_at[longest] + 1) % values.shape[longest]] + index_at[longest + 1:]
    return values.at[tuple(index_at)].set(least).at[tuple(neighbour)].set(top_value)


def block_levels(rng, extent, split, least, high):
    def one(axis_at, blocks):
        steps = jax.random.uniform(jax.random.fold_in(jax.random.fold_in(rng, 6), axis_at), (blocks,), jnp.float32, least / len(split), high / len(split))
        return jnp.repeat(jnp.exp(steps), extent[axis_at] // blocks).reshape((-1,) + (1,) * (len(extent) - axis_at - 1))

    loudness = one(*split[0])
    for cut in split[1:]:
        loudness = loudness * one(*cut)
    return loudness


def deal_out(own_key, own, number, rows, number_of, top, most, skew):
    order = jax.random.permutation(own_key, number_of)
    packed, common = shares(number_of, rows * top, most, skew, True), shares(number_of, rows * top, most, skew, False)
    places = jnp.arange(number_of)

    def named(lengths, rotation):
        used = int((lengths > 0).sum())
        fixed = max(1, used // 4)
        moved = fixed + (places - fixed + rotation * (used - fixed)) % max(1, number_of - fixed)
        return jnp.zeros((number_of,), jnp.int32).at[order[jnp.where(places < fixed, places, moved)]].set(jnp.asarray(lengths, jnp.int32))

    lengths = jnp.where(number % 4 == 0, named(packed, number // 4), named(common, number - number // 4 - 1))
    mixed = jax.random.permutation(jax.random.fold_in(own, 3), number_of)
    source_of, sink = mixed[0:number_of // 2 * 2:2], mixed[1:number_of // 2 * 2:2]
    margin = jnp.minimum(lengths[source_of] - 1, most - lengths[sink]) // 2
    margin = jnp.where((source_of == order[0]) | (sink == order[0]) | (lengths[sink] == 0), 0, jnp.maximum(margin, 0))
    moved = jax.random.randint(jax.random.fold_in(own, 4), (number_of // 2,), 0, 1 << 20) % (margin + 1)
    lengths = lengths.at[source_of].add(-moved).at[sink].add(moved)
    labels = jnp.searchsorted(jnp.cumsum(lengths), jnp.arange(rows * top), side="right").astype(jnp.int32)
    grid = labels.reshape(top, rows).T
    grid = grid[jax.random.permutation(jax.random.fold_in(own, 1), rows)]
    rotation = jax.random.randint(jax.random.fold_in(own, 2), (rows, 1), 0, top)
    return jnp.take_along_axis(grid, (jnp.arange(top)[None, :] + rotation) % top, axis=1)


def shares(count, total, limit, skew, full):
    portions = [(1 << 20) // math.isqrt(standing ** skew) + 1 for standing in range(1, count + 1)]
    largest = limit if full else min(limit, max(-(-total // count), total * portions[0] // sum(portions)))
    least = 1 if total - largest >= count - 1 else 0
    holding, spare = [largest] + [least] * (count - 1), total - largest - least * (count - 1)
    while spare > 0:
        free = [i for i in range(1, count) if holding[i] < largest] or [i for i in range(1, count) if holding[i] < limit]
        mass, left = sum([portions[i] for i in free]), spare
        for i in free:
            extra = min(limit - holding[i], max(1, left * portions[i] // mass), spare)
            holding[i] = holding[i] + extra
            spare = spare - extra
    return np.array(holding)


def noise(rng, dims, width, bound, pieces=(), kind=jnp.bfloat16):
    array = jax.random.normal(rng, dims, jnp.float32) * width
    if len(pieces) > 0:
        array = block_levels(rng, dims, pieces, -0.22, 0.18) * array
    return jnp.clip(array, min=-bound, max=bound).astype(kind)


def setup_inputs(seed: int = 0) -> dict:
    streams_of = jax.random.split(jax.random.key(seed), 9)
    electric = noise(streams_of[0], (2, 3, NX, NY * NZ), 1.0, 6.0, ((2, 16), (3, 16)), jnp.float32)
    magnetic = noise(streams_of[1], (2, 3, NX, NY * NZ), 1.0, 6.0, ((2, 16), (3, 16)), jnp.float32)
    permittivity = jnp.clip(1.0 + 11.0 * jax.random.uniform(streams_of[2], (NX, NY * NZ), jnp.float32) ** block_levels(streams_of[2], (NX, NY * NZ), ((0, 16), (1, 16)), -0.2, 0.2), 1.0, 12.0)
    source_profile = noise(streams_of[3], (2, NX, NY), 1.0, 6.0, ((1, 16), (2, 16)), jnp.float32)
    source_plane = touch_ends(jax.random.randint(streams_of[4], (2, NX), 0, NZ), jax.random.fold_in(streams_of[4], 1), 0, NZ - 1).astype(jnp.int32)
    block_owner_keys = jax.random.split(jax.random.fold_in(streams_of[5], 1), N_GX * N_GY * NB_DEV // NB_DEV)
    block_owner_turns = jax.random.permutation(jax.random.fold_in(streams_of[5], 3), N_GX * N_GY * NB_DEV // NB_DEV)
    block_owner = jax.vmap(lambda own, number: deal_out(jax.random.fold_in(streams_of[5], 2), own, number, NB_DEV, N_GY, 1, CAP, 2))(block_owner_keys, block_owner_turns).reshape((N_GX, N_GY, NB_DEV, 1))
    design_slot = touch_ends(jax.random.randint(streams_of[6], (N_GX, N_GY, NB_DEV), 0, DB_DEV), jax.random.fold_in(streams_of[6], 1), 0, DB_DEV - 1).astype(jnp.int32)
    filter_matrix = noise(streams_of[7], (BCELLS, BCELLS), BCELLS ** -0.5, 0.5, (), jnp.float32)
    return dict(electric=electric, magnetic=magnetic, permittivity=permittivity, source_profile=source_profile, source_plane=source_plane, block_owner=block_owner, design_slot=design_slot, filter_matrix=filter_matrix)


time_step = 0.5
omega_source = 1.3


def upper_z(field, keep):
    return jnp.concatenate([field[..., 1:], jnp.zeros_like(field[..., :1])], -1) * keep


def lower_z(field, keep):
    return jnp.concatenate([jnp.zeros_like(field[..., :1]), field[..., :-1]], -1) * keep


def reference(electric, magnetic, permittivity, source_profile, source_plane, block_owner, design_slot, filter_matrix):
    length = NY * NZ
    position = jnp.arange(length, dtype=jnp.int32) % NZ
    keep_up = (position != NZ - 1).astype(jnp.float32)
    keep_down = (position != 0).astype(jnp.float32)
    inverse = 1.0 / permittivity
    level = jnp.arange(NZ, dtype=jnp.int32)
    source = (source_profile[:, :, :, None] * (level[None, None, None, :] == source_plane.astype(jnp.int32)[:, :, None, None]).astype(jnp.float32)).reshape(2, NX, length)
    accum = jnp.zeros((NX, length), jnp.float32)
    field_e, field_h = electric, magnetic
    for step in range(STEPS):
        ex, ey, ez = field_e[:, 0], field_e[:, 1], field_e[:, 2]
        curl_x = (jnp.roll(ez, -NZ, axis=-1) - ez) - (upper_z(ey, keep_up) - ey)
        curl_y = (upper_z(ex, keep_up) - ex) - (jnp.roll(ez, -1, axis=1) - ez)
        curl_z = (jnp.roll(ey, -1, axis=1) - ey) - (jnp.roll(ex, -NZ, axis=-1) - ex)
        field_h = field_h - time_step * jnp.stack([curl_x, curl_y, curl_z], 1)
        hx, hy, hz = field_h[:, 0], field_h[:, 1], field_h[:, 2]
        cx = (hz - jnp.roll(hz, NZ, axis=-1)) - (hy - lower_z(hy, keep_down))
        cy = (hx - lower_z(hx, keep_down)) - (hz - jnp.roll(hz, 1, axis=1))
        cz = (hy - jnp.roll(hy, 1, axis=1)) - (hx - jnp.roll(hx, NZ, axis=-1))
        wave = jnp.sin(jnp.asarray(step + 1, jnp.float32) * (omega_source * time_step))
        new_x = ex + time_step * inverse * cx + time_step * wave * source
        new_y = ey + time_step * inverse * cy
        new_z = ez + time_step * inverse * cz
        field_e = jnp.stack([new_x, new_y, new_z], 1)
        accum = accum + (new_x[0] * new_x[1] + new_y[0] * new_y[1] + new_z[0] * new_z[1])
    total = accum.reshape(NX, NY, NZ).sum(-1) / (STEPS * NZ)
    blocks = total.reshape(N_GX, NB_DEV, BROWS, N_GY, CY).transpose(0, 3, 1, 2, 4).reshape(N_GX * N_GY * NB_DEV, BCELLS)
    row_ids = jnp.arange(N_GX, dtype=jnp.int32)[:, None, None] * DESIGN
    ids = (row_ids + block_owner[..., 0].astype(jnp.int32) * DB_DEV + design_slot.astype(jnp.int32)).reshape(-1)
    design = jax.ops.segment_sum(blocks, ids, num_segments=N_GX * DESIGN)
    result = jnp.dot(design, filter_matrix, precision=lax.Precision.HIGHEST, preferred_element_type=jnp.float32)
    return field_e, field_h, result.reshape(N_GX, DESIGN, BCELLS)
```

```python
import functools

import jax
import jax.numpy as jnp
import numpy as np
from jax import lax
from jax.experimental import pallas as pl
from jax.experimental.pallas import tpu as pltpu
from jax.sharding import PartitionSpec as P

NZ = 32
STEPS = 12
BROWS = 2
DB_DEV = 4

time_step = 0.5
omega_source = 1.3

ROWS = 32
TILES = 16
HALO = STEPS
XR = ROWS + 2 * HALO
HT = HALO // 4
YV = 24
PAD = 8
NARR = 14
NEAR = 8
FAR = 4
FARW = TILES + HT + 1
LANES = 128
HIGH = lax.Precision.HIGHEST
VLIM = pltpu.CompilerParams(vmem_limit_bytes=60 * 1024 * 1024)


def shifted(array, axis, by):
    count = lax.axis_size(axis)
    return lax.ppermute(array, axis, [(i, (i + by) % count) for i in range(count)])


def planes(e, h, eps, aux):
    out = [e.at[r, c] for r in range(2) for c in range(3)]
    out += [h.at[r, c] for r in range(2) for c in range(3)]
    return out + [eps, aux]


def pack_near(e, h, eps, aux, to_prev, to_next, to_left, to_right):
    edge = HT * LANES
    length = TILES * LANES
    for a, src in enumerate(planes(e, h, eps, aux)):
        to_prev[a] = src[0:NEAR, :]
        to_next[a] = src[ROWS - NEAR : ROWS, :]
        to_left[a] = src[:, 0:edge]
        to_right[a] = src[:, length - edge : length]


def pack_far(e, h, eps, aux, left, right, to_prev, to_next):
    edge = HT * LANES
    length = TILES * LANES
    lo, hi = NEAR, ROWS - NEAR - FAR
    for a, src in enumerate(planes(e, h, eps, aux)):
        p, q = a // 2, pl.ds(FAR * (a % 2), FAR)
        to_prev[p, q, 0:edge] = left[a, lo : lo + FAR, :]
        to_prev[p, q, edge : edge + length] = src[lo : lo + FAR, :]
        to_prev[p, q, edge + length :] = right[a, lo : lo + FAR, 0:LANES]
        to_next[p, q, 0:LANES] = left[a, hi : hi + FAR, edge - LANES : edge]
        to_next[p, q, LANES : LANES + length] = src[hi : hi + FAR, :]
        to_next[p, q, LANES + length :] = right[a, hi : hi + FAR, :]


def pack_corner(behind, ahead, to_left, to_right):
    edge = HT * LANES
    length = TILES * LANES
    for a in range(NARR):
        to_left[a, 0:NEAR, :] = behind[a, :, 0:edge]
        to_left[a, NEAR:, :] = ahead[a, :, 0:edge]
        to_right[a, 0:NEAR, :] = behind[a, :, length - edge : length]
        to_right[a, NEAR:, :] = ahead[a, :, length - edge : length]


def at(a, x, v=0):
    return PAD + (a * XR + x) * YV + v


def place(dst, a, x, v, value):
    dst[pl.ds(at(a, x, v), value.shape[0], stride=YV), :] = value


def stepping(
    waves,
    e,
    h,
    eps,
    aux,
    left,
    right,
    near_b,
    near_a,
    far_b,
    far_a,
    corner_l,
    corner_r,
    select,
    marks,
    e_out,
    h_out,
    packed,
    we,
    wh,
    wc,
    ws,
    wa,
    acc,
):
    def unpack(dst, a, n, own, fix):
        for j in range(TILES):
            cols = pl.ds(j * LANES, LANES)
            for i in range(ROWS // 8):
                place(dst, a, HALO + 8 * i, HT + j, fix(own[pl.ds(8 * i, 8), cols]))
            place(dst, a, FAR, HT + j, fix(near_b[n, :, cols]))
            place(dst, a, HALO + ROWS, HT + j, fix(near_a[n, :, cols]))
        for j in range(HT):
            cols = pl.ds(j * LANES, LANES)
            for i in range(ROWS // 8):
                place(dst, a, HALO + 8 * i, j, fix(left[n, pl.ds(8 * i, 8), cols]))
                place(dst, a, HALO + 8 * i, HT + TILES + j, fix(right[n, pl.ds(8 * i, 8), cols]))
            for src, v in ((corner_l, j), (corner_r, HT + TILES + j)):
                place(dst, a, FAR, v, fix(src[n, 0:NEAR, cols]))
                place(dst, a, HALO + ROWS, v, fix(src[n, NEAR : 2 * NEAR, cols]))
        for j in range(FARW):
            cols = pl.ds(j * LANES, LANES)
            q = pl.ds(FAR * (n % 2), FAR)
            place(dst, a, 0, HT - 1 + j, fix(far_b[n // 2, q, cols]))
            place(dst, a, XR - FAR, j, fix(far_a[n // 2, q, cols]))

    for a in range(6):
        unpack(we, a, a, e.at[a // 3, a % 3], lambda t: t)
        unpack(wh, a, 6 + a, h.at[a // 3, a % 3], lambda t: t * 2.0)
    unpack(wc, 0, 12, eps, lambda t: 0.25 / t)
    unpack(wa, 0, 13, aux, lambda t: t)

    lane = lax.broadcasted_iota(jnp.int32, (YV, LANES), 1)
    level = lane % NZ
    up_keep = level != NZ - 1
    down_keep = level != 0
    first = lane < NZ
    last = lane >= LANES - NZ

    rows_i = lax.broadcasted_iota(jnp.int32, (LANES, LANES), 0)
    cols_i = lax.broadcasted_iota(jnp.int32, (LANES, LANES), 1)

    def spread(k):
        return (rows_i == (cols_i // NZ) * NZ + k).astype(jnp.float32)

    held = wa[pl.ds(PAD, XR * YV), :]
    lev = lax.broadcasted_iota(jnp.int32, (XR * YV, LANES), 1) % NZ
    held = jnp.where(lev < 4, held, 0.0)
    for r in range(2):
        strength = jnp.dot(held, spread(r), precision=HIGH, preferred_element_type=jnp.float32)
        where = jnp.dot(held, spread(2 + r), precision=HIGH, preferred_element_type=jnp.float32)
        ws[pl.ds(PAD + r * XR * YV, XR * YV), :] = jnp.where(
            lev.astype(jnp.float32) == where, strength, 0.0
        )
    acc[...] = jnp.zeros_like(acc)

    def up_z(t):
        return jnp.where(up_keep, pltpu.roll(t, LANES - 1, 1), 0.0)

    def down_z(t):
        return jnp.where(down_keep, pltpu.roll(t, 1, 1), 0.0)

    def up_y(t, after):
        return pltpu.roll(jnp.where(first, after, t), LANES - NZ, 1)

    def down_y(t, before):
        return pltpu.roll(jnp.where(last, before, t), NZ, 1)

    def row(ref, a, x):
        return ref[pl.ds(pl.multiple_of(at(a, x), 8), YV), :]

    def off(ref, a, x, by):
        return ref[pl.ds(at(a, x) + by, YV), :]

    def put(ref, a, x, value):
        ref[pl.ds(pl.multiple_of(at(a, x), 8), YV), :] = value

    def magnetic_row(r, x):
        ex, ey, ez = (row(we, 3 * r + c, x) for c in range(3))
        hx, hy, hz = (row(wh, 3 * r + c, x) for c in range(3))
        ey_x, ez_x = (row(we, 3 * r + c, x + 1) for c in (1, 2))
        ex_y = up_y(ex, off(we, 3 * r, x, 1))
        ez_y = up_y(ez, off(we, 3 * r + 2, x, 1))
        hx = hx - ((ez_y - ez) - (up_z(ey) - ey))
        hy = hy - ((up_z(ex) - ex) - (ez_x - ez))
        hz = hz - ((ey_x - ey) - (ex_y - ex))
        return (hx, hy, hz)

    def electric_row(r, x, c, wave):
        hx, hy, hz = (row(wh, 3 * r + k, x) for k in range(3))
        hy_x, hz_x = (row(wh, 3 * r + k, x - 1) for k in (1, 2))
        hx_y = down_y(hx, off(wh, 3 * r, x, -1))
        hz_y = down_y(hz, off(wh, 3 * r + 2, x, -1))
        ex, ey, ez = (row(we, 3 * r + k, x) for k in range(3))
        ex = ex + c * ((hz - hz_y) - (hy - down_z(hy))) + wave * row(ws, r, x)
        ey = ey + c * ((hx - down_z(hx)) - (hz - hz_x))
        ez = ez + c * ((hy - hy_x) - (hx - hx_y))
        return (ex, ey, ez)

    def magnetic_group(x, count):
        for r in range(2):
            done = [magnetic_row(r, x + i) for i in range(count)]
            for i in range(count):
                for k in range(3):
                    put(wh, 3 * r + k, x + i, done[i][k])

    def electric_group(x, count, wave):
        for i in range(count):
            c = row(wc, 0, x + i)
            f = electric_row(0, x + i, c, wave)
            g = electric_row(1, x + i, c, wave)
            total = row(acc, 0, x + i) + (f[0] * g[0] + f[1] * g[1] + f[2] * g[2])
            put(acc, 0, x + i, total)
            for k in range(3):
                put(we, k, x + i, f[k])
                put(we, 3 + k, x + i, g[k])

    unroll = 2

    def step(n, _):
        wave = waves[n]
        groups = (XR - n) // unroll - n // unroll

        def hgroup(g, _):
            magnetic_group((n // unroll + g) * unroll, unroll)
            return 0

        def egroup(g, _):
            electric_group((n // unroll + g) * unroll, unroll, wave)
            return 0

        lax.fori_loop(0, groups, hgroup, 0)
        lax.fori_loop(0, groups, egroup, 0)
        return 0

    lax.fori_loop(0, STEPS, step, 0)

    for a in range(6):
        for i in range(ROWS // 8):
            for j in range(TILES):
                src = pl.ds(at(a, HALO + 8 * i, HT + j), 8, stride=YV)
                dst = (a // 3, a % 3, pl.ds(8 * i, 8), pl.ds(j * LANES, LANES))
                e_out[dst] = we[src, :]
                h_out[dst] = wh[src, :] * 0.5

    group = (rows_i // NZ == cols_i % 4).astype(jnp.float32)
    mine = acc[pl.ds(at(0, HALO), ROWS * YV), :]
    sums = jnp.dot(mine, group, precision=HIGH, preferred_element_type=jnp.float32)
    per = BROWS * YV
    place_i = lax.broadcasted_iota(jnp.int32, (per, LANES), 0)
    cell_i = lax.broadcasted_iota(jnp.int32, (per, LANES), 1)
    keep = (place_i // YV == cell_i // (LANES // BROWS)) & (
        (cell_i % (LANES // BROWS)) // 4 == place_i % YV - HT
    )
    blocks = jnp.sum(
        jnp.where(keep[None], sums.reshape(ROWS // BROWS, per, LANES), 0.0), axis=1
    ) / (STEPS * NZ)
    packed[...] = (
        jnp.dot(select[...], blocks, precision=HIGH, preferred_element_type=jnp.float32)
        + marks[...]
    )


def collect(received, filter_matrix, out):
    rec = received[...]
    places = rec.shape[0]
    p = lax.broadcasted_iota(jnp.int32, (places, places), 0)
    q = lax.broadcasted_iota(jnp.int32, (places, places), 1)
    pick = (q == (p // 3) * 3 + 2).astype(jnp.float32)
    labels = jnp.dot(pick, rec, precision=HIGH, preferred_element_type=jnp.float32)
    pr = lax.broadcasted_iota(jnp.int32, (places, LANES), 0)
    ln = lax.broadcasted_iota(jnp.int32, (places, LANES), 1)
    label = jnp.sum(jnp.where((ln == pr % 3) & (pr % 3 < 2), labels, 0.0), axis=1, keepdims=True)
    want = lax.broadcasted_iota(jnp.int32, (places, 8), 1) + 1
    choose = (label == want.astype(jnp.float32)).astype(jnp.float32)
    design = lax.dot_general(
        choose, rec, (((0,), (0,)), ((), ())), precision=HIGH, preferred_element_type=jnp.float32
    )
    result = jnp.dot(
        design, filter_matrix[...], precision=HIGH, preferred_element_type=jnp.float32
    )
    out[...] = result[0:DB_DEV]


def call(kernel, out_shape, count, **kwargs):
    def struct(shape):
        return jax.ShapeDtypeStruct(shape, jnp.float32)

    specs = [pl.BlockSpec(memory_space=pltpu.VMEM)] * count
    outs = tuple(struct(s) for s in out_shape)
    return pl.pallas_call(
        kernel,
        in_specs=kwargs.pop("in_specs", specs),
        out_specs=tuple(pl.BlockSpec(memory_space=pltpu.VMEM) for _ in outs),
        out_shape=outs,
        compiler_params=VLIM,
        **kwargs,
    )


def per_device(
    electric,
    magnetic,
    permittivity,
    source_profile,
    source_plane,
    block_owner,
    design_slot,
    filter_matrix,
):
    length = TILES * LANES
    columns = length // NZ
    edge = HT * LANES
    cell = jnp.arange(length, dtype=jnp.int32)
    column = jnp.arange(columns, dtype=jnp.int32)
    run = jnp.arange(2, dtype=jnp.int32)
    spread = (
        (cell[None, None, :] // NZ == column[None, :, None])
        & (cell[None, None, :] % NZ == run[:, None, None])
    ).astype(jnp.float32)
    mark = (cell[None, :] % NZ == run[:, None] + 2).astype(jnp.float32)
    aux = jnp.einsum("krc,kcl->rl", source_profile, spread, precision=HIGH)
    aux = aux + jnp.einsum("kr,kl->rl", source_plane.astype(jnp.float32), mark, precision=HIGH)

    x_near = (NARR, NEAR, length)
    y_own = (NARR, ROWS, edge)
    own = (electric, magnetic, permittivity, aux)
    to_prev, to_next, to_left, to_right = call(pack_near, (x_near, x_near, y_own, y_own), 4)(*own)
    near_b = shifted(to_next, "gx", 1)
    near_a = shifted(to_prev, "gx", -1)
    left = shifted(to_right, "gy", 1)
    right = shifted(to_left, "gy", -1)

    x_far = (NARR // 2, 2 * FAR, FARW * LANES)
    far_prev, far_next = call(pack_far, (x_far, x_far), 6)(*own, left, right)
    far_b = shifted(far_next, "gx", 1)
    far_a = shifted(far_prev, "gx", -1)

    y_corner = (NARR, 2 * NEAR, edge)
    corner_left, corner_right = call(pack_corner, (y_corner, y_corner), 2)(near_b, near_a)
    corner_l = shifted(corner_right, "gy", 1)
    corner_r = shifted(corner_left, "gy", -1)

    count = ROWS // BROWS
    owner = block_owner[0, 0, :, 0]
    slot = design_slot[0, 0, :]
    owners = lax.axis_size("gy")
    index = jnp.arange(count, dtype=jnp.int32)
    earlier = (
        ((owner[:, None] == owner[None, :]) & (index[None, :] < index[:, None]))
        .astype(jnp.int32)
        .sum(1)
    )
    places = jnp.arange(3 * owners, dtype=jnp.int32)
    chosen = (places[:, None] == (owner * 3 + earlier)[None, :]).astype(jnp.float32)
    lane = jnp.arange(LANES, dtype=jnp.int32)
    holder = (places[:, None] == (owner * 3 + 2)[None, :]).astype(jnp.float32)
    tags = (lane[None, :] == earlier[:, None]).astype(jnp.float32) * (slot + 1).astype(
        jnp.float32
    )[:, None]
    marks = jnp.dot(holder, tags, precision=HIGH)

    waves = jnp.asarray(
        time_step
        * np.sin(np.arange(1, STEPS + 1).astype(np.float32) * np.float32(omega_source * time_step)),
        jnp.float32,
    )
    field = (2, 3, ROWS, length)
    many = XR * YV
    vmem = pl.BlockSpec(memory_space=pltpu.VMEM)
    field_e, field_h, packed = call(
        stepping,
        (field, field, (3 * owners, LANES)),
        15,
        in_specs=[pl.BlockSpec(memory_space=pltpu.SMEM)] + [vmem] * 14,
        scratch_shapes=[
            pltpu.VMEM((6 * many + PAD + YV, LANES), jnp.float32),
            pltpu.VMEM((6 * many + PAD + YV, LANES), jnp.float32),
            pltpu.VMEM((many + 2 * PAD, LANES), jnp.float32),
            pltpu.VMEM((2 * many + 2 * PAD, LANES), jnp.float32),
            pltpu.VMEM((many + 2 * PAD, LANES), jnp.float32),
            pltpu.VMEM((many + 2 * PAD, LANES), jnp.float32),
        ],
    )(
        waves,
        *own,
        left,
        right,
        near_b,
        near_a,
        far_b,
        far_a,
        corner_l,
        corner_r,
        chosen,
        marks,
    )
    received = lax.all_to_all(
        packed.reshape(owners, 3, LANES), "gy", split_axis=0, concat_axis=0, tiled=True
    )
    (result,) = call(collect, ((DB_DEV, LANES),), 2)(
        received.reshape(3 * owners, LANES), filter_matrix
    )
    return (field_e, field_h, result[None])


def solution(mesh):
    placed = (
        P(None, None, "gx", "gy"),
        P(None, None, "gx", "gy"),
        P("gx", "gy"),
        P(None, "gx", "gy"),
        P(None, "gx"),
        P("gx", "gy", None, None),
        P("gx", "gy", None),
        P(),
    )
    return jax.shard_map(
        per_device,
        mesh=mesh,
        in_specs=placed,
        out_specs=(P(None, None, "gx", "gy"), P(None, None, "gx", "gy"), P("gx", "gy", None)),
        check_vma=False,
    )
```

```python
import functools

import jax
import jax.numpy as jnp
import numpy as np
from jax import lax
from jax.experimental import pallas as pl
from jax.experimental.pallas import tpu as pltpu
from jax.sharding import PartitionSpec as P

NZ = 32
STEPS = 12
BROWS = 2
DB_DEV = 4

time_step = 0.5
omega_source = 1.3

ROWS = 32
TILES = 16
HALO = STEPS
XR = ROWS + 2 * HALO
HT = HALO // 4
YV = 24
PAD = 8
NARR = 14
NEAR = 8
FAR = 4
FARW = TILES + HT + 1
LANES = 128
HIGH = lax.Precision.HIGHEST


def shifted(array, axis, by):
    count = lax.axis_size(axis)
    return lax.ppermute(array, axis, [(i, (i + by) % count) for i in range(count)])


def dot(a, b):
    return jnp.dot(a, b, precision=HIGH, preferred_element_type=jnp.float32)


def iota(shape, axis):
    return lax.broadcasted_iota(jnp.int32, shape, axis)


def planes(e, h, eps, aux=None):
    out = [e.at[r, c] for r in range(2) for c in range(3)]
    out += [h.at[r, c] for r in range(2) for c in range(3)] + [eps]
    return out + ([] if aux is None else [aux])


def source_tags(profile, plane):
    half = LANES // 2
    c, l = iota((half, LANES), 0), iota((half, LANES), 1)
    strength = dot(profile[0], (l == c).astype(jnp.float32))
    strength = strength + dot(profile[1], (l == c + half).astype(jnp.float32))
    pick = (iota((2, LANES), 0) == iota((2, LANES), 1)).astype(jnp.float32)
    where = lax.dot_general(
        plane[...], pick, (((0,), (0,)), ((), ())), precision=HIGH, preferred_element_type=jnp.float32
    )
    return strength, where


def source_rows(strength, where):
    length = TILES * LANES
    half = LANES // 2
    c, l = iota((LANES, length), 0), iota((LANES, length), 1)
    spread = ((l // NZ == c % half) & (l % NZ == c // half)).astype(jnp.float32)
    level = iota((strength.shape[0], length), 1) % NZ
    out = dot(strength, spread)
    out = jnp.where(level == 2, where[:, 0:1], out)
    return jnp.where(level == 3, where[:, 1:2], out)


def pack_side(e, h, eps, profile, plane, to_left, to_right, aux):
    edge = HT * LANES
    length = TILES * LANES
    aux[...] = source_rows(*source_tags(profile, plane))
    for a, src in enumerate(planes(e, h, eps, aux)):
        to_left[a] = src[:, 0:edge]
        to_right[a] = src[:, length - edge : length]


def pack_near(e, h, eps, profile, plane, to_prev, to_next):
    length = TILES * LANES
    for a, src in enumerate(planes(e, h, eps)):
        to_prev[:, a * length : (a + 1) * length] = src[0:NEAR, :]
        to_next[:, a * length : (a + 1) * length] = src[ROWS - NEAR : ROWS, :]
    for k, tag in enumerate(source_tags(profile, plane)):
        cols = pl.ds((NARR - 1) * length + k * LANES, LANES)
        to_prev[:, cols] = tag[0:NEAR, :]
        to_next[:, cols] = tag[ROWS - NEAR : ROWS, :]


def near_source(ref):
    base = (NARR - 1) * TILES * LANES
    return source_rows(ref[:, base : base + LANES], ref[:, base + LANES : base + 2 * LANES])


def pack_far(e, h, eps, aux, left, right, to_prev, to_next):
    edge = HT * LANES
    length = TILES * LANES
    lo, hi = NEAR, ROWS - NEAR - FAR
    for a, src in enumerate(planes(e, h, eps, aux)):
        p, q = a // 2, pl.ds(FAR * (a % 2), FAR)
        to_prev[p, q, 0:edge] = left[a, lo : lo + FAR, :]
        to_prev[p, q, edge : edge + length] = src[lo : lo + FAR, :]
        to_prev[p, q, edge + length :] = right[a, lo : lo + FAR, 0:LANES]
        to_next[p, q, 0:LANES] = left[a, hi : hi + FAR, edge - LANES : edge]
        to_next[p, q, LANES : LANES + length] = src[hi : hi + FAR, :]
        to_next[p, q, LANES + length :] = right[a, hi : hi + FAR, :]


def pack_corner(behind, ahead, to_left, to_right, made):
    edge = HT * LANES
    length = TILES * LANES
    for k, src in enumerate((behind, ahead)):
        made[...] = near_source(src)
        rows = pl.ds(NEAR * k, NEAR)
        for a in range(NARR):
            part = made if a == NARR - 1 else src.at[:, pl.ds(a * length, length)]
            to_left[a, rows, :] = part[:, 0:edge]
            to_right[a, rows, :] = part[:, length - edge : length]


def at(a, x, v=0):
    return PAD + (a * XR + x) * YV + v


def place(dst, a, x, v, value):
    dst[pl.ds(at(a, x, v), value.shape[0], stride=YV), :] = value


def row(ref, a, x):
    return ref[pl.ds(pl.multiple_of(at(a, x), 8), YV), :]


def off(ref, a, x, by):
    return ref[pl.ds(at(a, x) + by, YV), :]


def put(ref, a, x, value):
    ref[pl.ds(pl.multiple_of(at(a, x), 8), YV), :] = value


def fill_sources(wa, ws, x, count):
    size = count * YV
    level = iota((size, LANES), 1) % NZ
    held = wa[pl.ds(at(0, x), size), :]
    held = jnp.where(level < 4, held, 0.0)
    i, j = iota((LANES, LANES), 0), iota((LANES, LANES), 1)
    for r in range(2):
        strength = dot(held, (i == (j // NZ) * NZ + r).astype(jnp.float32))
        where = dot(held, (i == (j // NZ) * NZ + 2 + r).astype(jnp.float32))
        ws[pl.ds(at(r, x), size), :] = jnp.where(level.astype(jnp.float32) == where, strength, 0.0)


def kinds(we, wh, wc, wa):
    def same(t):
        return t

    out = [(we, a, same) for a in range(6)]
    out += [(wh, a, lambda t: t * 2.0) for a in range(6)]
    return out + [(wc, 0, lambda t: 0.25 / t), (wa, 0, same)]


class Stepper:
    def __init__(self, waves, we, wh, wc, ws, acc):
        self.waves, self.we, self.wh, self.wc, self.ws, self.acc = waves, we, wh, wc, ws, acc
        lane = iota((YV, LANES), 1)
        self.up_keep = lane % NZ != NZ - 1
        self.down_keep = lane % NZ != 0
        self.first = lane < NZ
        self.last = lane >= LANES - NZ

    def up_z(self, t):
        return jnp.where(self.up_keep, pltpu.roll(t, LANES - 1, 1), 0.0)

    def down_z(self, t):
        return jnp.where(self.down_keep, pltpu.roll(t, 1, 1), 0.0)

    def up_y(self, t, after):
        return pltpu.roll(jnp.where(self.first, after, t), LANES - NZ, 1)

    def down_y(self, t, before):
        return pltpu.roll(jnp.where(self.last, before, t), NZ, 1)

    def magnetic_row(self, r, x):
        we, wh = self.we, self.wh
        ex, ey, ez = (row(we, 3 * r + c, x) for c in range(3))
        hx, hy, hz = (row(wh, 3 * r + c, x) for c in range(3))
        ey_x, ez_x = (row(we, 3 * r + c, x + 1) for c in (1, 2))
        ex_y = self.up_y(ex, off(we, 3 * r, x, 1))
        ez_y = self.up_y(ez, off(we, 3 * r + 2, x, 1))
        hx = hx - ((ez_y - ez) - (self.up_z(ey) - ey))
        hy = hy - ((self.up_z(ex) - ex) - (ez_x - ez))
        hz = hz - ((ey_x - ey) - (ex_y - ex))
        return (hx, hy, hz)

    def electric_row(self, r, x, c, wave):
        we, wh = self.we, self.wh
        hx, hy, hz = (row(wh, 3 * r + k, x) for k in range(3))
        hy_x, hz_x = (row(wh, 3 * r + k, x - 1) for k in (1, 2))
        hx_y = self.down_y(hx, off(wh, 3 * r, x, -1))
        hz_y = self.down_y(hz, off(wh, 3 * r + 2, x, -1))
        ex, ey, ez = (row(we, 3 * r + k, x) for k in range(3))
        ex = ex + c * ((hz - hz_y) - (hy - self.down_z(hy))) + wave * row(self.ws, r, x)
        ey = ey + c * ((hx - self.down_z(hx)) - (hz - hz_x))
        ez = ez + c * ((hy - hy_x) - (hx - hx_y))
        return (ex, ey, ez)

    def magnetic(self, x):
        for r in range(2):
            for k, value in enumerate(self.magnetic_row(r, x)):
                put(self.wh, 3 * r + k, x, value)

    def electric(self, x, wave):
        c = row(self.wc, 0, x)
        f = self.electric_row(0, x, c, wave)
        g = self.electric_row(1, x, c, wave)
        put(self.acc, 0, x, row(self.acc, 0, x) + (f[0] * g[0] + f[1] * g[1] + f[2] * g[2]))
        for k in range(3):
            put(self.we, k, x, f[k])
            put(self.we, 3 + k, x, g[k])

    def edges(self, low, high, count):
        def step(n, _):
            wave = self.waves[n]
            for i in range(count):
                self.magnetic(low + n + i)
                self.magnetic(high - n + i)
            for i in range(count):
                self.electric(low + 1 + n + i, wave)
                self.electric(high - n + i, wave)
            return 0

        lax.fori_loop(0, STEPS, step, 0)

    def inside(self, low, high):
        def sweep(one, x, count):
            def group(g, _):
                for i in range(8):
                    one(x + g * 8 + i)
                return 0

            lax.fori_loop(0, count // 8, group, 0)
            for size in (4, 2, 1):
                begin = x + count // (2 * size) * (2 * size)

                @pl.when(count % (2 * size) >= size)
                def _(size=size, begin=begin):
                    for i in range(size):
                        one(begin + i)

        def step(n, _):
            wave = self.waves[n]
            sweep(self.magnetic, low + n, high - low - 2 * n)
            sweep(lambda x: self.electric(x, wave), low + 1 + n, high - low - 1 - 2 * n)
            return 0

        lax.fori_loop(0, STEPS, step, 0)


def run_inside(waves, e, h, eps, aux, left, right, we, wh, wc, ws, acc, wa):
    own = planes(e, h, eps, aux)
    for n, (dst, a, fix) in enumerate(kinds(we, wh, wc, wa)):
        for i in range(ROWS // 8):
            rows = pl.ds(8 * i, 8)
            for j in range(TILES):
                place(dst, a, HALO + 8 * i, HT + j, fix(own[n][rows, pl.ds(j * LANES, LANES)]))
            for j in range(HT):
                cols = pl.ds(j * LANES, LANES)
                place(dst, a, HALO + 8 * i, j, fix(left[n, rows, cols]))
                place(dst, a, HALO + 8 * i, HT + TILES + j, fix(right[n, rows, cols]))
    fill_sources(wa, ws, HALO, ROWS)
    acc[...] = jnp.zeros_like(acc)
    Stepper(waves, we, wh, wc, ws, acc).inside(HALO, HALO + ROWS - 1)


def run_near(waves, _e, _h, _c, _s, _t, near_b, near_a, corner_l, corner_r, we, wh, wc, ws, acc, wa, made):
    length = TILES * LANES
    for k, (src, x) in enumerate(((near_b, FAR), (near_a, HALO + ROWS))):
        made[...] = near_source(src)
        rows = pl.ds(NEAR * k, NEAR)
        for n, (dst, a, fix) in enumerate(kinds(we, wh, wc, wa)):
            for j in range(TILES):
                cols = pl.ds(j * LANES, LANES)
                value = made[:, cols] if n == NARR - 1 else src[:, pl.ds(n * length + j * LANES, LANES)]
                place(dst, a, x, HT + j, fix(value))
            for j in range(HT):
                cols = pl.ds(j * LANES, LANES)
                place(dst, a, x, j, fix(corner_l[n, rows, cols]))
                place(dst, a, x, HT + TILES + j, fix(corner_r[n, rows, cols]))
        fill_sources(wa, ws, x, NEAR)
    Stepper(waves, we, wh, wc, ws, acc).edges(FAR, HALO + ROWS - 1, NEAR)


def run_far(
    waves, _e, _h, _c, _s, _t, far_b, far_a, select, marks, e_out, h_out, packed, we, wh, wc, ws, acc, wa
):
    for n, (dst, a, fix) in enumerate(kinds(we, wh, wc, wa)):
        q = pl.ds(FAR * (n % 2), FAR)
        for j in range(FARW):
            cols = pl.ds(j * LANES, LANES)
            place(dst, a, 0, HT - 1 + j, fix(far_b[n // 2, q, cols]))
            place(dst, a, XR - FAR, j, fix(far_a[n // 2, q, cols]))
    fill_sources(wa, ws, 0, FAR)
    fill_sources(wa, ws, XR - FAR, FAR)
    Stepper(waves, we, wh, wc, ws, acc).edges(0, XR - FAR - 1, FAR)

    for a in range(6):
        for i in range(ROWS // 8):
            for j in range(TILES):
                src = pl.ds(at(a, HALO + 8 * i, HT + j), 8, stride=YV)
                dst = (a // 3, a % 3, pl.ds(8 * i, 8), pl.ds(j * LANES, LANES))
                e_out[dst] = we[src, :]
                h_out[dst] = wh[src, :] * 0.5

    i, j = iota((LANES, LANES), 0), iota((LANES, LANES), 1)
    sums = dot(acc[pl.ds(at(0, HALO), ROWS * YV), :], (i // NZ == j % 4).astype(jnp.float32))
    per = BROWS * YV
    p, q = iota((per, LANES), 0), iota((per, LANES), 1)
    half = LANES // BROWS
    keep = (p // YV == q // half) & ((q % half) // 4 == p % YV - HT)
    blocks = jnp.sum(
        jnp.where(keep[None], sums.reshape(ROWS // BROWS, per, LANES), 0.0), axis=1
    ) / (STEPS * NZ)
    packed[...] = dot(select[...], blocks) + marks[...]


def collect(received, filter_matrix, out):
    rec = received[...]
    places = rec.shape[0]
    p = lax.broadcasted_iota(jnp.int32, (places, places), 0)
    q = lax.broadcasted_iota(jnp.int32, (places, places), 1)
    pick = (q == (p // 3) * 3 + 2).astype(jnp.float32)
    labels = jnp.dot(pick, rec, precision=HIGH, preferred_element_type=jnp.float32)
    pr = lax.broadcasted_iota(jnp.int32, (places, LANES), 0)
    ln = lax.broadcasted_iota(jnp.int32, (places, LANES), 1)
    label = jnp.sum(jnp.where((ln == pr % 3) & (pr % 3 < 2), labels, 0.0), axis=1, keepdims=True)
    want = lax.broadcasted_iota(jnp.int32, (places, 8), 1) + 1
    choose = (label == want.astype(jnp.float32)).astype(jnp.float32)
    design = lax.dot_general(
        choose, rec, (((0,), (0,)), ((), ())), precision=HIGH, preferred_element_type=jnp.float32
    )
    result = jnp.dot(
        design, filter_matrix[...], precision=HIGH, preferred_element_type=jnp.float32
    )
    out[...] = result[0:DB_DEV]


def call(kernel, out_shape, count, micros, limit=32, **kwargs):
    vmem = pl.BlockSpec(memory_space=pltpu.VMEM)
    outs = tuple(jax.ShapeDtypeStruct(shape, jnp.float32) for shape in out_shape)
    return pl.pallas_call(
        kernel,
        in_specs=kwargs.pop("in_specs", [vmem] * count),
        out_specs=(vmem,) * len(outs),
        out_shape=outs,
        compiler_params=pltpu.CompilerParams(vmem_limit_bytes=limit * 1024 * 1024),
        name=kernel.__name__,
        cost_estimate=pl.CostEstimate(
            flops=0, transcendentals=0, bytes_accessed=micros * 3_000_000
        ),
        **kwargs,
    )


def per_device(
    electric,
    magnetic,
    permittivity,
    source_profile,
    source_plane,
    block_owner,
    design_slot,
    filter_matrix,
):
    length = TILES * LANES
    edge = HT * LANES
    plane = source_plane.astype(jnp.float32)
    raw = (electric, magnetic, permittivity, source_profile, plane)

    x_near = (NEAR, (NARR - 1) * length + 2 * LANES)
    to_prev, to_next = call(pack_near, (x_near, x_near), 5, 2)(*raw)
    to_prev, to_next, raw = lax.optimization_barrier((to_prev, to_next, raw))
    near_b = shifted(to_next, "gx", 1)
    near_a = shifted(to_prev, "gx", -1)

    y_own = (NARR, ROWS, edge)
    to_left, to_right, aux = call(pack_side, (y_own, y_own, (ROWS, length)), 5, 3)(*raw)
    left = shifted(to_right, "gy", 1)
    right = shifted(to_left, "gy", -1)

    y_corner = (NARR, 2 * NEAR, edge)
    made = pltpu.VMEM((NEAR, length), jnp.float32)
    corner_left, corner_right = call(
        pack_corner, (y_corner, y_corner), 2, 2, scratch_shapes=[made]
    )(near_b, near_a)
    corner_l = shifted(corner_right, "gy", 1)
    corner_r = shifted(corner_left, "gy", -1)

    own = (electric, magnetic, permittivity, aux)
    x_far = (NARR // 2, 2 * FAR, FARW * LANES)
    far_prev, far_next = call(pack_far, (x_far, x_far), 6, 2)(*own, left, right)
    far_prev, far_next, corner_l, corner_r, left, right = lax.optimization_barrier(
        (far_prev, far_next, corner_l, corner_r, left, right)
    )
    far_b = shifted(far_next, "gx", 1)
    far_a = shifted(far_prev, "gx", -1)

    waves = jnp.asarray(
        time_step
        * np.sin(np.arange(1, STEPS + 1).astype(np.float32) * np.float32(omega_source * time_step)),
        jnp.float32,
    )
    field = (2, 3, ROWS, length)
    many = XR * YV
    tail = PAD + YV
    vmem = pl.BlockSpec(memory_space=pltpu.VMEM)
    smem = pl.BlockSpec(memory_space=pltpu.SMEM)
    held = tuple((k * many + tail, LANES) for k in (6, 6, 1, 2, 1))
    tags = pltpu.VMEM((many + tail, LANES), jnp.float32)
    state = call(run_inside, held, 7, 15, in_specs=[smem] + [vmem] * 6, scratch_shapes=[tags])(
        waves, *own, left, right
    )

    count = ROWS // BROWS
    owner = block_owner[0, 0, :, 0]
    slot = design_slot[0, 0, :]
    owners = lax.axis_size("gy")
    index = jnp.arange(count, dtype=jnp.int32)
    earlier = (
        ((owner[:, None] == owner[None, :]) & (index[None, :] < index[:, None]))
        .astype(jnp.int32)
        .sum(1)
    )
    places = jnp.arange(3 * owners, dtype=jnp.int32)
    chosen = (places[:, None] == (owner * 3 + earlier)[None, :]).astype(jnp.float32)
    lane = jnp.arange(LANES, dtype=jnp.int32)
    holder = (places[:, None] == (owner * 3 + 2)[None, :]).astype(jnp.float32)
    named = (lane[None, :] == earlier[:, None]).astype(jnp.float32) * (slot + 1).astype(
        jnp.float32
    )[:, None]
    marks = jnp.dot(holder, named, precision=HIGH)

    state = call(
        run_near,
        held,
        10,
        12,
        in_specs=[smem] + [vmem] * 9,
        scratch_shapes=[tags, made],
        input_output_aliases={1 + k: k for k in range(5)},
    )(waves, *state, near_b, near_a, corner_l, corner_r)
    out = call(
        run_far,
        (field, field, (3 * owners, LANES)) + held,
        10,
        8,
        in_specs=[smem] + [vmem] * 9,
        scratch_shapes=[tags],
        input_output_aliases={1 + k: 3 + k for k in range(5)},
    )(waves, *state, far_b, far_a, chosen, marks)
    field_e, field_h, packed = out[:3]
    received = lax.all_to_all(
        packed.reshape(owners, 3, LANES), "gy", split_axis=0, concat_axis=0, tiled=True
    )
    (result,) = call(collect, ((DB_DEV, LANES),), 2, 1)(
        received.reshape(3 * owners, LANES), filter_matrix
    )
    return (field_e, field_h, result[None])


def solution(mesh):
    placed = (
        P(None, None, "gx", "gy"),
        P(None, None, "gx", "gy"),
        P("gx", "gy"),
        P(None, "gx", "gy"),
        P(None, "gx"),
        P("gx", "gy", None, None),
        P("gx", "gy", None),
        P(),
    )
    return jax.shard_map(
        per_device,
        mesh=mesh,
        in_specs=placed,
        out_specs=(P(None, None, "gx", "gy"), P(None, None, "gx", "gy"), P("gx", "gy", None)),
        check_vma=False,
    )
```

```python
import functools

import jax
import jax.numpy as jnp
import numpy as np
from jax import lax
from jax.experimental import pallas as pl
from jax.experimental.pallas import tpu as pltpu
from jax.sharding import PartitionSpec as P

NZ = 32
STEPS = 12
BROWS = 2
DB_DEV = 4

time_step = 0.5
omega_source = 1.3

ROWS = 32
TILES = 16
HALO = STEPS
XR = ROWS + 2 * HALO
HT = HALO // 4
YV = 24
PAD = 8
NARR = 14
NEAR = 8
FAR = 4
FARW = TILES + HT + 1
LANES = 128
HIGH = lax.Precision.HIGHEST


def shifted(array, axis, by):
    count = lax.axis_size(axis)
    return lax.ppermute(array, axis, [(i, (i + by) % count) for i in range(count)])


def dot(a, b):
    return jnp.dot(a, b, precision=HIGH, preferred_element_type=jnp.float32)


def iota(shape, axis):
    return lax.broadcasted_iota(jnp.int32, shape, axis)


def planes(e, h, eps, aux=None):
    out = [e.at[r, c] for r in range(2) for c in range(3)]
    out += [h.at[r, c] for r in range(2) for c in range(3)] + [eps]
    return out + ([] if aux is None else [aux])


def source_tags(profile, plane):
    half = LANES // 2
    c, l = iota((half, LANES), 0), iota((half, LANES), 1)
    strength = dot(profile[0], (l == c).astype(jnp.float32))
    strength = strength + dot(profile[1], (l == c + half).astype(jnp.float32))
    pick = (iota((2, LANES), 0) == iota((2, LANES), 1)).astype(jnp.float32)
    where = lax.dot_general(
        plane[...].astype(jnp.float32), pick, (((0,), (0,)), ((), ())), precision=HIGH, preferred_element_type=jnp.float32
    )
    return strength, where


def source_rows(strength, where):
    length = TILES * LANES
    half = LANES // 2
    c, l = iota((LANES, length), 0), iota((LANES, length), 1)
    spread = ((l // NZ == c % half) & (l % NZ == c // half)).astype(jnp.float32)
    level = iota((strength.shape[0], length), 1) % NZ
    out = dot(strength, spread)
    out = jnp.where(level == 2, where[:, 0:1], out)
    return jnp.where(level == 3, where[:, 1:2], out)


def moves(e, h, eps, view, put_at, sems, base):
    srcs = planes(e, h, eps)
    return [
        pltpu.make_async_copy(src.at[view], put_at(a), sems.at[base + a])
        for a, src in enumerate(srcs)
    ]


def pack_side(e, h, eps, profile, plane, to_left, to_right, aux, sems):
    edge = HT * LANES
    length = TILES * LANES
    first = (slice(None), pl.ds(0, edge))
    final = (slice(None), pl.ds(length - edge, edge))
    copies = moves(e, h, eps, first, lambda a: to_left.at[a], sems, 0)
    copies += moves(e, h, eps, final, lambda a: to_right.at[a], sems, NARR - 1)
    for copy in copies:
        copy.start()
    made = source_rows(*source_tags(profile, plane))
    aux[...] = made
    to_left[NARR - 1] = made[:, 0:edge]
    to_right[NARR - 1] = made[:, length - edge : length]
    for copy in copies:
        copy.wait()


def pack_near(e, h, eps, profile, plane, to_prev, to_next, sems):
    length = TILES * LANES

    def spot(ref):
        return lambda a: ref.at[:, pl.ds(a * length, length)]

    first = (pl.ds(0, NEAR), slice(None))
    final = (pl.ds(ROWS - NEAR, NEAR), slice(None))
    copies = moves(e, h, eps, first, spot(to_prev), sems, 0)
    copies += moves(e, h, eps, final, spot(to_next), sems, NARR - 1)
    for copy in copies:
        copy.start()
    for k, tag in enumerate(source_tags(profile, plane)):
        cols = pl.ds((NARR - 1) * length + k * LANES, LANES)
        to_prev[:, cols] = tag[0:NEAR, :]
        to_next[:, cols] = tag[ROWS - NEAR : ROWS, :]
    for copy in copies:
        copy.wait()


def near_source(ref):
    base = (NARR - 1) * TILES * LANES
    return source_rows(ref[:, base : base + LANES], ref[:, base + LANES : base + 2 * LANES])


def pack_far(e, h, eps, aux, left, right, to_prev, to_next):
    edge = HT * LANES
    length = TILES * LANES
    lo, hi = NEAR, ROWS - NEAR - FAR
    for a, src in enumerate(planes(e, h, eps, aux)):
        p, q = a // 2, pl.ds(FAR * (a % 2), FAR)
        to_prev[p, q, 0:edge] = left[a, lo : lo + FAR, :]
        to_prev[p, q, edge : edge + length] = src[lo : lo + FAR, :]
        to_prev[p, q, edge + length :] = right[a, lo : lo + FAR, 0:LANES]
        to_next[p, q, 0:LANES] = left[a, hi : hi + FAR, edge - LANES : edge]
        to_next[p, q, LANES : LANES + length] = src[hi : hi + FAR, :]
        to_next[p, q, LANES + length :] = right[a, hi : hi + FAR, :]


def pack_corner(behind, ahead, to_left, to_right, made):
    edge = HT * LANES
    length = TILES * LANES
    for k, src in enumerate((behind, ahead)):
        made[...] = near_source(src)
        rows = pl.ds(NEAR * k, NEAR)
        for a in range(NARR):
            part = made if a == NARR - 1 else src.at[:, pl.ds(a * length, length)]
            to_left[a, rows, :] = part[:, 0:edge]
            to_right[a, rows, :] = part[:, length - edge : length]


def at(a, x, v=0):
    return PAD + (a * XR + x) * YV + v


def place(dst, a, x, v, value):
    dst[pl.ds(at(a, x, v), value.shape[0], stride=YV), :] = value


def row(ref, a, x):
    return ref[pl.ds(pl.multiple_of(at(a, x), 8), YV), :]


def off(ref, a, x, by):
    return ref[pl.ds(at(a, x) + by, YV), :]


def put(ref, a, x, value):
    ref[pl.ds(pl.multiple_of(at(a, x), 8), YV), :] = value


def fill_sources(wa, ws, x, count):
    size = count * YV
    level = iota((size, LANES), 1) % NZ
    held = wa[pl.ds(at(0, x), size), :]
    held = jnp.where(level < 4, held, 0.0)
    i, j = iota((LANES, LANES), 0), iota((LANES, LANES), 1)
    for r in range(2):
        strength = dot(held, (i == (j // NZ) * NZ + r).astype(jnp.float32))
        where = dot(held, (i == (j // NZ) * NZ + 2 + r).astype(jnp.float32))
        ws[pl.ds(at(r, x), size), :] = jnp.where(level.astype(jnp.float32) == where, strength, 0.0)


def kinds(we, wh, wc, wa):
    def same(t):
        return t

    out = [(we, a, same) for a in range(6)]
    out += [(wh, a, lambda t: t * 2.0) for a in range(6)]
    return out + [(wc, 0, lambda t: 0.25 / t), (wa, 0, same)]


class Stepper:
    def __init__(self, waves, we, wh, wc, ws, acc):
        self.waves, self.we, self.wh, self.wc, self.ws, self.acc = waves, we, wh, wc, ws, acc
        lane = iota((YV, LANES), 1)
        self.up_keep = lane % NZ != NZ - 1
        self.down_keep = lane % NZ != 0
        self.first = lane < NZ
        self.last = lane >= LANES - NZ

    def up_z(self, t):
        return jnp.where(self.up_keep, pltpu.roll(t, LANES - 1, 1), 0.0)

    def down_z(self, t):
        return jnp.where(self.down_keep, pltpu.roll(t, 1, 1), 0.0)

    def up_y(self, t, after):
        return pltpu.roll(jnp.where(self.first, after, t), LANES - NZ, 1)

    def down_y(self, t, before):
        return pltpu.roll(jnp.where(self.last, before, t), NZ, 1)

    def magnetic_row(self, r, x):
        we, wh = self.we, self.wh
        ex, ey, ez = (row(we, 3 * r + c, x) for c in range(3))
        hx, hy, hz = (row(wh, 3 * r + c, x) for c in range(3))
        ey_x, ez_x = (row(we, 3 * r + c, x + 1) for c in (1, 2))
        ex_y = self.up_y(ex, off(we, 3 * r, x, 1))
        ez_y = self.up_y(ez, off(we, 3 * r + 2, x, 1))
        hx = hx - ((ez_y - ez) - (self.up_z(ey) - ey))
        hy = hy - ((self.up_z(ex) - ex) - (ez_x - ez))
        hz = hz - ((ey_x - ey) - (ex_y - ex))
        return (hx, hy, hz)

    def electric_row(self, r, x, c, wave):
        we, wh = self.we, self.wh
        hx, hy, hz = (row(wh, 3 * r + k, x) for k in range(3))
        hy_x, hz_x = (row(wh, 3 * r + k, x - 1) for k in (1, 2))
        hx_y = self.down_y(hx, off(wh, 3 * r, x, -1))
        hz_y = self.down_y(hz, off(wh, 3 * r + 2, x, -1))
        ex, ey, ez = (row(we, 3 * r + k, x) for k in range(3))
        ex = ex + c * ((hz - hz_y) - (hy - self.down_z(hy))) + wave * row(self.ws, r, x)
        ey = ey + c * ((hx - self.down_z(hx)) - (hz - hz_x))
        ez = ez + c * ((hy - hy_x) - (hx - hx_y))
        return (ex, ey, ez)

    def magnetic(self, x):
        for r in range(2):
            for k, value in enumerate(self.magnetic_row(r, x)):
                put(self.wh, 3 * r + k, x, value)

    def electric(self, x, wave):
        c = row(self.wc, 0, x)
        f = self.electric_row(0, x, c, wave)
        g = self.electric_row(1, x, c, wave)
        put(self.acc, 0, x, row(self.acc, 0, x) + (f[0] * g[0] + f[1] * g[1] + f[2] * g[2]))
        for k in range(3):
            put(self.we, k, x, f[k])
            put(self.we, 3 + k, x, g[k])

    def edges(self, low, high, count):
        def step(n, _):
            wave = self.waves[n]
            for i in range(count):
                self.magnetic(low + n + i)
                self.magnetic(high - n + i)
            for i in range(count):
                self.electric(low + 1 + n + i, wave)
                self.electric(high - n + i, wave)
            return 0

        lax.fori_loop(0, STEPS, step, 0)

    def inside(self, low, high):
        def sweep(one, x, count):
            def group(g, _):
                for i in range(8):
                    one(x + g * 8 + i)
                return 0

            lax.fori_loop(0, count // 8, group, 0)
            for size in (4, 2, 1):
                begin = x + count // (2 * size) * (2 * size)

                @pl.when(count % (2 * size) >= size)
                def _(size=size, begin=begin):
                    for i in range(size):
                        one(begin + i)

        def step(n, _):
            wave = self.waves[n]
            sweep(self.magnetic, low + n, high - low - 2 * n)
            sweep(lambda x: self.electric(x, wave), low + 1 + n, high - low - 1 - 2 * n)
            return 0

        lax.fori_loop(0, STEPS, step, 0)


def run_inside(waves, e, h, eps, aux, left, right, we, wh, wc, ws, acc, wa):
    own = planes(e, h, eps, aux)
    for n, (dst, a, fix) in enumerate(kinds(we, wh, wc, wa)):
        for i in range(ROWS // 8):
            rows = pl.ds(8 * i, 8)
            for j in range(TILES):
                place(dst, a, HALO + 8 * i, HT + j, fix(own[n][rows, pl.ds(j * LANES, LANES)]))
            for j in range(HT):
                cols = pl.ds(j * LANES, LANES)
                place(dst, a, HALO + 8 * i, j, fix(left[n, rows, cols]))
                place(dst, a, HALO + 8 * i, HT + TILES + j, fix(right[n, rows, cols]))
    fill_sources(wa, ws, HALO, ROWS)
    acc[...] = jnp.zeros_like(acc)
    Stepper(waves, we, wh, wc, ws, acc).inside(HALO, HALO + ROWS - 1)


def store_rows(we, wh, stage, e_out, h_out, sems, x, count):
    copies = []
    for a in range(6):
        for k, (src, out, scale) in enumerate(((we, e_out, None), (wh, h_out, 0.5))):
            for i in range(count // 8):
                for j in range(TILES):
                    value = src[pl.ds(at(a, HALO + x + 8 * i, HT + j), 8, stride=YV), :]
                    value = value if scale is None else value * scale
                    stage[6 * k + a, pl.ds(8 * i, 8), pl.ds(j * LANES, LANES)] = value
            copy = pltpu.make_async_copy(
                stage.at[6 * k + a], out.at[a // 3, a % 3, pl.ds(x, count), :], sems.at[6 * k + a]
            )
            copy.start()
            copies.append(copy)
    return copies


def run_near(waves, _e, _h, _c, _s, _t, near_b, near_a, corner_l, corner_r, e_out, h_out, we, wh, wc, ws, acc, wa, made, stage, sems):
    length = TILES * LANES
    for k, (src, x) in enumerate(((near_b, FAR), (near_a, HALO + ROWS))):
        made[...] = near_source(src)
        rows = pl.ds(NEAR * k, NEAR)
        for n, (dst, a, fix) in enumerate(kinds(we, wh, wc, wa)):
            for j in range(TILES):
                cols = pl.ds(j * LANES, LANES)
                value = made[:, cols] if n == NARR - 1 else src[:, pl.ds(n * length + j * LANES, LANES)]
                place(dst, a, x, HT + j, fix(value))
            for j in range(HT):
                cols = pl.ds(j * LANES, LANES)
                place(dst, a, x, j, fix(corner_l[n, rows, cols]))
                place(dst, a, x, HT + TILES + j, fix(corner_r[n, rows, cols]))
        fill_sources(wa, ws, x, NEAR)
    Stepper(waves, we, wh, wc, ws, acc).edges(FAR, HALO + ROWS - 1, NEAR)
    for copy in store_rows(we, wh, stage, e_out, h_out, sems, 8, 16):
        copy.wait()


def run_far(
    waves, _e, _h, _c, _s, _t, _x, _y, far_b, far_a, select, marks, e_out, h_out, packed, we, wh, wc, ws, acc, wa, stage_lo, stage_hi, sems
):
    for n, (dst, a, fix) in enumerate(kinds(we, wh, wc, wa)):
        q = pl.ds(FAR * (n % 2), FAR)
        for j in range(FARW):
            cols = pl.ds(j * LANES, LANES)
            place(dst, a, 0, HT - 1 + j, fix(far_b[n // 2, q, cols]))
            place(dst, a, XR - FAR, j, fix(far_a[n // 2, q, cols]))
    fill_sources(wa, ws, 0, FAR)
    fill_sources(wa, ws, XR - FAR, FAR)
    Stepper(waves, we, wh, wc, ws, acc).edges(0, XR - FAR - 1, FAR)

    stores = store_rows(we, wh, stage_lo, e_out, h_out, sems, 0, 8)
    stores += store_rows(we, wh, stage_hi, e_out, h_out, sems.at[pl.ds(12, 12)], 24, 8)
    i, j = iota((LANES, LANES), 0), iota((LANES, LANES), 1)
    sums = dot(acc[pl.ds(at(0, HALO), ROWS * YV), :], (i // NZ == j % 4).astype(jnp.float32))
    per = BROWS * YV
    p, q = iota((per, LANES), 0), iota((per, LANES), 1)
    half = LANES // BROWS
    keep = (p // YV == q // half) & ((q % half) // 4 == p % YV - HT)
    blocks = jnp.sum(
        jnp.where(keep[None], sums.reshape(ROWS // BROWS, per, LANES), 0.0), axis=1
    ) / (STEPS * NZ)
    packed[...] = dot(select[...], blocks) + marks[...]
    for copy in stores:
        copy.wait()


def collect(received, filter_matrix, out):
    rec = received[...]
    places = rec.shape[0]
    p = lax.broadcasted_iota(jnp.int32, (places, places), 0)
    q = lax.broadcasted_iota(jnp.int32, (places, places), 1)
    pick = (q == (p // 3) * 3 + 2).astype(jnp.float32)
    labels = jnp.dot(pick, rec, precision=HIGH, preferred_element_type=jnp.float32)
    pr = lax.broadcasted_iota(jnp.int32, (places, LANES), 0)
    ln = lax.broadcasted_iota(jnp.int32, (places, LANES), 1)
    label = jnp.sum(jnp.where((ln == pr % 3) & (pr % 3 < 2), labels, 0.0), axis=1, keepdims=True)
    want = lax.broadcasted_iota(jnp.int32, (places, 8), 1) + 1
    choose = (label == want.astype(jnp.float32)).astype(jnp.float32)
    design = lax.dot_general(
        choose, rec, (((0,), (0,)), ((), ())), precision=HIGH, preferred_element_type=jnp.float32
    )
    result = jnp.dot(
        design, filter_matrix[...], precision=HIGH, preferred_element_type=jnp.float32
    )
    out[...] = result[0:DB_DEV]


def call(kernel, out_shape, count, micros, limit=32, **kwargs):
    vmem = pl.BlockSpec(memory_space=pltpu.VMEM)
    outs = tuple(jax.ShapeDtypeStruct(shape, jnp.float32) for shape in out_shape)
    return pl.pallas_call(
        kernel,
        in_specs=kwargs.pop("in_specs", [vmem] * count),
        out_specs=kwargs.pop("out_specs", (vmem,) * len(outs)),
        out_shape=outs,
        compiler_params=pltpu.CompilerParams(vmem_limit_bytes=limit * 1024 * 1024),
        name=kernel.__name__,
        cost_estimate=pl.CostEstimate(
            flops=0, transcendentals=0, bytes_accessed=micros * 3_000_000
        ),
        **kwargs,
    )


def per_device(
    electric,
    magnetic,
    permittivity,
    source_profile,
    source_plane,
    block_owner,
    design_slot,
    filter_matrix,
):
    length = TILES * LANES
    edge = HT * LANES
    raw = (electric, magnetic, permittivity, source_profile, source_plane)
    vmem = pl.BlockSpec(memory_space=pltpu.VMEM)
    smem = pl.BlockSpec(memory_space=pltpu.SMEM)
    hbm = pl.BlockSpec(memory_space=pltpu.HBM)
    fixed = tuple(pltpu.with_memory_space_constraint(t, pltpu.HBM) for t in raw[:3])
    raw = fixed + raw[3:]
    packing = dict(
        in_specs=[hbm] * 3 + [vmem] * 2,
        scratch_shapes=[pltpu.SemaphoreType.DMA((2 * (NARR - 1),))],
    )

    y_own = (NARR, ROWS, edge)
    to_left, to_right, aux = call(pack_side, (y_own, y_own, (ROWS, length)), 5, 3, **packing)(*raw)
    left = shifted(to_right, "gy", 1)
    right = shifted(to_left, "gy", -1)

    x_near = (NEAR, (NARR - 1) * length + 2 * LANES)
    to_prev, to_next = call(pack_near, (x_near, x_near), 5, 2, **packing)(*raw)
    left, right, to_prev, to_next = lax.optimization_barrier((left, right, to_prev, to_next))
    near_b = shifted(to_next, "gx", 1)
    near_a = shifted(to_prev, "gx", -1)

    own = (electric, magnetic, permittivity, aux)
    x_far = (NARR // 2, 2 * FAR, FARW * LANES)
    far_prev, far_next = call(pack_far, (x_far, x_far), 6, 2)(*own, left, right)
    far_prev, far_next, left, right = lax.optimization_barrier((far_prev, far_next, left, right))
    waves = jnp.asarray(
        time_step
        * np.sin(np.arange(1, STEPS + 1).astype(np.float32) * np.float32(omega_source * time_step)),
        jnp.float32,
    )
    field = (2, 3, ROWS, length)
    many = XR * YV
    tail = PAD + YV
    held = tuple((k * many + tail, LANES) for k in (6, 6, 1, 2, 1))
    tags = pltpu.VMEM((many + tail, LANES), jnp.float32)
    state = call(run_inside, held, 7, 15, in_specs=[smem] + [vmem] * 6, scratch_shapes=[tags])(
        waves, *own, left, right
    )
    state, near_b, near_a = lax.optimization_barrier((state, near_b, near_a))

    y_corner = (NARR, 2 * NEAR, edge)
    made = pltpu.VMEM((NEAR, length), jnp.float32)
    corner_left, corner_right = call(
        pack_corner, (y_corner, y_corner), 2, 2, scratch_shapes=[made]
    )(near_b, near_a)
    corner_l = shifted(corner_right, "gy", 1)
    corner_r = shifted(corner_left, "gy", -1)

    far_prev, far_next, corner_l, corner_r = lax.optimization_barrier(
        (far_prev, far_next, corner_l, corner_r)
    )
    far_b = shifted(far_next, "gx", 1)
    far_a = shifted(far_prev, "gx", -1)

    count = ROWS // BROWS
    owner = block_owner[0, 0, :, 0]
    slot = design_slot[0, 0, :]
    owners = lax.axis_size("gy")
    index = jnp.arange(count, dtype=jnp.int32)
    earlier = (
        ((owner[:, None] == owner[None, :]) & (index[None, :] < index[:, None]))
        .astype(jnp.int32)
        .sum(1)
    )
    places = jnp.arange(3 * owners, dtype=jnp.int32)
    chosen = (places[:, None] == (owner * 3 + earlier)[None, :]).astype(jnp.float32)
    lane = jnp.arange(LANES, dtype=jnp.int32)
    holder = (places[:, None] == (owner * 3 + 2)[None, :]).astype(jnp.float32)
    named = (lane[None, :] == earlier[:, None]).astype(jnp.float32) * (slot + 1).astype(
        jnp.float32
    )[:, None]
    marks = jnp.dot(holder, named, precision=HIGH)

    copy_sem = pltpu.SemaphoreType.DMA
    state = call(
        run_near,
        (field, field) + held,
        10,
        12,
        in_specs=[smem] + [vmem] * 9,
        out_specs=(hbm,) * 2 + (vmem,) * 5,
        scratch_shapes=[tags, made, pltpu.VMEM((12, 16, length), jnp.float32), copy_sem((12,))],
        input_output_aliases={1 + k: 2 + k for k in range(5)},
    )(waves, *state, near_b, near_a, corner_l, corner_r)
    stage = pltpu.VMEM((12, 8, length), jnp.float32)
    out = call(
        run_far,
        (field, field, (3 * owners, LANES)) + held,
        12,
        8,
        in_specs=[smem] + [vmem] * 5 + [hbm] * 2 + [vmem] * 4,
        out_specs=(hbm,) * 2 + (vmem,) * 6,
        scratch_shapes=[tags, stage, stage, copy_sem((24,))],
        input_output_aliases={6: 0, 7: 1} | {1 + k: 3 + k for k in range(5)},
    )(waves, *state[2:], *state[:2], far_b, far_a, chosen, marks)
    field_e, field_h, packed = out[:3]
    received = lax.all_to_all(
        packed.reshape(owners, 3, LANES), "gy", split_axis=0, concat_axis=0, tiled=True
    )
    (result,) = call(collect, ((DB_DEV, LANES),), 2, 1)(
        received.reshape(3 * owners, LANES), filter_matrix
    )
    return (field_e, field_h, result[None])


def solution(mesh):
    placed = (
        P(None, None, "gx", "gy"),
        P(None, None, "gx", "gy"),
        P("gx", "gy"),
        P(None, "gx", "gy"),
        P(None, "gx"),
        P("gx", "gy", None, None),
        P("gx", "gy", None),
        P(),
    )
    return jax.shard_map(
        per_device,
        mesh=mesh,
        in_specs=placed,
        out_specs=(P(None, None, "gx", "gy"), P(None, None, "gx", "gy"), P("gx", "gy", None)),
        check_vma=False,
    )
```

```python
import functools

import jax
import jax.numpy as jnp
import numpy as np
from jax import lax
from jax.experimental import pallas as pl
from jax.experimental.pallas import tpu as pltpu
from jax.sharding import PartitionSpec as P

NZ = 32
STEPS = 12
BROWS = 2
DB_DEV = 4

time_step = 0.5
omega_source = 1.3

ROWS = 32
TILES = 16
HALO = STEPS
XR = ROWS + 2 * HALO
HT = HALO // 4
YV = 24
PAD = 8
NARR = 14
NEAR = 8
FAR = 4
FARW = TILES + HT + 1
LANES = 128
HIGH = lax.Precision.HIGHEST


def shifted(array, axis, by):
    count = lax.axis_size(axis)
    return lax.ppermute(array, axis, [(i, (i + by) % count) for i in range(count)])


def dot(a, b):
    return jnp.dot(a, b, precision=HIGH, preferred_element_type=jnp.float32)


def iota(shape, axis):
    return lax.broadcasted_iota(jnp.int32, shape, axis)


def planes(e, h, eps, aux=None):
    out = [e.at[r, c] for r in range(2) for c in range(3)]
    out += [h.at[r, c] for r in range(2) for c in range(3)] + [eps]
    return out + ([] if aux is None else [aux])


def source_tags(profile, plane):
    half = LANES // 2
    c, l = iota((half, LANES), 0), iota((half, LANES), 1)
    strength = dot(profile[0], (l == c).astype(jnp.float32))
    strength = strength + dot(profile[1], (l == c + half).astype(jnp.float32))
    pick = (iota((2, LANES), 0) == iota((2, LANES), 1)).astype(jnp.float32)
    where = lax.dot_general(
        plane[...].astype(jnp.float32), pick, (((0,), (0,)), ((), ())), precision=HIGH, preferred_element_type=jnp.float32
    )
    return strength, where


def source_rows(strength, where):
    length = TILES * LANES
    half = LANES // 2
    c, l = iota((LANES, length), 0), iota((LANES, length), 1)
    spread = ((l // NZ == c % half) & (l % NZ == c // half)).astype(jnp.float32)
    level = iota((strength.shape[0], length), 1) % NZ
    out = dot(strength, spread)
    out = jnp.where(level == 2, where[:, 0:1], out)
    return jnp.where(level == 3, where[:, 1:2], out)


def fetch_tags(profile, plane, pv, lv, sems):
    copies = [
        pltpu.make_async_copy(profile, pv, sems.at[0]),
        pltpu.make_async_copy(plane, lv, sems.at[1]),
    ]
    for copy in copies:
        copy.start()
    return copies


def pack_side(e, h, eps, profile, plane, to_left, to_right, aux, pv, lv, sems):
    edge = HT * LANES
    length = TILES * LANES
    tags = fetch_tags(profile, plane, pv, lv, sems)
    copies = []
    for part, begin in ((to_left, 0), (to_right, length - edge)):
        for a, src in enumerate(planes(e, h, eps)):
            copies.append(
                pltpu.make_async_copy(
                    src.at[:, pl.ds(begin, edge)], part.at[a], sems.at[2 + len(copies)]
                )
            )
            copies[-1].start()
    for copy in tags:
        copy.wait()
    made = source_rows(*source_tags(pv, lv))
    aux[...] = made
    to_left[NARR - 1] = made[:, 0:edge]
    to_right[NARR - 1] = made[:, length - edge : length]
    for copy in copies:
        copy.wait()


def pack_near(e, h, eps, profile, plane, edge_p, edge_n, mid_p, mid_n, pv, lv, sems):
    edge = HT * LANES
    length = TILES * LANES
    inner = length - 2 * edge
    tags = fetch_tags(profile, plane, pv, lv, sems)
    copies = []
    for x, side, middle in ((0, edge_p, mid_p), (ROWS - NEAR, edge_n, mid_n)):
        for a, src in enumerate(planes(e, h, eps)):
            for part, begin, size, to in (
                (side, 0, edge, 2 * a * edge),
                (side, length - edge, edge, (2 * a + 1) * edge),
                (middle, edge, inner, a * inner),
            ):
                copies.append(
                    pltpu.make_async_copy(
                        src.at[pl.ds(x, NEAR), pl.ds(begin, size)],
                        part.at[:, pl.ds(to, size)],
                        sems.at[2 + len(copies)],
                    )
                )
                copies[-1].start()
    for copy in tags:
        copy.wait()
    for k, tag in enumerate(source_tags(pv, lv)):
        cols = pl.ds((NARR - 1) * 2 * edge + k * LANES, LANES)
        edge_p[:, cols] = tag[0:NEAR, :]
        edge_n[:, cols] = tag[ROWS - NEAR : ROWS, :]
    for copy in copies:
        copy.wait()


def near_source(ref):
    base = (NARR - 1) * 2 * HT * LANES
    return source_rows(ref[:, base : base + LANES], ref[:, base + LANES : base + 2 * LANES])


def pack_far(e, h, eps, aux, left, right, to_prev, to_next):
    edge = HT * LANES
    length = TILES * LANES
    lo, hi = NEAR, ROWS - NEAR - FAR
    for a, src in enumerate(planes(e, h, eps, aux)):
        p, q = a // 2, pl.ds(FAR * (a % 2), FAR)
        to_prev[p, q, 0:edge] = left[a, lo : lo + FAR, :]
        to_prev[p, q, edge : edge + length] = src[lo : lo + FAR, :]
        to_prev[p, q, edge + length :] = right[a, lo : lo + FAR, 0:LANES]
        to_next[p, q, 0:LANES] = left[a, hi : hi + FAR, edge - LANES : edge]
        to_next[p, q, LANES : LANES + length] = src[hi : hi + FAR, :]
        to_next[p, q, LANES + length :] = right[a, hi : hi + FAR, :]


def pack_corner(behind, ahead, to_left, to_right):
    edge = HT * LANES
    length = TILES * LANES
    for k, src in enumerate((behind, ahead)):
        made = near_source(src)
        rows = pl.ds(NEAR * k, NEAR)
        to_left[NARR - 1, rows, :] = made[:, 0:edge]
        to_right[NARR - 1, rows, :] = made[:, length - edge : length]
        for a in range(NARR - 1):
            to_left[a, rows, :] = src[:, 2 * a * edge : (2 * a + 1) * edge]
            to_right[a, rows, :] = src[:, (2 * a + 1) * edge : (2 * a + 2) * edge]


def at(a, x, v=0):
    return PAD + (a * XR + x) * YV + v


def place(dst, a, x, v, value):
    dst[pl.ds(at(a, x, v), value.shape[0], stride=YV), :] = value


def row(ref, a, x):
    return ref[pl.ds(pl.multiple_of(at(a, x), 8), YV), :]


def off(ref, a, x, by):
    return ref[pl.ds(at(a, x) + by, YV), :]


def put(ref, a, x, value):
    ref[pl.ds(pl.multiple_of(at(a, x), 8), YV), :] = value


def fill_sources(wa, ws, x, count):
    size = count * YV
    level = iota((size, LANES), 1) % NZ
    held = wa[pl.ds(at(0, x), size), :]
    held = jnp.where(level < 4, held, 0.0)
    i, j = iota((LANES, LANES), 0), iota((LANES, LANES), 1)
    for r in range(2):
        strength = dot(held, (i == (j // NZ) * NZ + r).astype(jnp.float32))
        where = dot(held, (i == (j // NZ) * NZ + 2 + r).astype(jnp.float32))
        ws[pl.ds(at(r, x), size), :] = jnp.where(level.astype(jnp.float32) == where, strength, 0.0)


def kinds(we, wh, wc, wa):
    def same(t):
        return t

    out = [(we, a, same) for a in range(6)]
    out += [(wh, a, lambda t: t * 2.0) for a in range(6)]
    return out + [(wc, 0, lambda t: 0.25 / t), (wa, 0, same)]


class Stepper:
    def __init__(self, waves, we, wh, wc, ws, acc):
        self.waves, self.we, self.wh, self.wc, self.ws, self.acc = waves, we, wh, wc, ws, acc
        lane = iota((YV, LANES), 1)
        self.up_keep = lane % NZ != NZ - 1
        self.down_keep = lane % NZ != 0
        self.first = lane < NZ
        self.last = lane >= LANES - NZ

    def up_z(self, t):
        return jnp.where(self.up_keep, pltpu.roll(t, LANES - 1, 1), 0.0)

    def down_z(self, t):
        return jnp.where(self.down_keep, pltpu.roll(t, 1, 1), 0.0)

    def up_y(self, t, after):
        return pltpu.roll(jnp.where(self.first, after, t), LANES - NZ, 1)

    def down_y(self, t, before):
        return pltpu.roll(jnp.where(self.last, before, t), NZ, 1)

    def magnetic_row(self, r, x):
        we, wh = self.we, self.wh
        ex, ey, ez = (row(we, 3 * r + c, x) for c in range(3))
        hx, hy, hz = (row(wh, 3 * r + c, x) for c in range(3))
        ey_x, ez_x = (row(we, 3 * r + c, x + 1) for c in (1, 2))
        ex_y = self.up_y(ex, off(we, 3 * r, x, 1))
        ez_y = self.up_y(ez, off(we, 3 * r + 2, x, 1))
        hx = hx - ((ez_y - ez) - (self.up_z(ey) - ey))
        hy = hy - ((self.up_z(ex) - ex) - (ez_x - ez))
        hz = hz - ((ey_x - ey) - (ex_y - ex))
        return (hx, hy, hz)

    def electric_row(self, r, x, c, wave):
        we, wh = self.we, self.wh
        hx, hy, hz = (row(wh, 3 * r + k, x) for k in range(3))
        hy_x, hz_x = (row(wh, 3 * r + k, x - 1) for k in (1, 2))
        hx_y = self.down_y(hx, off(wh, 3 * r, x, -1))
        hz_y = self.down_y(hz, off(wh, 3 * r + 2, x, -1))
        ex, ey, ez = (row(we, 3 * r + k, x) for k in range(3))
        ex = ex + c * ((hz - hz_y) - (hy - self.down_z(hy))) + wave * row(self.ws, r, x)
        ey = ey + c * ((hx - self.down_z(hx)) - (hz - hz_x))
        ez = ez + c * ((hy - hy_x) - (hx - hx_y))
        return (ex, ey, ez)

    def magnetic(self, x):
        for r in range(2):
            for k, value in enumerate(self.magnetic_row(r, x)):
                put(self.wh, 3 * r + k, x, value)

    def electric(self, x, wave):
        c = row(self.wc, 0, x)
        f = self.electric_row(0, x, c, wave)
        g = self.electric_row(1, x, c, wave)
        put(self.acc, 0, x, row(self.acc, 0, x) + (f[0] * g[0] + f[1] * g[1] + f[2] * g[2]))
        for k in range(3):
            put(self.we, k, x, f[k])
            put(self.we, 3 + k, x, g[k])

    def edges(self, low, high, count):
        def step(n, _):
            wave = self.waves[n]
            for i in range(count):
                self.magnetic(low + n + i)
                self.magnetic(high - n + i)
            for i in range(count):
                self.electric(low + 1 + n + i, wave)
                self.electric(high - n + i, wave)
            return 0

        lax.fori_loop(0, STEPS, step, 0)

    def inside(self, low, high):
        def sweep(one, x, count):
            def group(g, _):
                for i in range(8):
                    one(x + g * 8 + i)
                return 0

            lax.fori_loop(0, count // 8, group, 0)
            for size in (4, 2, 1):
                begin = x + count // (2 * size) * (2 * size)

                @pl.when(count % (2 * size) >= size)
                def _(size=size, begin=begin):
                    for i in range(size):
                        one(begin + i)

        def step(n, _):
            wave = self.waves[n]
            sweep(self.magnetic, low + n, high - low - 2 * n)
            sweep(lambda x: self.electric(x, wave), low + 1 + n, high - low - 1 - 2 * n)
            return 0

        lax.fori_loop(0, STEPS, step, 0)


def run_inside(waves, e, h, eps, aux, left, right, we, wh, wc, ws, acc, wa):
    own = planes(e, h, eps, aux)
    for n, (dst, a, fix) in enumerate(kinds(we, wh, wc, wa)):
        for i in range(ROWS // 8):
            rows = pl.ds(8 * i, 8)
            for j in range(TILES):
                place(dst, a, HALO + 8 * i, HT + j, fix(own[n][rows, pl.ds(j * LANES, LANES)]))
            for j in range(HT):
                cols = pl.ds(j * LANES, LANES)
                place(dst, a, HALO + 8 * i, j, fix(left[n, rows, cols]))
                place(dst, a, HALO + 8 * i, HT + TILES + j, fix(right[n, rows, cols]))
    fill_sources(wa, ws, HALO, ROWS)
    acc[...] = jnp.zeros_like(acc)
    Stepper(waves, we, wh, wc, ws, acc).inside(HALO, HALO + ROWS - 1)


def store_rows(we, wh, stage, e_out, h_out, sems, x, count):
    copies = []
    for a in range(6):
        for k, (src, out, scale) in enumerate(((we, e_out, None), (wh, h_out, 0.5))):
            for i in range(count // 8):
                for j in range(TILES):
                    value = src[pl.ds(at(a, HALO + x + 8 * i, HT + j), 8, stride=YV), :]
                    value = value if scale is None else value * scale
                    stage[6 * k + a, pl.ds(8 * i, 8), pl.ds(j * LANES, LANES)] = value
            copy = pltpu.make_async_copy(
                stage.at[6 * k + a], out.at[a // 3, a % 3, pl.ds(x, count), :], sems.at[6 * k + a]
            )
            copy.start()
            copies.append(copy)
    return copies


def run_near(waves, _e, _h, _c, _s, _t, edge_b, edge_a, mid_b, mid_a, corner_l, corner_r, e_out, h_out, we, wh, wc, ws, acc, wa, made, stage, sems):
    edge = HT * LANES
    inner = (TILES - 2 * HT) * LANES

    def near_tile(side, middle, n, j):
        if n == NARR - 1:
            return made[:, pl.ds(j * LANES, LANES)]
        if HT <= j < TILES - HT:
            return middle[:, pl.ds(n * inner + (j - HT) * LANES, LANES)]
        j = j if j < HT else j - (TILES - 2 * HT)
        return side[:, pl.ds(2 * n * edge + j * LANES, LANES)]

    for k, (side, middle, x) in enumerate(
        ((edge_b, mid_b, FAR), (edge_a, mid_a, HALO + ROWS))
    ):
        made[...] = near_source(side)
        rows = pl.ds(NEAR * k, NEAR)
        for n, (dst, a, fix) in enumerate(kinds(we, wh, wc, wa)):
            for j in range(TILES):
                place(dst, a, x, HT + j, fix(near_tile(side, middle, n, j)))
            for j in range(HT):
                cols = pl.ds(j * LANES, LANES)
                place(dst, a, x, j, fix(corner_l[n, rows, cols]))
                place(dst, a, x, HT + TILES + j, fix(corner_r[n, rows, cols]))
        fill_sources(wa, ws, x, NEAR)
    Stepper(waves, we, wh, wc, ws, acc).edges(FAR, HALO + ROWS - 1, NEAR)
    for copy in store_rows(we, wh, stage, e_out, h_out, sems, 8, 16):
        copy.wait()


def run_far(
    waves, _e, _h, _c, _s, _t, _x, _y, far_b, far_a, select, marks, e_out, h_out, packed, we, wh, wc, ws, acc, wa, stage_lo, stage_hi, sems
):
    for n, (dst, a, fix) in enumerate(kinds(we, wh, wc, wa)):
        q = pl.ds(FAR * (n % 2), FAR)
        for j in range(FARW):
            cols = pl.ds(j * LANES, LANES)
            place(dst, a, 0, HT - 1 + j, fix(far_b[n // 2, q, cols]))
            place(dst, a, XR - FAR, j, fix(far_a[n // 2, q, cols]))
    fill_sources(wa, ws, 0, FAR)
    fill_sources(wa, ws, XR - FAR, FAR)
    Stepper(waves, we, wh, wc, ws, acc).edges(0, XR - FAR - 1, FAR)

    stores = store_rows(we, wh, stage_lo, e_out, h_out, sems, 0, 8)
    stores += store_rows(we, wh, stage_hi, e_out, h_out, sems.at[pl.ds(12, 12)], 24, 8)
    i, j = iota((LANES, LANES), 0), iota((LANES, LANES), 1)
    sums = dot(acc[pl.ds(at(0, HALO), ROWS * YV), :], (i // NZ == j % 4).astype(jnp.float32))
    per = BROWS * YV
    p, q = iota((per, LANES), 0), iota((per, LANES), 1)
    half = LANES // BROWS
    keep = (p // YV == q // half) & ((q % half) // 4 == p % YV - HT)
    blocks = jnp.sum(
        jnp.where(keep[None], sums.reshape(ROWS // BROWS, per, LANES), 0.0), axis=1
    ) / (STEPS * NZ)
    packed[...] = dot(select[...], blocks) + marks[...]
    for copy in stores:
        copy.wait()


def collect(received, filter_matrix, out):
    rec = received[...]
    places = rec.shape[0]
    p = lax.broadcasted_iota(jnp.int32, (places, places), 0)
    q = lax.broadcasted_iota(jnp.int32, (places, places), 1)
    pick = (q == (p // 3) * 3 + 2).astype(jnp.float32)
    labels = jnp.dot(pick, rec, precision=HIGH, preferred_element_type=jnp.float32)
    pr = lax.broadcasted_iota(jnp.int32, (places, LANES), 0)
    ln = lax.broadcasted_iota(jnp.int32, (places, LANES), 1)
    label = jnp.sum(jnp.where((ln == pr % 3) & (pr % 3 < 2), labels, 0.0), axis=1, keepdims=True)
    want = lax.broadcasted_iota(jnp.int32, (places, 8), 1) + 1
    choose = (label == want.astype(jnp.float32)).astype(jnp.float32)
    design = lax.dot_general(
        choose, rec, (((0,), (0,)), ((), ())), precision=HIGH, preferred_element_type=jnp.float32
    )
    result = jnp.dot(
        design, filter_matrix[...], precision=HIGH, preferred_element_type=jnp.float32
    )
    out[...] = result[0:DB_DEV]


def call(kernel, out_shape, count, micros, limit=32, **kwargs):
    vmem = pl.BlockSpec(memory_space=pltpu.VMEM)
    outs = tuple(jax.ShapeDtypeStruct(shape, jnp.float32) for shape in out_shape)
    return pl.pallas_call(
        kernel,
        in_specs=kwargs.pop("in_specs", [vmem] * count),
        out_specs=kwargs.pop("out_specs", (vmem,) * len(outs)),
        out_shape=outs,
        compiler_params=pltpu.CompilerParams(vmem_limit_bytes=limit * 1024 * 1024),
        name=kernel.__name__,
        cost_estimate=pl.CostEstimate(
            flops=0, transcendentals=0, bytes_accessed=micros * 3_000_000
        ),
        **kwargs,
    )


def per_device(
    electric,
    magnetic,
    permittivity,
    source_profile,
    source_plane,
    block_owner,
    design_slot,
    filter_matrix,
):
    length = TILES * LANES
    edge = HT * LANES
    raw = (electric, magnetic, permittivity, source_profile, source_plane)
    vmem = pl.BlockSpec(memory_space=pltpu.VMEM)
    smem = pl.BlockSpec(memory_space=pltpu.SMEM)
    hbm = pl.BlockSpec(memory_space=pltpu.HBM)
    raw = tuple(pltpu.with_memory_space_constraint(t, pltpu.HBM) for t in raw)

    def packing(copies):
        return dict(
            in_specs=[hbm] * 5,
            scratch_shapes=[
                pltpu.VMEM(source_profile.shape, jnp.float32),
                pltpu.VMEM(source_plane.shape, jnp.int32),
                pltpu.SemaphoreType.DMA((2 + copies,)),
            ],
        )

    x_edge = (NEAR, (NARR - 1) * 2 * edge + 2 * LANES)
    x_mid = (NEAR, (NARR - 1) * (length - 2 * edge))
    edge_prev, edge_next, mid_prev, mid_next = call(
        pack_near, (x_edge, x_edge, x_mid, x_mid), 5, 2, **packing(6 * (NARR - 1))
    )(*raw)
    edge_prev, edge_next, raw = lax.optimization_barrier((edge_prev, edge_next, raw))
    edge_b = shifted(edge_next, "gx", 1)
    edge_a = shifted(edge_prev, "gx", -1)

    y_own = (NARR, ROWS, edge)
    to_left, to_right, aux = call(
        pack_side, (y_own, y_own, (ROWS, length)), 5, 3, **packing(2 * (NARR - 1))
    )(*raw)
    edge_b, edge_a, to_left, to_right = lax.optimization_barrier(
        (edge_b, edge_a, to_left, to_right)
    )
    left = shifted(to_right, "gy", 1)
    right = shifted(to_left, "gy", -1)

    y_corner = (NARR, 2 * NEAR, edge)
    made = pltpu.VMEM((NEAR, length), jnp.float32)
    corner_left, corner_right = call(pack_corner, (y_corner, y_corner), 2, 2)(edge_b, edge_a)
    corner_left, corner_right, mid_prev, mid_next = lax.optimization_barrier(
        (corner_left, corner_right, mid_prev, mid_next)
    )
    corner_l = shifted(corner_right, "gy", 1)
    corner_r = shifted(corner_left, "gy", -1)
    mid_b = shifted(mid_next, "gx", 1)
    mid_a = shifted(mid_prev, "gx", -1)

    own = (electric, magnetic, permittivity, aux)
    x_far = (NARR // 2, 2 * FAR, FARW * LANES)
    far_prev, far_next = call(pack_far, (x_far, x_far), 6, 2)(*own, left, right)
    far_prev, far_next, left, right = lax.optimization_barrier((far_prev, far_next, left, right))
    waves = jnp.asarray(
        time_step
        * np.sin(np.arange(1, STEPS + 1).astype(np.float32) * np.float32(omega_source * time_step)),
        jnp.float32,
    )
    field = (2, 3, ROWS, length)
    many = XR * YV
    tail = PAD + YV
    held = tuple((k * many + tail, LANES) for k in (6, 6, 1, 2, 1))
    tags = pltpu.VMEM((many + tail, LANES), jnp.float32)
    state = call(run_inside, held, 7, 15, in_specs=[smem] + [vmem] * 6, scratch_shapes=[tags])(
        waves, *own, left, right
    )
    far_prev, far_next, corner_l, corner_r = lax.optimization_barrier(
        (far_prev, far_next, corner_l, corner_r)
    )
    far_b = shifted(far_next, "gx", 1)
    far_a = shifted(far_prev, "gx", -1)
    state, mid_b, mid_a = lax.optimization_barrier((state, mid_b, mid_a))

    count = ROWS // BROWS
    owner = block_owner[0, 0, :, 0]
    slot = design_slot[0, 0, :]
    owners = lax.axis_size("gy")
    index = jnp.arange(count, dtype=jnp.int32)
    earlier = (
        ((owner[:, None] == owner[None, :]) & (index[None, :] < index[:, None]))
        .astype(jnp.int32)
        .sum(1)
    )
    places = jnp.arange(3 * owners, dtype=jnp.int32)
    chosen = (places[:, None] == (owner * 3 + earlier)[None, :]).astype(jnp.float32)
    lane = jnp.arange(LANES, dtype=jnp.int32)
    holder = (places[:, None] == (owner * 3 + 2)[None, :]).astype(jnp.float32)
    named = (lane[None, :] == earlier[:, None]).astype(jnp.float32) * (slot + 1).astype(
        jnp.float32
    )[:, None]
    marks = jnp.dot(holder, named, precision=HIGH)

    copy_sem = pltpu.SemaphoreType.DMA
    state = call(
        run_near,
        (field, field) + held,
        12,
        12,
        in_specs=[smem] + [vmem] * 11,
        out_specs=(hbm,) * 2 + (vmem,) * 5,
        scratch_shapes=[tags, made, pltpu.VMEM((12, 16, length), jnp.float32), copy_sem((12,))],
        input_output_aliases={1 + k: 2 + k for k in range(5)},
    )(waves, *state, edge_b, edge_a, mid_b, mid_a, corner_l, corner_r)
    stage = pltpu.VMEM((12, 8, length), jnp.float32)
    out = call(
        run_far,
        (field, field, (3 * owners, LANES)) + held,
        12,
        8,
        in_specs=[smem] + [vmem] * 5 + [hbm] * 2 + [vmem] * 4,
        out_specs=(hbm,) * 2 + (vmem,) * 6,
        scratch_shapes=[tags, stage, stage, copy_sem((24,))],
        input_output_aliases={6: 0, 7: 1} | {1 + k: 3 + k for k in range(5)},
    )(waves, *state[2:], *state[:2], far_b, far_a, chosen, marks)
    field_e, field_h, packed = out[:3]
    received = lax.all_to_all(
        packed.reshape(owners, 3, LANES), "gy", split_axis=0, concat_axis=0, tiled=True
    )
    (result,) = call(collect, ((DB_DEV, LANES),), 2, 1)(
        received.reshape(3 * owners, LANES), filter_matrix
    )
    return (field_e, field_h, result[None])


def solution(mesh):
    placed = (
        P(None, None, "gx", "gy"),
        P(None, None, "gx", "gy"),
        P("gx", "gy"),
        P(None, "gx", "gy"),
        P(None, "gx"),
        P("gx", "gy", None, None),
        P("gx", "gy", None),
        P(),
    )
    return jax.shard_map(
        per_device,
        mesh=mesh,
        in_specs=placed,
        out_specs=(P(None, None, "gx", "gy"), P(None, None, "gx", "gy"), P("gx", "gy", None)),
        check_vma=False,
    )
```

```python
import functools

import jax
import jax.numpy as jnp
import numpy as np
from jax import lax
from jax.experimental import pallas as pl
from jax.experimental.pallas import tpu as pltpu
from jax.sharding import PartitionSpec as P

NZ = 32
STEPS = 12
BROWS = 2
DB_DEV = 4

time_step = 0.5
omega_source = 1.3

ROWS = 32
TILES = 16
HALO = STEPS
XR = ROWS + 2 * HALO
HT = HALO // 4
YV = 24
PAD = 8
NARR = 14
NEAR = 8
FAR = 4
FARW = TILES + HT + 1
LANES = 128
HIGH = lax.Precision.HIGHEST


def shifted(array, axis, by):
    count = lax.axis_size(axis)
    return lax.ppermute(array, axis, [(i, (i + by) % count) for i in range(count)])


def dot(a, b):
    return jnp.dot(a, b, precision=HIGH, preferred_element_type=jnp.float32)


def iota(shape, axis):
    return lax.broadcasted_iota(jnp.int32, shape, axis)


def planes(e, h, eps, aux=None):
    out = [e.at[r, c] for r in range(2) for c in range(3)]
    out += [h.at[r, c] for r in range(2) for c in range(3)] + [eps]
    return out + ([] if aux is None else [aux])


def source_tags(profile, plane):
    half = LANES // 2
    c, l = iota((half, LANES), 0), iota((half, LANES), 1)
    strength = dot(profile[0], (l == c).astype(jnp.float32))
    strength = strength + dot(profile[1], (l == c + half).astype(jnp.float32))
    pick = (iota((2, LANES), 0) == iota((2, LANES), 1)).astype(jnp.float32)
    where = lax.dot_general(
        plane[...].astype(jnp.float32), pick, (((0,), (0,)), ((), ())), precision=HIGH, preferred_element_type=jnp.float32
    )
    return strength, where


def source_rows(strength, where):
    length = TILES * LANES
    half = LANES // 2
    c, l = iota((LANES, length), 0), iota((LANES, length), 1)
    spread = ((l // NZ == c % half) & (l % NZ == c // half)).astype(jnp.float32)
    level = iota((strength.shape[0], length), 1) % NZ
    out = dot(strength, spread)
    out = jnp.where(level == 2, where[:, 0:1], out)
    return jnp.where(level == 3, where[:, 1:2], out)


def fetch_tags(profile, plane, pv, lv, sems):
    copies = [
        pltpu.make_async_copy(profile, pv, sems.at[0]),
        pltpu.make_async_copy(plane, lv, sems.at[1]),
    ]
    for copy in copies:
        copy.start()
    return copies


def pack_side(e, h, eps, profile, plane, to_left, to_right, aux, pv, lv, sems):
    edge = HT * LANES
    length = TILES * LANES
    tags = fetch_tags(profile, plane, pv, lv, sems)
    copies = []
    for part, begin in ((to_left, 0), (to_right, length - edge)):
        for a, src in enumerate(planes(e, h, eps)):
            copies.append(
                pltpu.make_async_copy(
                    src.at[:, pl.ds(begin, edge)], part.at[a], sems.at[2 + len(copies)]
                )
            )
            copies[-1].start()
    for copy in tags:
        copy.wait()
    made = source_rows(*source_tags(pv, lv))
    aux[...] = made
    to_left[NARR - 1] = made[:, 0:edge]
    to_right[NARR - 1] = made[:, length - edge : length]
    for copy in copies:
        copy.wait()


def pack_near(e, h, eps, profile, plane, edge_p, edge_n, mid_p, mid_n, pv, lv, sems):
    edge = HT * LANES
    length = TILES * LANES
    inner = length - 2 * edge
    tags = fetch_tags(profile, plane, pv, lv, sems)
    copies = []
    for x, side, middle in ((0, edge_p, mid_p), (ROWS - NEAR, edge_n, mid_n)):
        for a, src in enumerate(planes(e, h, eps)):
            for part, begin, size, to in (
                (side, 0, edge, 2 * a * edge),
                (side, length - edge, edge, (2 * a + 1) * edge),
                (middle, edge, inner, a * inner),
            ):
                copies.append(
                    pltpu.make_async_copy(
                        src.at[pl.ds(x, NEAR), pl.ds(begin, size)],
                        part.at[:, pl.ds(to, size)],
                        sems.at[2 + len(copies)],
                    )
                )
                copies[-1].start()
    for copy in tags:
        copy.wait()
    for k, tag in enumerate(source_tags(pv, lv)):
        cols = pl.ds((NARR - 1) * 2 * edge + k * LANES, LANES)
        edge_p[:, cols] = tag[0:NEAR, :]
        edge_n[:, cols] = tag[ROWS - NEAR : ROWS, :]
    for copy in copies:
        copy.wait()


def near_source(ref):
    base = (NARR - 1) * 2 * HT * LANES
    return source_rows(ref[:, base : base + LANES], ref[:, base + LANES : base + 2 * LANES])


def pack_far(e, h, eps, aux, left, right, to_prev, to_next):
    edge = HT * LANES
    length = TILES * LANES
    lo, hi = NEAR, ROWS - NEAR - FAR
    for a, src in enumerate(planes(e, h, eps, aux)):
        p, q = a // 2, pl.ds(FAR * (a % 2), FAR)
        to_prev[p, q, 0:edge] = left[a, lo : lo + FAR, :]
        to_prev[p, q, edge : edge + length] = src[lo : lo + FAR, :]
        to_prev[p, q, edge + length :] = right[a, lo : lo + FAR, 0:LANES]
        to_next[p, q, 0:LANES] = left[a, hi : hi + FAR, edge - LANES : edge]
        to_next[p, q, LANES : LANES + length] = src[hi : hi + FAR, :]
        to_next[p, q, LANES + length :] = right[a, hi : hi + FAR, :]


def pack_corner(behind, ahead, to_left, to_right):
    edge = HT * LANES
    length = TILES * LANES
    for k, src in enumerate((behind, ahead)):
        made = near_source(src)
        rows = pl.ds(NEAR * k, NEAR)
        to_left[NARR - 1, rows, :] = made[:, 0:edge]
        to_right[NARR - 1, rows, :] = made[:, length - edge : length]
        for a in range(NARR - 1):
            to_left[a, rows, :] = src[:, 2 * a * edge : (2 * a + 1) * edge]
            to_right[a, rows, :] = src[:, (2 * a + 1) * edge : (2 * a + 2) * edge]


def at(a, x, v=0):
    return PAD + (a * XR + x) * YV + v


def place(dst, a, x, v, value):
    dst[pl.ds(at(a, x, v), value.shape[0], stride=YV), :] = value


def row(ref, a, x):
    return ref[pl.ds(pl.multiple_of(at(a, x), 8), YV), :]


def off(ref, a, x, by):
    return ref[pl.ds(at(a, x) + by, YV), :]


def put(ref, a, x, value):
    ref[pl.ds(pl.multiple_of(at(a, x), 8), YV), :] = value


def fill_sources(wa, ws, x, count):
    size = count * YV
    level = iota((size, LANES), 1) % NZ
    held = wa[pl.ds(at(0, x), size), :]
    held = jnp.where(level < 4, held, 0.0)
    i, j = iota((LANES, LANES), 0), iota((LANES, LANES), 1)
    for r in range(2):
        strength = dot(held, (i == (j // NZ) * NZ + r).astype(jnp.float32))
        where = dot(held, (i == (j // NZ) * NZ + 2 + r).astype(jnp.float32))
        ws[pl.ds(at(r, x), size), :] = jnp.where(level.astype(jnp.float32) == where, strength, 0.0)


def kinds(we, wh, wc, wa):
    def same(t):
        return t

    out = [(we, a, same) for a in range(6)]
    out += [(wh, a, lambda t: t * 2.0) for a in range(6)]
    return out + [(wc, 0, lambda t: 0.25 / t), (wa, 0, same)]


class Stepper:
    def __init__(self, waves, we, wh, wc, ws, acc):
        self.waves, self.we, self.wh, self.wc, self.ws, self.acc = waves, we, wh, wc, ws, acc
        lane = iota((YV, LANES), 1)
        self.up_keep = lane % NZ != NZ - 1
        self.down_keep = lane % NZ != 0
        self.first = lane < NZ
        self.last = lane >= LANES - NZ

    def up_z(self, t):
        return jnp.where(self.up_keep, pltpu.roll(t, LANES - 1, 1), 0.0)

    def down_z(self, t):
        return jnp.where(self.down_keep, pltpu.roll(t, 1, 1), 0.0)

    def up_y(self, t, after):
        return pltpu.roll(jnp.where(self.first, after, t), LANES - NZ, 1)

    def down_y(self, t, before):
        return pltpu.roll(jnp.where(self.last, before, t), NZ, 1)

    def magnetic_row(self, r, x):
        we, wh = self.we, self.wh
        ex, ey, ez = (row(we, 3 * r + c, x) for c in range(3))
        hx, hy, hz = (row(wh, 3 * r + c, x) for c in range(3))
        ey_x, ez_x = (row(we, 3 * r + c, x + 1) for c in (1, 2))
        ex_y = self.up_y(ex, off(we, 3 * r, x, 1))
        ez_y = self.up_y(ez, off(we, 3 * r + 2, x, 1))
        hx = hx - ((ez_y - ez) - (self.up_z(ey) - ey))
        hy = hy - ((self.up_z(ex) - ex) - (ez_x - ez))
        hz = hz - ((ey_x - ey) - (ex_y - ex))
        return (hx, hy, hz)

    def electric_row(self, r, x, c, wave):
        we, wh = self.we, self.wh
        hx, hy, hz = (row(wh, 3 * r + k, x) for k in range(3))
        hy_x, hz_x = (row(wh, 3 * r + k, x - 1) for k in (1, 2))
        hx_y = self.down_y(hx, off(wh, 3 * r, x, -1))
        hz_y = self.down_y(hz, off(wh, 3 * r + 2, x, -1))
        ex, ey, ez = (row(we, 3 * r + k, x) for k in range(3))
        ex = ex + c * ((hz - hz_y) - (hy - self.down_z(hy))) + wave * row(self.ws, r, x)
        ey = ey + c * ((hx - self.down_z(hx)) - (hz - hz_x))
        ez = ez + c * ((hy - hy_x) - (hx - hx_y))
        return (ex, ey, ez)

    def magnetic(self, x):
        for r in range(2):
            for k, value in enumerate(self.magnetic_row(r, x)):
                put(self.wh, 3 * r + k, x, value)

    def electric(self, x, wave):
        c = row(self.wc, 0, x)
        f = self.electric_row(0, x, c, wave)
        g = self.electric_row(1, x, c, wave)
        put(self.acc, 0, x, row(self.acc, 0, x) + (f[0] * g[0] + f[1] * g[1] + f[2] * g[2]))
        for k in range(3):
            put(self.we, k, x, f[k])
            put(self.we, 3 + k, x, g[k])

    def edges(self, low, high, count):
        def step(n, _):
            wave = self.waves[n]
            for i in range(count):
                self.magnetic(low + n + i)
                self.magnetic(high - n + i)
            for i in range(count):
                self.electric(low + 1 + n + i, wave)
                self.electric(high - n + i, wave)
            return 0

        lax.fori_loop(0, STEPS, step, 0)

    def inside(self, low, high):
        def sweep(one, x, count):
            def group(g, _):
                for i in range(8):
                    one(x + g * 8 + i)
                return 0

            lax.fori_loop(0, count // 8, group, 0)
            for size in (4, 2, 1):
                begin = x + count // (2 * size) * (2 * size)

                @pl.when(count % (2 * size) >= size)
                def _(size=size, begin=begin):
                    for i in range(size):
                        one(begin + i)

        def step(n, _):
            wave = self.waves[n]
            sweep(self.magnetic, low + n, high - low - 2 * n)
            sweep(lambda x: self.electric(x, wave), low + 1 + n, high - low - 1 - 2 * n)
            return 0

        lax.fori_loop(0, STEPS, step, 0)


def run_inside(waves, e, h, eps, aux, left, right, we, wh, wc, ws, acc, wa):
    own = planes(e, h, eps, aux)
    for n, (dst, a, fix) in enumerate(kinds(we, wh, wc, wa)):
        for i in range(ROWS // 8):
            rows = pl.ds(8 * i, 8)
            for j in range(TILES):
                place(dst, a, HALO + 8 * i, HT + j, fix(own[n][rows, pl.ds(j * LANES, LANES)]))
            for j in range(HT):
                cols = pl.ds(j * LANES, LANES)
                place(dst, a, HALO + 8 * i, j, fix(left[n, rows, cols]))
                place(dst, a, HALO + 8 * i, HT + TILES + j, fix(right[n, rows, cols]))
    fill_sources(wa, ws, HALO, ROWS)
    acc[...] = jnp.zeros_like(acc)
    Stepper(waves, we, wh, wc, ws, acc).inside(HALO, HALO + ROWS - 1)


def store_rows(we, wh, stage, e_out, h_out, sems, x, count):
    copies = []
    for a in range(6):
        for k, (src, out, scale) in enumerate(((we, e_out, None), (wh, h_out, 0.5))):
            for i in range(count // 8):
                for j in range(TILES):
                    value = src[pl.ds(at(a, HALO + x + 8 * i, HT + j), 8, stride=YV), :]
                    value = value if scale is None else value * scale
                    stage[6 * k + a, pl.ds(8 * i, 8), pl.ds(j * LANES, LANES)] = value
            copy = pltpu.make_async_copy(
                stage.at[6 * k + a], out.at[a // 3, a % 3, pl.ds(x, count), :], sems.at[6 * k + a]
            )
            copy.start()
            copies.append(copy)
    return copies


def run_near(waves, _e, _h, _c, _s, _t, edge_b, edge_a, mid_b, mid_a, corner_l, corner_r, e_out, h_out, we, wh, wc, ws, acc, wa, made, stage, sems):
    edge = HT * LANES
    inner = (TILES - 2 * HT) * LANES

    def near_tile(side, middle, n, j):
        if n == NARR - 1:
            return made[:, pl.ds(j * LANES, LANES)]
        if HT <= j < TILES - HT:
            return middle[:, pl.ds(n * inner + (j - HT) * LANES, LANES)]
        j = j if j < HT else j - (TILES - 2 * HT)
        return side[:, pl.ds(2 * n * edge + j * LANES, LANES)]

    for k, (side, middle, x) in enumerate(
        ((edge_b, mid_b, FAR), (edge_a, mid_a, HALO + ROWS))
    ):
        made[...] = near_source(side)
        rows = pl.ds(NEAR * k, NEAR)
        for n, (dst, a, fix) in enumerate(kinds(we, wh, wc, wa)):
            for j in range(TILES):
                place(dst, a, x, HT + j, fix(near_tile(side, middle, n, j)))
            for j in range(HT):
                cols = pl.ds(j * LANES, LANES)
                place(dst, a, x, j, fix(corner_l[n, rows, cols]))
                place(dst, a, x, HT + TILES + j, fix(corner_r[n, rows, cols]))
        fill_sources(wa, ws, x, NEAR)
    Stepper(waves, we, wh, wc, ws, acc).edges(FAR, HALO + ROWS - 1, NEAR)
    for copy in store_rows(we, wh, stage, e_out, h_out, sems, 8, 16):
        copy.wait()


def run_far(
    waves, _e, _h, _c, _s, _t, _x, _y, far_b, far_a, select, marks, e_out, h_out, packed, we, wh, wc, ws, acc, wa, stage_lo, stage_hi, sems
):
    for n, (dst, a, fix) in enumerate(kinds(we, wh, wc, wa)):
        q = pl.ds(FAR * (n % 2), FAR)
        for j in range(FARW):
            cols = pl.ds(j * LANES, LANES)
            place(dst, a, 0, HT - 1 + j, fix(far_b[n // 2, q, cols]))
            place(dst, a, XR - FAR, j, fix(far_a[n // 2, q, cols]))
    fill_sources(wa, ws, 0, FAR)
    fill_sources(wa, ws, XR - FAR, FAR)
    Stepper(waves, we, wh, wc, ws, acc).edges(0, XR - FAR - 1, FAR)

    stores = store_rows(we, wh, stage_lo, e_out, h_out, sems, 0, 8)
    stores += store_rows(we, wh, stage_hi, e_out, h_out, sems.at[pl.ds(12, 12)], 24, 8)
    i, j = iota((LANES, LANES), 0), iota((LANES, LANES), 1)
    sums = dot(acc[pl.ds(at(0, HALO), ROWS * YV), :], (i // NZ == j % 4).astype(jnp.float32))
    per = BROWS * YV
    p, q = iota((per, LANES), 0), iota((per, LANES), 1)
    half = LANES // BROWS
    keep = (p // YV == q // half) & ((q % half) // 4 == p % YV - HT)
    blocks = jnp.sum(
        jnp.where(keep[None], sums.reshape(ROWS // BROWS, per, LANES), 0.0), axis=1
    ) / (STEPS * NZ)
    packed[...] = dot(select[...], blocks) + marks[...]
    for copy in stores:
        copy.wait()


def collect(received, filter_matrix, out):
    rec = received[...]
    places = rec.shape[0]
    p = lax.broadcasted_iota(jnp.int32, (places, places), 0)
    q = lax.broadcasted_iota(jnp.int32, (places, places), 1)
    pick = (q == (p // 3) * 3 + 2).astype(jnp.float32)
    labels = jnp.dot(pick, rec, precision=HIGH, preferred_element_type=jnp.float32)
    pr = lax.broadcasted_iota(jnp.int32, (places, LANES), 0)
    ln = lax.broadcasted_iota(jnp.int32, (places, LANES), 1)
    label = jnp.sum(jnp.where((ln == pr % 3) & (pr % 3 < 2), labels, 0.0), axis=1, keepdims=True)
    want = lax.broadcasted_iota(jnp.int32, (places, 8), 1) + 1
    choose = (label == want.astype(jnp.float32)).astype(jnp.float32)
    design = lax.dot_general(
        choose, rec, (((0,), (0,)), ((), ())), precision=HIGH, preferred_element_type=jnp.float32
    )
    result = jnp.dot(
        design, filter_matrix[...], precision=HIGH, preferred_element_type=jnp.float32
    )
    out[...] = result[0:DB_DEV]


def call(kernel, out_shape, count, micros, limit=32, **kwargs):
    vmem = pl.BlockSpec(memory_space=pltpu.VMEM)
    outs = tuple(jax.ShapeDtypeStruct(shape, jnp.float32) for shape in out_shape)
    return pl.pallas_call(
        kernel,
        in_specs=kwargs.pop("in_specs", [vmem] * count),
        out_specs=kwargs.pop("out_specs", (vmem,) * len(outs)),
        out_shape=outs,
        compiler_params=pltpu.CompilerParams(vmem_limit_bytes=limit * 1024 * 1024),
        name=kernel.__name__,
        cost_estimate=pl.CostEstimate(
            flops=0, transcendentals=0, bytes_accessed=micros * 3_000_000
        ),
        **kwargs,
    )


def per_device(
    electric,
    magnetic,
    permittivity,
    source_profile,
    source_plane,
    block_owner,
    design_slot,
    filter_matrix,
):
    length = TILES * LANES
    edge = HT * LANES
    raw = (electric, magnetic, permittivity, source_profile, source_plane)
    vmem = pl.BlockSpec(memory_space=pltpu.VMEM)
    smem = pl.BlockSpec(memory_space=pltpu.SMEM)
    hbm = pl.BlockSpec(memory_space=pltpu.HBM)
    raw = tuple(pltpu.with_memory_space_constraint(t, pltpu.HBM) for t in raw)

    def packing(copies):
        return dict(
            in_specs=[hbm] * 5,
            scratch_shapes=[
                pltpu.VMEM(source_profile.shape, jnp.float32),
                pltpu.VMEM(source_plane.shape, jnp.int32),
                pltpu.SemaphoreType.DMA((2 + copies,)),
            ],
        )

    x_edge = (NEAR, (NARR - 1) * 2 * edge + 2 * LANES)
    x_mid = (NEAR, (NARR - 1) * (length - 2 * edge))
    edge_prev, edge_next, mid_prev, mid_next = call(
        pack_near, (x_edge, x_edge, x_mid, x_mid), 5, 2, **packing(6 * (NARR - 1))
    )(*raw)
    edge_prev, edge_next, raw = lax.optimization_barrier((edge_prev, edge_next, raw))
    edge_b = shifted(edge_next, "gx", 1)
    edge_a = shifted(edge_prev, "gx", -1)

    y_own = (NARR, ROWS, edge)
    to_left, to_right, aux = call(
        pack_side, (y_own, y_own, (ROWS, length)), 5, 3, **packing(2 * (NARR - 1))
    )(*raw)
    left = shifted(to_right, "gy", 1)
    right = shifted(to_left, "gy", -1)

    y_corner = (NARR, 2 * NEAR, edge)
    made = pltpu.VMEM((NEAR, length), jnp.float32)
    corner_left, corner_right = call(pack_corner, (y_corner, y_corner), 2, 2)(edge_b, edge_a)
    corner_left, corner_right, mid_prev, mid_next = lax.optimization_barrier(
        (corner_left, corner_right, mid_prev, mid_next)
    )
    corner_l = shifted(corner_right, "gy", 1)
    corner_r = shifted(corner_left, "gy", -1)
    mid_b = shifted(mid_next, "gx", 1)
    mid_a = shifted(mid_prev, "gx", -1)

    own = (electric, magnetic, permittivity, aux)
    x_far = (NARR // 2, 2 * FAR, FARW * LANES)
    far_prev, far_next = call(pack_far, (x_far, x_far), 6, 2)(*own, left, right)
    far_prev, far_next, left, right, corner_l, corner_r = lax.optimization_barrier(
        (far_prev, far_next, left, right, corner_l, corner_r)
    )
    waves = jnp.asarray(
        time_step
        * np.sin(np.arange(1, STEPS + 1).astype(np.float32) * np.float32(omega_source * time_step)),
        jnp.float32,
    )
    field = (2, 3, ROWS, length)
    many = XR * YV
    tail = PAD + YV
    held = tuple((k * many + tail, LANES) for k in (6, 6, 1, 2, 1))
    tags = pltpu.VMEM((many + tail, LANES), jnp.float32)
    state = call(run_inside, held, 7, 15, in_specs=[smem] + [vmem] * 6, scratch_shapes=[tags])(
        waves, *own, left, right
    )
    far_prev, far_next, state = lax.optimization_barrier((far_prev, far_next, state))
    far_b = shifted(far_next, "gx", 1)
    far_a = shifted(far_prev, "gx", -1)

    count = ROWS // BROWS
    owner = block_owner[0, 0, :, 0]
    slot = design_slot[0, 0, :]
    owners = lax.axis_size("gy")
    index = jnp.arange(count, dtype=jnp.int32)
    earlier = (
        ((owner[:, None] == owner[None, :]) & (index[None, :] < index[:, None]))
        .astype(jnp.int32)
        .sum(1)
    )
    places = jnp.arange(3 * owners, dtype=jnp.int32)
    chosen = (places[:, None] == (owner * 3 + earlier)[None, :]).astype(jnp.float32)
    lane = jnp.arange(LANES, dtype=jnp.int32)
    holder = (places[:, None] == (owner * 3 + 2)[None, :]).astype(jnp.float32)
    named = (lane[None, :] == earlier[:, None]).astype(jnp.float32) * (slot + 1).astype(
        jnp.float32
    )[:, None]
    marks = jnp.dot(holder, named, precision=HIGH)

    copy_sem = pltpu.SemaphoreType.DMA
    state = call(
        run_near,
        (field, field) + held,
        12,
        12,
        in_specs=[smem] + [vmem] * 11,
        out_specs=(hbm,) * 2 + (vmem,) * 5,
        scratch_shapes=[tags, made, pltpu.VMEM((12, 16, length), jnp.float32), copy_sem((12,))],
        input_output_aliases={1 + k: 2 + k for k in range(5)},
    )(waves, *state, edge_b, edge_a, mid_b, mid_a, corner_l, corner_r)
    stage = pltpu.VMEM((12, 8, length), jnp.float32)
    out = call(
        run_far,
        (field, field, (3 * owners, LANES)) + held,
        12,
        8,
        in_specs=[smem] + [vmem] * 5 + [hbm] * 2 + [vmem] * 4,
        out_specs=(hbm,) * 2 + (vmem,) * 6,
        scratch_shapes=[tags, stage, stage, copy_sem((24,))],
        input_output_aliases={6: 0, 7: 1} | {1 + k: 3 + k for k in range(5)},
    )(waves, *state[2:], *state[:2], far_b, far_a, chosen, marks)
    field_e, field_h, packed = out[:3]
    received = lax.all_to_all(
        packed.reshape(owners, 3, LANES), "gy", split_axis=0, concat_axis=0, tiled=True
    )
    (result,) = call(collect, ((DB_DEV, LANES),), 2, 1)(
        received.reshape(3 * owners, LANES), filter_matrix
    )
    return (field_e, field_h, result[None])


def solution(mesh):
    placed = (
        P(None, None, "gx", "gy"),
        P(None, None, "gx", "gy"),
        P("gx", "gy"),
        P(None, "gx", "gy"),
        P(None, "gx"),
        P("gx", "gy", None, None),
        P("gx", "gy", None),
        P(),
    )
    return jax.shard_map(
        per_device,
        mesh=mesh,
        in_specs=placed,
        out_specs=(P(None, None, "gx", "gy"), P(None, None, "gx", "gy"), P("gx", "gy", None)),
        check_vma=False,
    )
```

```python
import functools

import jax
import jax.numpy as jnp
import numpy as np
from jax import lax
from jax.experimental import pallas as pl
from jax.experimental.pallas import tpu as pltpu
from jax.sharding import PartitionSpec as P

NZ = 32
STEPS = 12
BROWS = 2
DB_DEV = 4

time_step = 0.5
omega_source = 1.3

ROWS = 32
TILES = 16
HALO = STEPS
XR = ROWS + 2 * HALO
HT = HALO // 4
YV = 24
PAD = 8
NARR = 14
NEAR = 8
FAR = 4
FARW = TILES + HT + 1
LANES = 128
HIGH = lax.Precision.HIGHEST


def shifted(array, axis, by):
    count = lax.axis_size(axis)
    return lax.ppermute(array, axis, [(i, (i + by) % count) for i in range(count)])


def dot(a, b):
    return jnp.dot(a, b, precision=HIGH, preferred_element_type=jnp.float32)


def iota(shape, axis):
    return lax.broadcasted_iota(jnp.int32, shape, axis)


def planes(e, h, eps, aux=None):
    out = [e.at[r, c] for r in range(2) for c in range(3)]
    out += [h.at[r, c] for r in range(2) for c in range(3)] + [eps]
    return out + ([] if aux is None else [aux])


def source_tags(profile, plane):
    half = LANES // 2
    c, l = iota((half, LANES), 0), iota((half, LANES), 1)
    strength = dot(profile[0], (l == c).astype(jnp.float32))
    strength = strength + dot(profile[1], (l == c + half).astype(jnp.float32))
    pick = (iota((2, LANES), 0) == iota((2, LANES), 1)).astype(jnp.float32)
    where = lax.dot_general(
        plane[...].astype(jnp.float32), pick, (((0,), (0,)), ((), ())), precision=HIGH, preferred_element_type=jnp.float32
    )
    return strength, where


def source_rows(strength, where):
    length = TILES * LANES
    half = LANES // 2
    c, l = iota((LANES, length), 0), iota((LANES, length), 1)
    spread = ((l // NZ == c % half) & (l % NZ == c // half)).astype(jnp.float32)
    level = iota((strength.shape[0], length), 1) % NZ
    out = dot(strength, spread)
    out = jnp.where(level == 2, where[:, 0:1], out)
    return jnp.where(level == 3, where[:, 1:2], out)


def fetch_tags(profile, plane, pv, lv, sems):
    copies = [
        pltpu.make_async_copy(profile, pv, sems.at[0]),
        pltpu.make_async_copy(plane, lv, sems.at[1]),
    ]
    for copy in copies:
        copy.start()
    return copies


def pack_side(e, h, eps, profile, plane, to_left, to_right, aux, pv, lv, sems):
    edge = HT * LANES
    length = TILES * LANES
    tags = fetch_tags(profile, plane, pv, lv, sems)
    copies = []
    for part, begin in ((to_left, 0), (to_right, length - edge)):
        for a, src in enumerate(planes(e, h, eps)):
            copies.append(
                pltpu.make_async_copy(
                    src.at[:, pl.ds(begin, edge)], part.at[a], sems.at[2 + len(copies)]
                )
            )
            copies[-1].start()
    for copy in tags:
        copy.wait()
    made = source_rows(*source_tags(pv, lv))
    aux[...] = made
    to_left[NARR - 1] = made[:, 0:edge]
    to_right[NARR - 1] = made[:, length - edge : length]
    for copy in copies:
        copy.wait()


def pack_near(e, h, eps, profile, plane, edge_p, edge_n, mid_p, mid_n, pv, lv, sems):
    edge = HT * LANES
    length = TILES * LANES
    inner = length - 2 * edge
    tags = fetch_tags(profile, plane, pv, lv, sems)
    copies = []
    for x, side, middle in ((0, edge_p, mid_p), (ROWS - NEAR, edge_n, mid_n)):
        for a, src in enumerate(planes(e, h, eps)):
            for part, begin, size, to in (
                (side, 0, edge, 2 * a * edge),
                (side, length - edge, edge, (2 * a + 1) * edge),
                (middle, edge, inner, a * inner),
            ):
                copies.append(
                    pltpu.make_async_copy(
                        src.at[pl.ds(x, NEAR), pl.ds(begin, size)],
                        part.at[:, pl.ds(to, size)],
                        sems.at[2 + len(copies)],
                    )
                )
                copies[-1].start()
    for copy in tags:
        copy.wait()
    for k, tag in enumerate(source_tags(pv, lv)):
        cols = pl.ds((NARR - 1) * 2 * edge + k * LANES, LANES)
        edge_p[:, cols] = tag[0:NEAR, :]
        edge_n[:, cols] = tag[ROWS - NEAR : ROWS, :]
    for copy in copies:
        copy.wait()


def near_source(ref):
    base = (NARR - 1) * 2 * HT * LANES
    return source_rows(ref[:, base : base + LANES], ref[:, base + LANES : base + 2 * LANES])


def pack_far(e, h, eps, aux, left, right, to_prev, to_next):
    edge = HT * LANES
    length = TILES * LANES
    lo, hi = NEAR, ROWS - NEAR - FAR
    for a, src in enumerate(planes(e, h, eps, aux)):
        p, q = a // 2, pl.ds(FAR * (a % 2), FAR)
        to_prev[p, q, 0:edge] = left[a, lo : lo + FAR, :]
        to_prev[p, q, edge : edge + length] = src[lo : lo + FAR, :]
        to_prev[p, q, edge + length :] = right[a, lo : lo + FAR, 0:LANES]
        to_next[p, q, 0:LANES] = left[a, hi : hi + FAR, edge - LANES : edge]
        to_next[p, q, LANES : LANES + length] = src[hi : hi + FAR, :]
        to_next[p, q, LANES + length :] = right[a, hi : hi + FAR, :]


def pack_corner(behind, ahead, to_left, to_right):
    edge = HT * LANES
    length = TILES * LANES
    for k, src in enumerate((behind, ahead)):
        made = near_source(src)
        rows = pl.ds(NEAR * k, NEAR)
        to_left[NARR - 1, rows, :] = made[:, 0:edge]
        to_right[NARR - 1, rows, :] = made[:, length - edge : length]
        for a in range(NARR - 1):
            to_left[a, rows, :] = src[:, 2 * a * edge : (2 * a + 1) * edge]
            to_right[a, rows, :] = src[:, (2 * a + 1) * edge : (2 * a + 2) * edge]


def at(a, x, v=0):
    return PAD + (a * XR + x) * YV + v


def place(dst, a, x, v, value):
    dst[pl.ds(at(a, x, v), value.shape[0], stride=YV), :] = value


def row(ref, a, x):
    return ref[pl.ds(pl.multiple_of(at(a, x), 8), YV), :]


def off(ref, a, x, by):
    return ref[pl.ds(at(a, x) + by, YV), :]


def put(ref, a, x, value):
    ref[pl.ds(pl.multiple_of(at(a, x), 8), YV), :] = value


def fill_sources(wa, ws, x, count):
    size = count * YV
    level = iota((size, LANES), 1) % NZ
    held = wa[pl.ds(at(0, x), size), :]
    held = jnp.where(level < 4, held, 0.0)
    i, j = iota((LANES, LANES), 0), iota((LANES, LANES), 1)
    for r in range(2):
        strength = dot(held, (i == (j // NZ) * NZ + r).astype(jnp.float32))
        where = dot(held, (i == (j // NZ) * NZ + 2 + r).astype(jnp.float32))
        ws[pl.ds(at(r, x), size), :] = jnp.where(level.astype(jnp.float32) == where, strength, 0.0)


def kinds(we, wh, wc, wa):
    def same(t):
        return t

    out = [(we, a, same) for a in range(6)]
    out += [(wh, a, lambda t: t * 2.0) for a in range(6)]
    return out + [(wc, 0, lambda t: 0.25 / t), (wa, 0, same)]


class Stepper:
    def __init__(self, waves, we, wh, wc, ws, acc):
        self.waves, self.we, self.wh, self.wc, self.ws, self.acc = waves, we, wh, wc, ws, acc
        lane = iota((YV, LANES), 1)
        self.up_keep = lane % NZ != NZ - 1
        self.down_keep = lane % NZ != 0
        self.first = lane < NZ
        self.last = lane >= LANES - NZ

    def up_z(self, t):
        return jnp.where(self.up_keep, pltpu.roll(t, LANES - 1, 1), 0.0)

    def down_z(self, t):
        return jnp.where(self.down_keep, pltpu.roll(t, 1, 1), 0.0)

    def up_y(self, t, after):
        return pltpu.roll(jnp.where(self.first, after, t), LANES - NZ, 1)

    def down_y(self, t, before):
        return pltpu.roll(jnp.where(self.last, before, t), NZ, 1)

    def magnetic_row(self, r, x):
        we, wh = self.we, self.wh
        ex, ey, ez = (row(we, 3 * r + c, x) for c in range(3))
        hx, hy, hz = (row(wh, 3 * r + c, x) for c in range(3))
        ey_x, ez_x = (row(we, 3 * r + c, x + 1) for c in (1, 2))
        ex_y = self.up_y(ex, off(we, 3 * r, x, 1))
        ez_y = self.up_y(ez, off(we, 3 * r + 2, x, 1))
        hx = hx - ((ez_y - ez) - (self.up_z(ey) - ey))
        hy = hy - ((self.up_z(ex) - ex) - (ez_x - ez))
        hz = hz - ((ey_x - ey) - (ex_y - ex))
        return (hx, hy, hz)

    def electric_row(self, r, x, c, wave):
        we, wh = self.we, self.wh
        hx, hy, hz = (row(wh, 3 * r + k, x) for k in range(3))
        hy_x, hz_x = (row(wh, 3 * r + k, x - 1) for k in (1, 2))
        hx_y = self.down_y(hx, off(wh, 3 * r, x, -1))
        hz_y = self.down_y(hz, off(wh, 3 * r + 2, x, -1))
        ex, ey, ez = (row(we, 3 * r + k, x) for k in range(3))
        ex = ex + c * ((hz - hz_y) - (hy - self.down_z(hy))) + wave * row(self.ws, r, x)
        ey = ey + c * ((hx - self.down_z(hx)) - (hz - hz_x))
        ez = ez + c * ((hy - hy_x) - (hx - hx_y))
        return (ex, ey, ez)

    def magnetic(self, x):
        for r in range(2):
            for k, value in enumerate(self.magnetic_row(r, x)):
                put(self.wh, 3 * r + k, x, value)

    def electric(self, x, wave):
        c = row(self.wc, 0, x)
        f = self.electric_row(0, x, c, wave)
        g = self.electric_row(1, x, c, wave)
        put(self.acc, 0, x, row(self.acc, 0, x) + (f[0] * g[0] + f[1] * g[1] + f[2] * g[2]))
        for k in range(3):
            put(self.we, k, x, f[k])
            put(self.we, 3 + k, x, g[k])

    def edges(self, low, high, count):
        def step(n, _):
            wave = self.waves[n]
            for i in range(count):
                self.magnetic(low + n + i)
                self.magnetic(high - n + i)
            for i in range(count):
                self.electric(low + 1 + n + i, wave)
                self.electric(high - n + i, wave)
            return 0

        lax.fori_loop(0, STEPS, step, 0)

    def inside(self, low, high):
        def sweep(one, x, count):
            def group(g, _):
                for i in range(8):
                    one(x + g * 8 + i)
                return 0

            lax.fori_loop(0, count // 8, group, 0)
            for size in (4, 2, 1):
                begin = x + count // (2 * size) * (2 * size)

                @pl.when(count % (2 * size) >= size)
                def _(size=size, begin=begin):
                    for i in range(size):
                        one(begin + i)

        def step(n, _):
            wave = self.waves[n]
            sweep(self.magnetic, low + n, high - low - 2 * n)
            sweep(lambda x: self.electric(x, wave), low + 1 + n, high - low - 1 - 2 * n)
            return 0

        lax.fori_loop(0, STEPS, step, 0)


def run_inside(waves, e, h, eps, aux, left, right, we, wh, wc, ws, acc, wa):
    own = planes(e, h, eps, aux)
    for n, (dst, a, fix) in enumerate(kinds(we, wh, wc, wa)):
        for i in range(ROWS // 8):
            rows = pl.ds(8 * i, 8)
            for j in range(TILES):
                place(dst, a, HALO + 8 * i, HT + j, fix(own[n][rows, pl.ds(j * LANES, LANES)]))
            for j in range(HT):
                cols = pl.ds(j * LANES, LANES)
                place(dst, a, HALO + 8 * i, j, fix(left[n, rows, cols]))
                place(dst, a, HALO + 8 * i, HT + TILES + j, fix(right[n, rows, cols]))
    fill_sources(wa, ws, HALO, ROWS)
    acc[...] = jnp.zeros_like(acc)
    Stepper(waves, we, wh, wc, ws, acc).inside(HALO, HALO + ROWS - 1)


def store_rows(we, wh, stage, e_out, h_out, sems, x, count):
    copies = []
    for a in range(6):
        for k, (src, out, scale) in enumerate(((we, e_out, None), (wh, h_out, 0.5))):
            for i in range(count // 8):
                for j in range(TILES):
                    value = src[pl.ds(at(a, HALO + x + 8 * i, HT + j), 8, stride=YV), :]
                    value = value if scale is None else value * scale
                    stage[6 * k + a, pl.ds(8 * i, 8), pl.ds(j * LANES, LANES)] = value
            copy = pltpu.make_async_copy(
                stage.at[6 * k + a], out.at[a // 3, a % 3, pl.ds(x, count), :], sems.at[6 * k + a]
            )
            copy.start()
            copies.append(copy)
    return copies


def run_near(waves, _e, _h, _c, _s, _t, edge_b, edge_a, mid_b, mid_a, corner_l, corner_r, e_out, h_out, we, wh, wc, ws, acc, wa, made, stage, sems):
    edge = HT * LANES
    inner = (TILES - 2 * HT) * LANES

    def near_tile(side, middle, n, j):
        if n == NARR - 1:
            return made[:, pl.ds(j * LANES, LANES)]
        if HT <= j < TILES - HT:
            return middle[:, pl.ds(n * inner + (j - HT) * LANES, LANES)]
        j = j if j < HT else j - (TILES - 2 * HT)
        return side[:, pl.ds(2 * n * edge + j * LANES, LANES)]

    for k, (side, middle, x) in enumerate(
        ((edge_b, mid_b, FAR), (edge_a, mid_a, HALO + ROWS))
    ):
        made[...] = near_source(side)
        rows = pl.ds(NEAR * k, NEAR)
        for n, (dst, a, fix) in enumerate(kinds(we, wh, wc, wa)):
            for j in range(TILES):
                place(dst, a, x, HT + j, fix(near_tile(side, middle, n, j)))
            for j in range(HT):
                cols = pl.ds(j * LANES, LANES)
                place(dst, a, x, j, fix(corner_l[n, rows, cols]))
                place(dst, a, x, HT + TILES + j, fix(corner_r[n, rows, cols]))
        fill_sources(wa, ws, x, NEAR)
    Stepper(waves, we, wh, wc, ws, acc).edges(FAR, HALO + ROWS - 1, NEAR)
    for copy in store_rows(we, wh, stage, e_out, h_out, sems, 8, 16):
        copy.wait()


def run_far(
    waves, _e, _h, _c, _s, _t, _x, _y, far_b, far_a, select, marks, e_out, h_out, packed, we, wh, wc, ws, acc, wa, stage_lo, stage_hi, sems
):
    for n, (dst, a, fix) in enumerate(kinds(we, wh, wc, wa)):
        q = pl.ds(FAR * (n % 2), FAR)
        for j in range(FARW):
            cols = pl.ds(j * LANES, LANES)
            place(dst, a, 0, HT - 1 + j, fix(far_b[n // 2, q, cols]))
            place(dst, a, XR - FAR, j, fix(far_a[n // 2, q, cols]))
    fill_sources(wa, ws, 0, FAR)
    fill_sources(wa, ws, XR - FAR, FAR)
    Stepper(waves, we, wh, wc, ws, acc).edges(0, XR - FAR - 1, FAR)

    stores = store_rows(we, wh, stage_lo, e_out, h_out, sems, 0, 8)
    stores += store_rows(we, wh, stage_hi, e_out, h_out, sems.at[pl.ds(12, 12)], 24, 8)
    i, j = iota((LANES, LANES), 0), iota((LANES, LANES), 1)
    sums = dot(acc[pl.ds(at(0, HALO), ROWS * YV), :], (i // NZ == j % 4).astype(jnp.float32))
    per = BROWS * YV
    p, q = iota((per, LANES), 0), iota((per, LANES), 1)
    half = LANES // BROWS
    keep = (p // YV == q // half) & ((q % half) // 4 == p % YV - HT)
    blocks = jnp.sum(
        jnp.where(keep[None], sums.reshape(ROWS // BROWS, per, LANES), 0.0), axis=1
    ) / (STEPS * NZ)
    packed[...] = dot(select[...], blocks) + marks[...]
    for copy in stores:
        copy.wait()


def collect(received, filter_matrix, out):
    rec = received[...]
    places = rec.shape[0]
    p = lax.broadcasted_iota(jnp.int32, (places, places), 0)
    q = lax.broadcasted_iota(jnp.int32, (places, places), 1)
    pick = (q == (p // 3) * 3 + 2).astype(jnp.float32)
    labels = jnp.dot(pick, rec, precision=HIGH, preferred_element_type=jnp.float32)
    pr = lax.broadcasted_iota(jnp.int32, (places, LANES), 0)
    ln = lax.broadcasted_iota(jnp.int32, (places, LANES), 1)
    label = jnp.sum(jnp.where((ln == pr % 3) & (pr % 3 < 2), labels, 0.0), axis=1, keepdims=True)
    want = lax.broadcasted_iota(jnp.int32, (places, 8), 1) + 1
    choose = (label == want.astype(jnp.float32)).astype(jnp.float32)
    design = lax.dot_general(
        choose, rec, (((0,), (0,)), ((), ())), precision=HIGH, preferred_element_type=jnp.float32
    )
    result = jnp.dot(
        design, filter_matrix[...], precision=HIGH, preferred_element_type=jnp.float32
    )
    out[...] = result[0:DB_DEV]


def call(kernel, out_shape, count, micros, limit=32, **kwargs):
    vmem = pl.BlockSpec(memory_space=pltpu.VMEM)
    outs = tuple(jax.ShapeDtypeStruct(shape, jnp.float32) for shape in out_shape)
    return pl.pallas_call(
        kernel,
        in_specs=kwargs.pop("in_specs", [vmem] * count),
        out_specs=kwargs.pop("out_specs", (vmem,) * len(outs)),
        out_shape=outs,
        compiler_params=pltpu.CompilerParams(vmem_limit_bytes=limit * 1024 * 1024),
        name=kernel.__name__,
        cost_estimate=pl.CostEstimate(
            flops=0, transcendentals=0, bytes_accessed=micros * 3_000_000
        ),
        **kwargs,
    )


def per_device(
    electric,
    magnetic,
    permittivity,
    source_profile,
    source_plane,
    block_owner,
    design_slot,
    filter_matrix,
):
    length = TILES * LANES
    edge = HT * LANES
    raw = (electric, magnetic, permittivity, source_profile, source_plane)
    vmem = pl.BlockSpec(memory_space=pltpu.VMEM)
    smem = pl.BlockSpec(memory_space=pltpu.SMEM)
    hbm = pl.BlockSpec(memory_space=pltpu.HBM)
    raw = tuple(pltpu.with_memory_space_constraint(t, pltpu.HBM) for t in raw)

    def packing(copies):
        return dict(
            in_specs=[hbm] * 5,
            scratch_shapes=[
                pltpu.VMEM(source_profile.shape, jnp.float32),
                pltpu.VMEM(source_plane.shape, jnp.int32),
                pltpu.SemaphoreType.DMA((2 + copies,)),
            ],
        )

    x_edge = (NEAR, (NARR - 1) * 2 * edge + 2 * LANES)
    x_mid = (NEAR, (NARR - 1) * (length - 2 * edge))
    edge_prev, edge_next, mid_prev, mid_next = call(
        pack_near, (x_edge, x_edge, x_mid, x_mid), 5, 2, **packing(6 * (NARR - 1))
    )(*raw)
    edge_prev, edge_next, raw = lax.optimization_barrier((edge_prev, edge_next, raw))
    edge_b = shifted(edge_next, "gx", 1)
    edge_a = shifted(edge_prev, "gx", -1)

    y_own = (NARR, ROWS, edge)
    to_left, to_right, aux = call(
        pack_side, (y_own, y_own, (ROWS, length)), 5, 3, **packing(2 * (NARR - 1))
    )(*raw)
    edge_b, edge_a, to_left, to_right = lax.optimization_barrier(
        (edge_b, edge_a, to_left, to_right)
    )
    left = shifted(to_right, "gy", 1)
    right = shifted(to_left, "gy", -1)

    y_corner = (NARR, 2 * NEAR, edge)
    made = pltpu.VMEM((NEAR, length), jnp.float32)
    corner_left, corner_right = call(pack_corner, (y_corner, y_corner), 2, 2)(edge_b, edge_a)
    corner_l = shifted(corner_right, "gy", 1)
    corner_r = shifted(corner_left, "gy", -1)
    corner_l, corner_r, left, right, mid_prev, mid_next = lax.optimization_barrier(
        (corner_l, corner_r, left, right, mid_prev, mid_next)
    )
    mid_b = shifted(mid_next, "gx", 1)
    mid_a = shifted(mid_prev, "gx", -1)

    own = (electric, magnetic, permittivity, aux)
    x_far = (NARR // 2, 2 * FAR, FARW * LANES)
    far_prev, far_next = call(pack_far, (x_far, x_far), 6, 2)(*own, left, right)
    far_prev, far_next, left, right = lax.optimization_barrier((far_prev, far_next, left, right))
    waves = jnp.asarray(
        time_step
        * np.sin(np.arange(1, STEPS + 1).astype(np.float32) * np.float32(omega_source * time_step)),
        jnp.float32,
    )
    field = (2, 3, ROWS, length)
    many = XR * YV
    tail = PAD + YV
    held = tuple((k * many + tail, LANES) for k in (6, 6, 1, 2, 1))
    tags = pltpu.VMEM((many + tail, LANES), jnp.float32)
    state = call(run_inside, held, 7, 15, in_specs=[smem] + [vmem] * 6, scratch_shapes=[tags])(
        waves, *own, left, right
    )
    far_prev, far_next, state = lax.optimization_barrier((far_prev, far_next, state))
    far_b = shifted(far_next, "gx", 1)
    far_a = shifted(far_prev, "gx", -1)

    count = ROWS // BROWS
    owner = block_owner[0, 0, :, 0]
    slot = design_slot[0, 0, :]
    owners = lax.axis_size("gy")
    index = jnp.arange(count, dtype=jnp.int32)
    earlier = (
        ((owner[:, None] == owner[None, :]) & (index[None, :] < index[:, None]))
        .astype(jnp.int32)
        .sum(1)
    )
    places = jnp.arange(3 * owners, dtype=jnp.int32)
    chosen = (places[:, None] == (owner * 3 + earlier)[None, :]).astype(jnp.float32)
    lane = jnp.arange(LANES, dtype=jnp.int32)
    holder = (places[:, None] == (owner * 3 + 2)[None, :]).astype(jnp.float32)
    named = (lane[None, :] == earlier[:, None]).astype(jnp.float32) * (slot + 1).astype(
        jnp.float32
    )[:, None]
    marks = jnp.dot(holder, named, precision=HIGH)

    copy_sem = pltpu.SemaphoreType.DMA
    state = call(
        run_near,
        (field, field) + held,
        12,
        12,
        in_specs=[smem] + [vmem] * 11,
        out_specs=(hbm,) * 2 + (vmem,) * 5,
        scratch_shapes=[tags, made, pltpu.VMEM((12, 16, length), jnp.float32), copy_sem((12,))],
        input_output_aliases={1 + k: 2 + k for k in range(5)},
    )(waves, *state, edge_b, edge_a, mid_b, mid_a, corner_l, corner_r)
    stage = pltpu.VMEM((12, 8, length), jnp.float32)
    out = call(
        run_far,
        (field, field, (3 * owners, LANES)) + held,
        12,
        8,
        in_specs=[smem] + [vmem] * 5 + [hbm] * 2 + [vmem] * 4,
        out_specs=(hbm,) * 2 + (vmem,) * 6,
        scratch_shapes=[tags, stage, stage, copy_sem((24,))],
        input_output_aliases={6: 0, 7: 1} | {1 + k: 3 + k for k in range(5)},
    )(waves, *state[2:], *state[:2], far_b, far_a, chosen, marks)
    field_e, field_h, packed = out[:3]
    received = lax.all_to_all(
        packed.reshape(owners, 3, LANES), "gy", split_axis=0, concat_axis=0, tiled=True
    )
    (result,) = call(collect, ((DB_DEV, LANES),), 2, 1)(
        received.reshape(3 * owners, LANES), filter_matrix
    )
    return (field_e, field_h, result[None])


def solution(mesh):
    placed = (
        P(None, None, "gx", "gy"),
        P(None, None, "gx", "gy"),
        P("gx", "gy"),
        P(None, "gx", "gy"),
        P(None, "gx"),
        P("gx", "gy", None, None),
        P("gx", "gy", None),
        P(),
    )
    return jax.shard_map(
        per_device,
        mesh=mesh,
        in_specs=placed,
        out_specs=(P(None, None, "gx", "gy"), P(None, None, "gx", "gy"), P("gx", "gy", None)),
        check_vma=False,
    )
```

```python
import functools

import jax
import jax.numpy as jnp
import numpy as np
from jax import lax
from jax.experimental import pallas as pl
from jax.experimental.pallas import tpu as pltpu
from jax.sharding import PartitionSpec as P

NZ = 32
STEPS = 12
BROWS = 2
DB_DEV = 4

time_step = 0.5
omega_source = 1.3

ROWS = 32
TILES = 16
HALO = STEPS
XR = ROWS + 2 * HALO
HT = HALO // 4
YV = 24
PAD = 8
NARR = 14
NEAR = 8
FAR = 4
FARW = TILES + HT + 1
LANES = 128
HIGH = lax.Precision.HIGHEST


def shifted(array, axis, by):
    count = lax.axis_size(axis)
    return lax.ppermute(array, axis, [(i, (i + by) % count) for i in range(count)])


def dot(a, b):
    return jnp.dot(a, b, precision=HIGH, preferred_element_type=jnp.float32)


def iota(shape, axis):
    return lax.broadcasted_iota(jnp.int32, shape, axis)


def planes(e, h, eps, aux=None):
    out = [e.at[r, c] for r in range(2) for c in range(3)]
    out += [h.at[r, c] for r in range(2) for c in range(3)] + [eps]
    return out + ([] if aux is None else [aux])


def source_tags(profile, plane):
    half = LANES // 2
    c, l = iota((half, LANES), 0), iota((half, LANES), 1)
    strength = dot(profile[0], (l == c).astype(jnp.float32))
    strength = strength + dot(profile[1], (l == c + half).astype(jnp.float32))
    pick = (iota((2, LANES), 0) == iota((2, LANES), 1)).astype(jnp.float32)
    where = lax.dot_general(
        plane[...].astype(jnp.float32), pick, (((0,), (0,)), ((), ())), precision=HIGH, preferred_element_type=jnp.float32
    )
    return strength, where


def source_rows(strength, where):
    length = TILES * LANES
    half = LANES // 2
    c, l = iota((LANES, length), 0), iota((LANES, length), 1)
    spread = ((l // NZ == c % half) & (l % NZ == c // half)).astype(jnp.float32)
    level = iota((strength.shape[0], length), 1) % NZ
    out = dot(strength, spread)
    out = jnp.where(level == 2, where[:, 0:1], out)
    return jnp.where(level == 3, where[:, 1:2], out)


def fetch_tags(profile, plane, pv, lv, sems):
    copies = [
        pltpu.make_async_copy(profile, pv, sems.at[0]),
        pltpu.make_async_copy(plane, lv, sems.at[1]),
    ]
    for copy in copies:
        copy.start()
    return copies


def pack_side(e, h, eps, profile, plane, to_left, to_right, aux, pv, lv, sems):
    edge = HT * LANES
    length = TILES * LANES
    tags = fetch_tags(profile, plane, pv, lv, sems)
    copies = []
    for part, begin in ((to_left, 0), (to_right, length - edge)):
        for a, src in enumerate(planes(e, h, eps)):
            copies.append(
                pltpu.make_async_copy(
                    src.at[:, pl.ds(begin, edge)], part.at[a], sems.at[2 + len(copies)]
                )
            )
            copies[-1].start()
    for copy in tags:
        copy.wait()
    made = source_rows(*source_tags(pv, lv))
    aux[...] = made
    to_left[NARR - 1] = made[:, 0:edge]
    to_right[NARR - 1] = made[:, length - edge : length]
    for copy in copies:
        copy.wait()


def pack_near(e, h, eps, profile, plane, edge_p, edge_n, mid_p, mid_n, pv, lv, sems):
    edge = HT * LANES
    length = TILES * LANES
    inner = length - 2 * edge
    tags = fetch_tags(profile, plane, pv, lv, sems)
    copies = []
    for x, side, middle in ((0, edge_p, mid_p), (ROWS - NEAR, edge_n, mid_n)):
        for a, src in enumerate(planes(e, h, eps)):
            for part, begin, size, to in (
                (side, 0, edge, 2 * a * edge),
                (side, length - edge, edge, (2 * a + 1) * edge),
                (middle, edge, inner, a * inner),
            ):
                copies.append(
                    pltpu.make_async_copy(
                        src.at[pl.ds(x, NEAR), pl.ds(begin, size)],
                        part.at[:, pl.ds(to, size)],
                        sems.at[2 + len(copies)],
                    )
                )
                copies[-1].start()
    for copy in tags:
        copy.wait()
    for k, tag in enumerate(source_tags(pv, lv)):
        cols = pl.ds((NARR - 1) * 2 * edge + k * LANES, LANES)
        edge_p[:, cols] = tag[0:NEAR, :]
        edge_n[:, cols] = tag[ROWS - NEAR : ROWS, :]
    for copy in copies:
        copy.wait()


def near_source(ref):
    base = (NARR - 1) * 2 * HT * LANES
    return source_rows(ref[:, base : base + LANES], ref[:, base + LANES : base + 2 * LANES])


def pack_far(e, h, eps, aux, left, right, to_prev, to_next):
    edge = HT * LANES
    length = TILES * LANES
    lo, hi = NEAR, ROWS - NEAR - FAR
    for a, src in enumerate(planes(e, h, eps, aux)):
        p, q = a // 2, pl.ds(FAR * (a % 2), FAR)
        to_prev[p, q, 0:edge] = left[a, lo : lo + FAR, :]
        to_prev[p, q, edge : edge + length] = src[lo : lo + FAR, :]
        to_prev[p, q, edge + length :] = right[a, lo : lo + FAR, 0:LANES]
        to_next[p, q, 0:LANES] = left[a, hi : hi + FAR, edge - LANES : edge]
        to_next[p, q, LANES : LANES + length] = src[hi : hi + FAR, :]
        to_next[p, q, LANES + length :] = right[a, hi : hi + FAR, :]


def pack_corner(behind, ahead, to_left, to_right):
    edge = HT * LANES
    length = TILES * LANES
    for k, src in enumerate((behind, ahead)):
        made = near_source(src)
        rows = pl.ds(NEAR * k, NEAR)
        to_left[NARR - 1, rows, :] = made[:, 0:edge]
        to_right[NARR - 1, rows, :] = made[:, length - edge : length]
        for a in range(NARR - 1):
            to_left[a, rows, :] = src[:, 2 * a * edge : (2 * a + 1) * edge]
            to_right[a, rows, :] = src[:, (2 * a + 1) * edge : (2 * a + 2) * edge]


def at(a, x, v=0):
    return PAD + (a * XR + x) * YV + v


def place(dst, a, x, v, value):
    dst[pl.ds(at(a, x, v), value.shape[0], stride=YV), :] = value


def row(ref, a, x):
    return ref[pl.ds(pl.multiple_of(at(a, x), 8), YV), :]


def off(ref, a, x, by):
    return ref[pl.ds(at(a, x) + by, YV), :]


def put(ref, a, x, value):
    ref[pl.ds(pl.multiple_of(at(a, x), 8), YV), :] = value


def fill_sources(wa, ws, spans):
    held = jnp.concatenate([wa[pl.ds(at(0, x), n * YV), :] for x, n in spans], axis=0)
    level = iota(held.shape, 1) % NZ
    held = jnp.where(level < 4, held, 0.0)
    i, j = iota((LANES, 4 * LANES), 0), iota((LANES, 4 * LANES), 1)
    spread = dot(held, (i == (j % LANES) // NZ * NZ + j // LANES).astype(jnp.float32))
    for r in range(2):
        strength = spread[:, r * LANES : (r + 1) * LANES]
        where = spread[:, (2 + r) * LANES : (3 + r) * LANES]
        term = jnp.where(level.astype(jnp.float32) == where, strength, 0.0)
        begin = 0
        for x, n in spans:
            ws[pl.ds(at(r, x), n * YV), :] = term[begin : begin + n * YV]
            begin += n * YV


def kinds(we, wh, wc, wa):
    def same(t):
        return t

    out = [(we, a, same) for a in range(6)]
    out += [(wh, a, lambda t: t * 2.0) for a in range(6)]
    return out + [(wc, 0, lambda t: 0.25 / t), (wa, 0, same)]


class Stepper:
    def __init__(self, waves, we, wh, wc, ws, acc):
        self.waves, self.we, self.wh, self.wc, self.ws, self.acc = waves, we, wh, wc, ws, acc
        lane = iota((YV, LANES), 1)
        self.up_keep = lane % NZ != NZ - 1
        self.down_keep = lane % NZ != 0
        self.first = lane < NZ
        self.last = lane >= LANES - NZ

    def up_z(self, t):
        return jnp.where(self.up_keep, pltpu.roll(t, LANES - 1, 1), 0.0)

    def down_z(self, t):
        return jnp.where(self.down_keep, pltpu.roll(t, 1, 1), 0.0)

    def up_y(self, t, after):
        return pltpu.roll(jnp.where(self.first, after, t), LANES - NZ, 1)

    def down_y(self, t, before):
        return pltpu.roll(jnp.where(self.last, before, t), NZ, 1)

    def magnetic_row(self, r, x):
        we, wh = self.we, self.wh
        ex, ey, ez = (row(we, 3 * r + c, x) for c in range(3))
        hx, hy, hz = (row(wh, 3 * r + c, x) for c in range(3))
        ey_x, ez_x = (row(we, 3 * r + c, x + 1) for c in (1, 2))
        ex_y = self.up_y(ex, off(we, 3 * r, x, 1))
        ez_y = self.up_y(ez, off(we, 3 * r + 2, x, 1))
        hx = hx - ((ez_y - ez) - (self.up_z(ey) - ey))
        hy = hy - ((self.up_z(ex) - ex) - (ez_x - ez))
        hz = hz - ((ey_x - ey) - (ex_y - ex))
        return (hx, hy, hz)

    def electric_row(self, r, x, c, wave):
        we, wh = self.we, self.wh
        hx, hy, hz = (row(wh, 3 * r + k, x) for k in range(3))
        hy_x, hz_x = (row(wh, 3 * r + k, x - 1) for k in (1, 2))
        hx_y = self.down_y(hx, off(wh, 3 * r, x, -1))
        hz_y = self.down_y(hz, off(wh, 3 * r + 2, x, -1))
        ex, ey, ez = (row(we, 3 * r + k, x) for k in range(3))
        ex = ex + c * ((hz - hz_y) - (hy - self.down_z(hy))) + wave * row(self.ws, r, x)
        ey = ey + c * ((hx - self.down_z(hx)) - (hz - hz_x))
        ez = ez + c * ((hy - hy_x) - (hx - hx_y))
        return (ex, ey, ez)

    def magnetic(self, x):
        for r in range(2):
            for k, value in enumerate(self.magnetic_row(r, x)):
                put(self.wh, 3 * r + k, x, value)

    def electric(self, x, wave):
        c = row(self.wc, 0, x)
        f = self.electric_row(0, x, c, wave)
        g = self.electric_row(1, x, c, wave)
        put(self.acc, 0, x, row(self.acc, 0, x) + (f[0] * g[0] + f[1] * g[1] + f[2] * g[2]))
        for k in range(3):
            put(self.we, k, x, f[k])
            put(self.we, 3 + k, x, g[k])

    def edges(self, low, high, count):
        def step(n, _):
            wave = self.waves[n]
            for i in range(count):
                self.magnetic(low + n + i)
                self.magnetic(high - n + i)
            for i in range(count):
                self.electric(low + 1 + n + i, wave)
                self.electric(high - n + i, wave)
            return 0

        lax.fori_loop(0, STEPS, step, 0)

    def inside(self, low, high, begin, end):
        def sweep(one, x, count):
            def group(g, _):
                for i in range(8):
                    one(x + g * 8 + i)
                return 0

            lax.fori_loop(0, count // 8, group, 0)
            for size in (4, 2, 1):
                start = x + count // (2 * size) * (2 * size)

                @pl.when(count % (2 * size) >= size)
                def _(size=size, start=start):
                    for i in range(size):
                        one(start + i)

        def step(n, _):
            wave = self.waves[n]
            sweep(self.magnetic, low + n, high - low - 2 * n)
            sweep(lambda x: self.electric(x, wave), low + 1 + n, high - low - 1 - 2 * n)
            return 0

        lax.fori_loop(begin, end, step, 0)


def run_inside(waves, e, h, eps, aux, left, right, we, wh, wc, ws, acc, wa):
    own = planes(e, h, eps, aux)
    for n, (dst, a, fix) in enumerate(kinds(we, wh, wc, wa)):
        for i in range(ROWS // 8):
            rows = pl.ds(8 * i, 8)
            for j in range(TILES):
                place(dst, a, HALO + 8 * i, HT + j, fix(own[n][rows, pl.ds(j * LANES, LANES)]))
            for j in range(HT):
                cols = pl.ds(j * LANES, LANES)
                place(dst, a, HALO + 8 * i, j, fix(left[n, rows, cols]))
                place(dst, a, HALO + 8 * i, HT + TILES + j, fix(right[n, rows, cols]))
    fill_sources(wa, ws, ((HALO, ROWS),))
    acc[...] = jnp.zeros_like(acc)
    Stepper(waves, we, wh, wc, ws, acc).inside(HALO, HALO + ROWS - 1, 0, STEPS // 2)


def run_inside_rest(waves, _e, _h, _c, _s, _t, we, wh, wc, ws, acc):
    Stepper(waves, we, wh, wc, ws, acc).inside(HALO, HALO + ROWS - 1, STEPS // 2, STEPS)


def store_rows(we, wh, stage, e_out, h_out, sems, x, count):
    copies = []
    for a in range(6):
        for k, (src, out, scale) in enumerate(((we, e_out, None), (wh, h_out, 0.5))):
            for i in range(count // 8):
                for j in range(TILES):
                    value = src[pl.ds(at(a, HALO + x + 8 * i, HT + j), 8, stride=YV), :]
                    value = value if scale is None else value * scale
                    stage[6 * k + a, pl.ds(8 * i, 8), pl.ds(j * LANES, LANES)] = value
            copy = pltpu.make_async_copy(
                stage.at[6 * k + a], out.at[a // 3, a % 3, pl.ds(x, count), :], sems.at[6 * k + a]
            )
            copy.start()
            copies.append(copy)
    return copies


def run_near(waves, _e, _h, _c, _s, _t, edge_b, edge_a, mid_b, mid_a, corner_l, corner_r, e_out, h_out, we, wh, wc, ws, acc, wa, made, stage, sems):
    edge = HT * LANES
    inner = (TILES - 2 * HT) * LANES

    def near_tile(side, middle, n, j):
        if n == NARR - 1:
            return made[:, pl.ds(j * LANES, LANES)]
        if HT <= j < TILES - HT:
            return middle[:, pl.ds(n * inner + (j - HT) * LANES, LANES)]
        j = j if j < HT else j - (TILES - 2 * HT)
        return side[:, pl.ds(2 * n * edge + j * LANES, LANES)]

    for k, (side, middle, x) in enumerate(
        ((edge_b, mid_b, FAR), (edge_a, mid_a, HALO + ROWS))
    ):
        made[...] = near_source(side)
        rows = pl.ds(NEAR * k, NEAR)
        for n, (dst, a, fix) in enumerate(kinds(we, wh, wc, wa)):
            for j in range(TILES):
                place(dst, a, x, HT + j, fix(near_tile(side, middle, n, j)))
            for j in range(HT):
                cols = pl.ds(j * LANES, LANES)
                place(dst, a, x, j, fix(corner_l[n, rows, cols]))
                place(dst, a, x, HT + TILES + j, fix(corner_r[n, rows, cols]))
    fill_sources(wa, ws, ((FAR, NEAR), (HALO + ROWS, NEAR)))
    Stepper(waves, we, wh, wc, ws, acc).edges(FAR, HALO + ROWS - 1, NEAR)
    for copy in store_rows(we, wh, stage, e_out, h_out, sems, 8, 16):
        copy.wait()


def run_far(
    waves, _e, _h, _c, _s, _t, _x, _y, far_b, far_a, select, marks, e_out, h_out, packed, we, wh, wc, ws, acc, wa, stage_lo, stage_hi, sems
):
    for n, (dst, a, fix) in enumerate(kinds(we, wh, wc, wa)):
        q = pl.ds(FAR * (n % 2), FAR)
        for j in range(FARW):
            cols = pl.ds(j * LANES, LANES)
            place(dst, a, 0, HT - 1 + j, fix(far_b[n // 2, q, cols]))
            place(dst, a, XR - FAR, j, fix(far_a[n // 2, q, cols]))
    fill_sources(wa, ws, ((0, FAR), (XR - FAR, FAR)))
    Stepper(waves, we, wh, wc, ws, acc).edges(0, XR - FAR - 1, FAR)

    stores = store_rows(we, wh, stage_lo, e_out, h_out, sems, 0, 8)
    stores += store_rows(we, wh, stage_hi, e_out, h_out, sems.at[pl.ds(12, 12)], 24, 8)

    i, j = iota((LANES, LANES), 0), iota((LANES, LANES), 1)
    sums = dot(acc[pl.ds(at(0, HALO), ROWS * YV), :], (i // NZ == j % 4).astype(jnp.float32))
    per = BROWS * YV
    p, q = iota((per, LANES), 0), iota((per, LANES), 1)
    half = LANES // BROWS
    keep = (p // YV == q // half) & ((q % half) // 4 == p % YV - HT)
    blocks = jnp.sum(
        jnp.where(keep[None], sums.reshape(ROWS // BROWS, per, LANES), 0.0), axis=1
    ) / (STEPS * NZ)
    packed[...] = dot(select[...], blocks) + marks[...]
    for copy in stores:
        copy.wait()


def collect(received, filter_matrix, out):
    rec = received[...]
    places = rec.shape[0]
    p = lax.broadcasted_iota(jnp.int32, (places, places), 0)
    q = lax.broadcasted_iota(jnp.int32, (places, places), 1)
    pick = (q == (p // 3) * 3 + 2).astype(jnp.float32)
    labels = jnp.dot(pick, rec, precision=HIGH, preferred_element_type=jnp.float32)
    pr = lax.broadcasted_iota(jnp.int32, (places, LANES), 0)
    ln = lax.broadcasted_iota(jnp.int32, (places, LANES), 1)
    label = jnp.sum(jnp.where((ln == pr % 3) & (pr % 3 < 2), labels, 0.0), axis=1, keepdims=True)
    want = lax.broadcasted_iota(jnp.int32, (places, 8), 1) + 1
    choose = (label == want.astype(jnp.float32)).astype(jnp.float32)
    design = lax.dot_general(
        choose, rec, (((0,), (0,)), ((), ())), precision=HIGH, preferred_element_type=jnp.float32
    )
    result = jnp.dot(
        design, filter_matrix[...], precision=HIGH, preferred_element_type=jnp.float32
    )
    out[...] = result[0:DB_DEV]


def call(kernel, out_shape, count, micros, limit=32, **kwargs):
    vmem = pl.BlockSpec(memory_space=pltpu.VMEM)
    outs = tuple(jax.ShapeDtypeStruct(shape, jnp.float32) for shape in out_shape)
    return pl.pallas_call(
        kernel,
        in_specs=kwargs.pop("in_specs", [vmem] * count),
        out_specs=kwargs.pop("out_specs", (vmem,) * len(outs)),
        out_shape=outs,
        compiler_params=pltpu.CompilerParams(vmem_limit_bytes=limit * 1024 * 1024),
        name=kernel.__name__,
        cost_estimate=pl.CostEstimate(
            flops=0, transcendentals=0, bytes_accessed=micros * 3_000_000
        ),
        **kwargs,
    )


def per_device(
    electric,
    magnetic,
    permittivity,
    source_profile,
    source_plane,
    block_owner,
    design_slot,
    filter_matrix,
):
    length = TILES * LANES
    edge = HT * LANES
    raw = (electric, magnetic, permittivity, source_profile, source_plane)
    vmem = pl.BlockSpec(memory_space=pltpu.VMEM)
    smem = pl.BlockSpec(memory_space=pltpu.SMEM)
    hbm = pl.BlockSpec(memory_space=pltpu.HBM)
    raw = tuple(pltpu.with_memory_space_constraint(t, pltpu.HBM) for t in raw)

    def packing(copies):
        return dict(
            in_specs=[hbm] * 5,
            scratch_shapes=[
                pltpu.VMEM(source_profile.shape, jnp.float32),
                pltpu.VMEM(source_plane.shape, jnp.int32),
                pltpu.SemaphoreType.DMA((2 + copies,)),
            ],
        )

    x_edge = (NEAR, (NARR - 1) * 2 * edge + 2 * LANES)
    x_mid = (NEAR, (NARR - 1) * (length - 2 * edge))
    edge_prev, edge_next, mid_prev, mid_next = call(
        pack_near, (x_edge, x_edge, x_mid, x_mid), 5, 2, **packing(6 * (NARR - 1))
    )(*raw)
    edge_prev, edge_next, raw = lax.optimization_barrier((edge_prev, edge_next, raw))
    edge_b = shifted(edge_next, "gx", 1)
    edge_a = shifted(edge_prev, "gx", -1)

    y_own = (NARR, ROWS, edge)
    to_left, to_right, aux = call(
        pack_side, (y_own, y_own, (ROWS, length)), 5, 3, **packing(2 * (NARR - 1))
    )(*raw)
    edge_b, edge_a, to_left, to_right = lax.optimization_barrier(
        (edge_b, edge_a, to_left, to_right)
    )
    left = shifted(to_right, "gy", 1)
    right = shifted(to_left, "gy", -1)

    y_corner = (NARR, 2 * NEAR, edge)
    made = pltpu.VMEM((NEAR, length), jnp.float32)
    corner_left, corner_right = call(pack_corner, (y_corner, y_corner), 2, 2)(edge_b, edge_a)
    corner_l = shifted(corner_right, "gy", 1)
    corner_r = shifted(corner_left, "gy", -1)
    corner_l, corner_r, left, right, mid_prev, mid_next = lax.optimization_barrier(
        (corner_l, corner_r, left, right, mid_prev, mid_next)
    )
    mid_b = shifted(mid_next, "gx", 1)
    mid_a = shifted(mid_prev, "gx", -1)

    own = (electric, magnetic, permittivity, aux)
    x_far = (NARR // 2, 2 * FAR, FARW * LANES)
    far_prev, far_next = call(pack_far, (x_far, x_far), 6, 2)(*own, left, right)
    far_prev, far_next, left, right = lax.optimization_barrier((far_prev, far_next, left, right))
    waves = jnp.asarray(
        time_step
        * np.sin(np.arange(1, STEPS + 1).astype(np.float32) * np.float32(omega_source * time_step)),
        jnp.float32,
    )
    field = (2, 3, ROWS, length)
    many = XR * YV
    tail = PAD + YV
    held = tuple((k * many + tail, LANES) for k in (6, 6, 1, 2, 1))
    tags = pltpu.VMEM((many + tail, LANES), jnp.float32)
    state = call(run_inside, held, 7, 30, in_specs=[smem] + [vmem] * 6, scratch_shapes=[tags])(
        waves, *own, left, right
    )
    far_prev, far_next, state = lax.optimization_barrier((far_prev, far_next, state))
    far_b = shifted(far_next, "gx", 1)
    far_a = shifted(far_prev, "gx", -1)
    keep = {1 + k: k for k in range(5)}
    state = call(
        run_inside_rest,
        held,
        6,
        1,
        in_specs=[smem] + [vmem] * 5,
        input_output_aliases=keep,
    )(waves, *state)

    count = ROWS // BROWS
    owner = block_owner[0, 0, :, 0]
    slot = design_slot[0, 0, :]
    owners = lax.axis_size("gy")
    index = jnp.arange(count, dtype=jnp.int32)
    earlier = (
        ((owner[:, None] == owner[None, :]) & (index[None, :] < index[:, None]))
        .astype(jnp.int32)
        .sum(1)
    )
    places = jnp.arange(3 * owners, dtype=jnp.int32)
    chosen = (places[:, None] == (owner * 3 + earlier)[None, :]).astype(jnp.float32)
    lane = jnp.arange(LANES, dtype=jnp.int32)
    holder = (places[:, None] == (owner * 3 + 2)[None, :]).astype(jnp.float32)
    named = (lane[None, :] == earlier[:, None]).astype(jnp.float32) * (slot + 1).astype(
        jnp.float32
    )[:, None]
    marks = jnp.dot(holder, named, precision=HIGH)

    copy_sem = pltpu.SemaphoreType.DMA
    state = call(
        run_near,
        (field, field) + held,
        12,
        12,
        in_specs=[smem] + [vmem] * 11,
        out_specs=(hbm,) * 2 + (vmem,) * 5,
        scratch_shapes=[tags, made, pltpu.VMEM((12, 16, length), jnp.float32), copy_sem((12,))],
        input_output_aliases={1 + k: 2 + k for k in range(5)},
    )(waves, *state, edge_b, edge_a, mid_b, mid_a, corner_l, corner_r)
    stage = pltpu.VMEM((12, 8, length), jnp.float32)
    out = call(
        run_far,
        (field, field, (3 * owners, LANES)) + held,
        12,
        8,
        in_specs=[smem] + [vmem] * 5 + [hbm] * 2 + [vmem] * 4,
        out_specs=(hbm,) * 2 + (vmem,) * 6,
        scratch_shapes=[tags, stage, stage, copy_sem((24,))],
        input_output_aliases={6: 0, 7: 1} | {1 + k: 3 + k for k in range(5)},
    )(waves, *state[2:], *state[:2], far_b, far_a, chosen, marks)
    field_e, field_h, packed = out[:3]
    received = lax.all_to_all(
        packed.reshape(owners, 3, LANES), "gy", split_axis=0, concat_axis=0, tiled=True
    )
    (result,) = call(collect, ((DB_DEV, LANES),), 2, 1)(
        received.reshape(3 * owners, LANES), filter_matrix
    )
    return (field_e, field_h, result[None])


def solution(mesh):
    placed = (
        P(None, None, "gx", "gy"),
        P(None, None, "gx", "gy"),
        P("gx", "gy"),
        P(None, "gx", "gy"),
        P(None, "gx"),
        P("gx", "gy", None, None),
        P("gx", "gy", None),
        P(),
    )
    return jax.shard_map(
        per_device,
        mesh=mesh,
        in_specs=placed,
        out_specs=(P(None, None, "gx", "gy"), P(None, None, "gx", "gy"), P("gx", "gy", None)),
        check_vma=False,
    )
```

```python
import functools

import jax
import jax.numpy as jnp
import numpy as np
from jax import lax
from jax.experimental import pallas as pl
from jax.experimental.pallas import tpu as pltpu
from jax.sharding import PartitionSpec as P

NZ = 32
STEPS = 12
BROWS = 2
DB_DEV = 4

time_step = 0.5
omega_source = 1.3

ROWS = 32
TILES = 16
HALO = STEPS
XR = ROWS + 2 * HALO
HT = HALO // 4
YV = 24
PAD = 8
NARR = 14
NEAR = 8
FAR = 4
FARW = TILES + HT + 1
LANES = 128
HIGH = lax.Precision.HIGHEST
CUT = 8


def shifted(array, axis, by):
    count = lax.axis_size(axis)
    return lax.ppermute(array, axis, [(i, (i + by) % count) for i in range(count)])


def dot(a, b):
    return jnp.dot(a, b, precision=HIGH, preferred_element_type=jnp.float32)


def iota(shape, axis):
    return lax.broadcasted_iota(jnp.int32, shape, axis)


def planes(e, h, eps, aux=None):
    out = [e.at[r, c] for r in range(2) for c in range(3)]
    out += [h.at[r, c] for r in range(2) for c in range(3)] + [eps]
    return out + ([] if aux is None else [aux])


def source_tags(profile, plane):
    half = LANES // 2
    c, l = iota((half, LANES), 0), iota((half, LANES), 1)
    strength = dot(profile[0], (l == c).astype(jnp.float32))
    strength = strength + dot(profile[1], (l == c + half).astype(jnp.float32))
    pick = (iota((2, LANES), 0) == iota((2, LANES), 1)).astype(jnp.float32)
    where = lax.dot_general(
        plane[...].astype(jnp.float32), pick, (((0,), (0,)), ((), ())), precision=HIGH, preferred_element_type=jnp.float32
    )
    return strength, where


def source_rows(strength, where):
    length = TILES * LANES
    half = LANES // 2
    c, l = iota((LANES, length), 0), iota((LANES, length), 1)
    spread = ((l // NZ == c % half) & (l % NZ == c // half)).astype(jnp.float32)
    level = iota((strength.shape[0], length), 1) % NZ
    out = dot(strength, spread)
    out = jnp.where(level == 2, where[:, 0:1], out)
    return jnp.where(level == 3, where[:, 1:2], out)


def fetch_tags(profile, plane, pv, lv, sems):
    copies = [
        pltpu.make_async_copy(profile, pv, sems.at[0]),
        pltpu.make_async_copy(plane, lv, sems.at[1]),
    ]
    for copy in copies:
        copy.start()
    return copies


def pack_side(e, h, eps, profile, plane, to_left, to_right, aux, pv, lv, sems):
    edge = HT * LANES
    length = TILES * LANES
    tags = fetch_tags(profile, plane, pv, lv, sems)
    copies = []
    for part, begin in ((to_left, 0), (to_right, length - edge)):
        for a, src in enumerate(planes(e, h, eps)):
            copies.append(
                pltpu.make_async_copy(
                    src.at[:, pl.ds(begin, edge)], part.at[a], sems.at[2 + len(copies)]
                )
            )
            copies[-1].start()
    for copy in tags:
        copy.wait()
    made = source_rows(*source_tags(pv, lv))
    aux[...] = made
    to_left[NARR - 1] = made[:, 0:edge]
    to_right[NARR - 1] = made[:, length - edge : length]
    for copy in copies:
        copy.wait()


def pack_near(e, h, eps, profile, plane, edge_p, edge_n, mid_p, mid_n, pv, lv, sems):
    edge = HT * LANES
    length = TILES * LANES
    inner = length - 2 * edge
    tags = fetch_tags(profile, plane, pv, lv, sems)
    copies = []
    for x, side, middle in ((0, edge_p, mid_p), (ROWS - NEAR, edge_n, mid_n)):
        for a, src in enumerate(planes(e, h, eps)):
            for part, begin, size, to in (
                (side, 0, edge, 2 * a * edge),
                (side, length - edge, edge, (2 * a + 1) * edge),
                (middle, edge, inner, a * inner),
            ):
                copies.append(
                    pltpu.make_async_copy(
                        src.at[pl.ds(x, NEAR), pl.ds(begin, size)],
                        part.at[:, pl.ds(to, size)],
                        sems.at[2 + len(copies)],
                    )
                )
                copies[-1].start()
    for copy in tags:
        copy.wait()
    for k, tag in enumerate(source_tags(pv, lv)):
        cols = pl.ds((NARR - 1) * 2 * edge + k * LANES, LANES)
        edge_p[:, cols] = tag[0:NEAR, :]
        edge_n[:, cols] = tag[ROWS - NEAR : ROWS, :]
    for copy in copies:
        copy.wait()


def near_source(ref):
    base = (NARR - 1) * 2 * HT * LANES
    return source_rows(ref[:, base : base + LANES], ref[:, base + LANES : base + 2 * LANES])


def pack_far(e, h, eps, aux, left, right, to_prev, to_next):
    edge = HT * LANES
    length = TILES * LANES
    lo, hi = NEAR, ROWS - NEAR - FAR
    for a, src in enumerate(planes(e, h, eps, aux)):
        p, q = a // 2, pl.ds(FAR * (a % 2), FAR)
        to_prev[p, q, 0:edge] = left[a, lo : lo + FAR, :]
        to_prev[p, q, edge : edge + length] = src[lo : lo + FAR, :]
        to_prev[p, q, edge + length :] = right[a, lo : lo + FAR, 0:LANES]
        to_next[p, q, 0:LANES] = left[a, hi : hi + FAR, edge - LANES : edge]
        to_next[p, q, LANES : LANES + length] = src[hi : hi + FAR, :]
        to_next[p, q, LANES + length :] = right[a, hi : hi + FAR, :]


def pack_corner(behind, ahead, to_left, to_right, aux):
    edge = HT * LANES
    length = TILES * LANES
    for k, src in enumerate((behind, ahead)):
        made = near_source(src)
        rows = pl.ds(NEAR * k, NEAR)
        aux[rows, :] = made
        to_left[NARR - 1, rows, :] = made[:, 0:edge]
        to_right[NARR - 1, rows, :] = made[:, length - edge : length]
        for a in range(NARR - 1):
            to_left[a, rows, :] = src[:, 2 * a * edge : (2 * a + 1) * edge]
            to_right[a, rows, :] = src[:, (2 * a + 1) * edge : (2 * a + 2) * edge]


def at(a, x, v=0):
    return PAD + (a * XR + x) * YV + v


def place(dst, a, x, v, value):
    dst[pl.ds(at(a, x, v), value.shape[0], stride=YV), :] = value


def row(ref, a, x):
    return ref[pl.ds(pl.multiple_of(at(a, x), 8), YV), :]


def off(ref, a, x, by):
    return ref[pl.ds(at(a, x) + by, YV), :]


def put(ref, a, x, value):
    ref[pl.ds(pl.multiple_of(at(a, x), 8), YV), :] = value


def fill_sources(wa, ws, spans):
    held = jnp.concatenate([wa[pl.ds(at(0, x), n * YV), :] for x, n in spans], axis=0)
    level = iota(held.shape, 1) % NZ
    held = jnp.where(level < 4, held, 0.0)
    i, j = iota((LANES, 4 * LANES), 0), iota((LANES, 4 * LANES), 1)
    spread = dot(held, (i == (j % LANES) // NZ * NZ + j // LANES).astype(jnp.float32))
    for r in range(2):
        strength = spread[:, r * LANES : (r + 1) * LANES]
        where = spread[:, (2 + r) * LANES : (3 + r) * LANES]
        term = jnp.where(level.astype(jnp.float32) == where, strength, 0.0)
        begin = 0
        for x, n in spans:
            ws[pl.ds(at(r, x), n * YV), :] = term[begin : begin + n * YV]
            begin += n * YV


def kinds(we, wh, wc, wa):
    def same(t):
        return t

    out = [(we, a, same) for a in range(6)]
    out += [(wh, a, lambda t: t * 2.0) for a in range(6)]
    return out + [(wc, 0, lambda t: 0.25 / t), (wa, 0, same)]


class Stepper:
    def __init__(self, waves, we, wh, wc, ws, acc):
        self.waves, self.we, self.wh, self.wc, self.ws, self.acc = waves, we, wh, wc, ws, acc
        lane = iota((YV, LANES), 1)
        self.up_keep = lane % NZ != NZ - 1
        self.down_keep = lane % NZ != 0
        self.first = lane < NZ
        self.last = lane >= LANES - NZ

    def up_z(self, t):
        return jnp.where(self.up_keep, pltpu.roll(t, LANES - 1, 1), 0.0)

    def down_z(self, t):
        return jnp.where(self.down_keep, pltpu.roll(t, 1, 1), 0.0)

    def up_y(self, t, after):
        return pltpu.roll(jnp.where(self.first, after, t), LANES - NZ, 1)

    def down_y(self, t, before):
        return pltpu.roll(jnp.where(self.last, before, t), NZ, 1)

    def magnetic_row(self, r, x):
        we, wh = self.we, self.wh
        ex, ey, ez = (row(we, 3 * r + c, x) for c in range(3))
        hx, hy, hz = (row(wh, 3 * r + c, x) for c in range(3))
        ey_x, ez_x = (row(we, 3 * r + c, x + 1) for c in (1, 2))
        ex_y = self.up_y(ex, off(we, 3 * r, x, 1))
        ez_y = self.up_y(ez, off(we, 3 * r + 2, x, 1))
        hx = hx - ((ez_y - ez) - (self.up_z(ey) - ey))
        hy = hy - ((self.up_z(ex) - ex) - (ez_x - ez))
        hz = hz - ((ey_x - ey) - (ex_y - ex))
        return (hx, hy, hz)

    def electric_row(self, r, x, c, wave):
        we, wh = self.we, self.wh
        hx, hy, hz = (row(wh, 3 * r + k, x) for k in range(3))
        hy_x, hz_x = (row(wh, 3 * r + k, x - 1) for k in (1, 2))
        hx_y = self.down_y(hx, off(wh, 3 * r, x, -1))
        hz_y = self.down_y(hz, off(wh, 3 * r + 2, x, -1))
        ex, ey, ez = (row(we, 3 * r + k, x) for k in range(3))
        ex = ex + c * ((hz - hz_y) - (hy - self.down_z(hy))) + wave * row(self.ws, r, x)
        ey = ey + c * ((hx - self.down_z(hx)) - (hz - hz_x))
        ez = ez + c * ((hy - hy_x) - (hx - hx_y))
        return (ex, ey, ez)

    def magnetic(self, x):
        for r in range(2):
            for k, value in enumerate(self.magnetic_row(r, x)):
                put(self.wh, 3 * r + k, x, value)

    def electric(self, x, wave):
        c = row(self.wc, 0, x)
        f = self.electric_row(0, x, c, wave)
        g = self.electric_row(1, x, c, wave)
        put(self.acc, 0, x, row(self.acc, 0, x) + (f[0] * g[0] + f[1] * g[1] + f[2] * g[2]))
        for k in range(3):
            put(self.we, k, x, f[k])
            put(self.we, 3 + k, x, g[k])

    def edges(self, low, high, count):
        def step(n, _):
            wave = self.waves[n]
            for i in range(count):
                self.magnetic(low + n + i)
                self.magnetic(high - n + i)
            for i in range(count):
                self.electric(low + 1 + n + i, wave)
                self.electric(high - n + i, wave)
            return 0

        lax.fori_loop(0, STEPS, step, 0)

    def inside(self, low, high, begin, end):
        def sweep(one, x, count):
            def group(g, _):
                for i in range(8):
                    one(x + g * 8 + i)
                return 0

            lax.fori_loop(0, count // 8, group, 0)
            for size in (4, 2, 1):
                start = x + count // (2 * size) * (2 * size)

                @pl.when(count % (2 * size) >= size)
                def _(size=size, start=start):
                    for i in range(size):
                        one(start + i)

        def step(n, _):
            wave = self.waves[n]
            sweep(self.magnetic, low + n, high - low - 2 * n)
            sweep(lambda x: self.electric(x, wave), low + 1 + n, high - low - 1 - 2 * n)
            return 0

        lax.fori_loop(begin, end, step, 0)


def run_inside(waves, e, h, eps, aux, left, right, we, wh, wc, ws, acc, wa):
    own = planes(e, h, eps, aux)
    for n, (dst, a, fix) in enumerate(kinds(we, wh, wc, wa)):
        for i in range(ROWS // 8):
            rows = pl.ds(8 * i, 8)
            for j in range(TILES):
                place(dst, a, HALO + 8 * i, HT + j, fix(own[n][rows, pl.ds(j * LANES, LANES)]))
            for j in range(HT):
                cols = pl.ds(j * LANES, LANES)
                place(dst, a, HALO + 8 * i, j, fix(left[n, rows, cols]))
                place(dst, a, HALO + 8 * i, HT + TILES + j, fix(right[n, rows, cols]))
    fill_sources(wa, ws, ((HALO, ROWS),))
    acc[...] = jnp.zeros_like(acc)
    Stepper(waves, we, wh, wc, ws, acc).inside(HALO, HALO + ROWS - 1, 0, CUT)


def run_inside_rest(waves, _e, _h, _c, _s, _t, we, wh, wc, ws, acc):
    Stepper(waves, we, wh, wc, ws, acc).inside(HALO, HALO + ROWS - 1, CUT, STEPS)


def store_rows(we, wh, stage, e_out, h_out, sems, x, count):
    copies = []
    for a in range(6):
        for k, (src, out, scale) in enumerate(((we, e_out, None), (wh, h_out, 0.5))):
            for i in range(count // 8):
                for j in range(TILES):
                    value = src[pl.ds(at(a, HALO + x + 8 * i, HT + j), 8, stride=YV), :]
                    value = value if scale is None else value * scale
                    stage[6 * k + a, pl.ds(8 * i, 8), pl.ds(j * LANES, LANES)] = value
            copy = pltpu.make_async_copy(
                stage.at[6 * k + a], out.at[a // 3, a % 3, pl.ds(x, count), :], sems.at[6 * k + a]
            )
            copy.start()
            copies.append(copy)
    return copies


def run_near(waves, _e, _h, _c, _s, _t, edge_b, edge_a, mid_b, mid_a, corner_l, corner_r, aux_near, e_out, h_out, we, wh, wc, ws, acc, wa, stage, sems):
    edge = HT * LANES
    inner = (TILES - 2 * HT) * LANES

    def near_tile(side, middle, n, j, rows):
        if n == NARR - 1:
            return aux_near[rows, pl.ds(j * LANES, LANES)]
        if HT <= j < TILES - HT:
            return middle[:, pl.ds(n * inner + (j - HT) * LANES, LANES)]
        j = j if j < HT else j - (TILES - 2 * HT)
        return side[:, pl.ds(2 * n * edge + j * LANES, LANES)]

    for k, (side, middle, x) in enumerate(
        ((edge_b, mid_b, FAR), (edge_a, mid_a, HALO + ROWS))
    ):
        rows = pl.ds(NEAR * k, NEAR)
        for n, (dst, a, fix) in enumerate(kinds(we, wh, wc, wa)):
            for j in range(TILES):
                place(dst, a, x, HT + j, fix(near_tile(side, middle, n, j, rows)))
            for j in range(HT):
                cols = pl.ds(j * LANES, LANES)
                place(dst, a, x, j, fix(corner_l[n, rows, cols]))
                place(dst, a, x, HT + TILES + j, fix(corner_r[n, rows, cols]))
    fill_sources(wa, ws, ((FAR, NEAR), (HALO + ROWS, NEAR)))
    Stepper(waves, we, wh, wc, ws, acc).edges(FAR, HALO + ROWS - 1, NEAR)
    for copy in store_rows(we, wh, stage, e_out, h_out, sems, 8, 16):
        copy.wait()


def run_far(
    waves, _e, _h, _c, _s, _t, _x, _y, far_b, far_a, select, marks, e_out, h_out, packed, we, wh, wc, ws, acc, wa, stage_lo, stage_hi, sems
):
    for n, (dst, a, fix) in enumerate(kinds(we, wh, wc, wa)):
        q = pl.ds(FAR * (n % 2), FAR)
        for j in range(FARW):
            cols = pl.ds(j * LANES, LANES)
            place(dst, a, 0, HT - 1 + j, fix(far_b[n // 2, q, cols]))
            place(dst, a, XR - FAR, j, fix(far_a[n // 2, q, cols]))
    fill_sources(wa, ws, ((0, FAR), (XR - FAR, FAR)))
    Stepper(waves, we, wh, wc, ws, acc).edges(0, XR - FAR - 1, FAR)

    stores = store_rows(we, wh, stage_lo, e_out, h_out, sems, 0, 8)
    stores += store_rows(we, wh, stage_hi, e_out, h_out, sems.at[pl.ds(12, 12)], 24, 8)

    i, j = iota((LANES, LANES), 0), iota((LANES, LANES), 1)
    sums = dot(acc[pl.ds(at(0, HALO), ROWS * YV), :], (i // NZ == j % 4).astype(jnp.float32))
    per = BROWS * YV
    p, q = iota((per, LANES), 0), iota((per, LANES), 1)
    half = LANES // BROWS
    keep = (p // YV == q // half) & ((q % half) // 4 == p % YV - HT)
    blocks = jnp.sum(
        jnp.where(keep[None], sums.reshape(ROWS // BROWS, per, LANES), 0.0), axis=1
    ) / (STEPS * NZ)
    packed[...] = dot(select[...], blocks) + marks[...]
    for copy in stores:
        copy.wait()


def collect(received, filter_matrix, out):
    rec = received[...]
    places = rec.shape[0]
    p = lax.broadcasted_iota(jnp.int32, (places, places), 0)
    q = lax.broadcasted_iota(jnp.int32, (places, places), 1)
    pick = (q == (p // 3) * 3 + 2).astype(jnp.float32)
    labels = jnp.dot(pick, rec, precision=HIGH, preferred_element_type=jnp.float32)
    pr = lax.broadcasted_iota(jnp.int32, (places, LANES), 0)
    ln = lax.broadcasted_iota(jnp.int32, (places, LANES), 1)
    label = jnp.sum(jnp.where((ln == pr % 3) & (pr % 3 < 2), labels, 0.0), axis=1, keepdims=True)
    want = lax.broadcasted_iota(jnp.int32, (places, 8), 1) + 1
    choose = (label == want.astype(jnp.float32)).astype(jnp.float32)
    design = lax.dot_general(
        choose, rec, (((0,), (0,)), ((), ())), precision=HIGH, preferred_element_type=jnp.float32
    )
    result = jnp.dot(
        design, filter_matrix[...], precision=HIGH, preferred_element_type=jnp.float32
    )
    out[...] = result[0:DB_DEV]


def call(kernel, out_shape, count, micros, limit=32, **kwargs):
    vmem = pl.BlockSpec(memory_space=pltpu.VMEM)
    outs = tuple(jax.ShapeDtypeStruct(shape, jnp.float32) for shape in out_shape)
    return pl.pallas_call(
        kernel,
        in_specs=kwargs.pop("in_specs", [vmem] * count),
        out_specs=kwargs.pop("out_specs", (vmem,) * len(outs)),
        out_shape=outs,
        compiler_params=pltpu.CompilerParams(vmem_limit_bytes=limit * 1024 * 1024),
        name=kernel.__name__,
        cost_estimate=pl.CostEstimate(
            flops=0, transcendentals=0, bytes_accessed=micros * 3_000_000
        ),
        **kwargs,
    )


def per_device(
    electric,
    magnetic,
    permittivity,
    source_profile,
    source_plane,
    block_owner,
    design_slot,
    filter_matrix,
):
    length = TILES * LANES
    edge = HT * LANES
    raw = (electric, magnetic, permittivity, source_profile, source_plane)
    vmem = pl.BlockSpec(memory_space=pltpu.VMEM)
    smem = pl.BlockSpec(memory_space=pltpu.SMEM)
    hbm = pl.BlockSpec(memory_space=pltpu.HBM)
    raw = tuple(pltpu.with_memory_space_constraint(t, pltpu.HBM) for t in raw)

    def packing(copies):
        return dict(
            in_specs=[hbm] * 5,
            scratch_shapes=[
                pltpu.VMEM(source_profile.shape, jnp.float32),
                pltpu.VMEM(source_plane.shape, jnp.int32),
                pltpu.SemaphoreType.DMA((2 + copies,)),
            ],
        )

    x_edge = (NEAR, (NARR - 1) * 2 * edge + 2 * LANES)
    x_mid = (NEAR, (NARR - 1) * (length - 2 * edge))
    edge_prev, edge_next, mid_prev, mid_next = call(
        pack_near, (x_edge, x_edge, x_mid, x_mid), 5, 2, **packing(6 * (NARR - 1))
    )(*raw)
    edge_prev, edge_next, raw = lax.optimization_barrier((edge_prev, edge_next, raw))
    edge_b = shifted(edge_next, "gx", 1)
    edge_a = shifted(edge_prev, "gx", -1)

    y_own = (NARR, ROWS, edge)
    to_left, to_right, aux = call(
        pack_side, (y_own, y_own, (ROWS, length)), 5, 3, **packing(2 * (NARR - 1))
    )(*raw)
    edge_b, edge_a, to_left, to_right = lax.optimization_barrier(
        (edge_b, edge_a, to_left, to_right)
    )
    left = shifted(to_right, "gy", 1)
    right = shifted(to_left, "gy", -1)

    y_corner = (NARR, 2 * NEAR, edge)
    corner_left, corner_right, aux_near = call(
        pack_corner, (y_corner, y_corner, (2 * NEAR, length)), 2, 2
    )(edge_b, edge_a)
    corner_l = shifted(corner_right, "gy", 1)
    corner_r = shifted(corner_left, "gy", -1)
    corner_l, corner_r, left, right, mid_prev, mid_next = lax.optimization_barrier(
        (corner_l, corner_r, left, right, mid_prev, mid_next)
    )
    mid_b = shifted(mid_next, "gx", 1)
    mid_a = shifted(mid_prev, "gx", -1)

    own = (electric, magnetic, permittivity, aux)
    x_far = (NARR // 2, 2 * FAR, FARW * LANES)
    far_prev, far_next = call(pack_far, (x_far, x_far), 6, 2)(*own, left, right)
    far_prev, far_next, left, right = lax.optimization_barrier((far_prev, far_next, left, right))
    waves = jnp.asarray(
        time_step
        * np.sin(np.arange(1, STEPS + 1).astype(np.float32) * np.float32(omega_source * time_step)),
        jnp.float32,
    )
    field = (2, 3, ROWS, length)
    many = XR * YV
    tail = PAD + YV
    held = tuple((k * many + tail, LANES) for k in (6, 6, 1, 2, 1))
    tags = pltpu.VMEM((many + tail, LANES), jnp.float32)
    state = call(run_inside, held, 7, 30, in_specs=[smem] + [vmem] * 6, scratch_shapes=[tags])(
        waves, *own, left, right
    )
    far_prev, far_next, state = lax.optimization_barrier((far_prev, far_next, state))
    far_b = shifted(far_next, "gx", 1)
    far_a = shifted(far_prev, "gx", -1)
    keep = {1 + k: k for k in range(5)}
    state = call(
        run_inside_rest,
        held,
        6,
        1,
        in_specs=[smem] + [vmem] * 5,
        input_output_aliases=keep,
    )(waves, *state)

    count = ROWS // BROWS
    owner = block_owner[0, 0, :, 0]
    slot = design_slot[0, 0, :]
    owners = lax.axis_size("gy")
    index = jnp.arange(count, dtype=jnp.int32)
    earlier = (
        ((owner[:, None] == owner[None, :]) & (index[None, :] < index[:, None]))
        .astype(jnp.int32)
        .sum(1)
    )
    places = jnp.arange(3 * owners, dtype=jnp.int32)
    chosen = (places[:, None] == (owner * 3 + earlier)[None, :]).astype(jnp.float32)
    lane = jnp.arange(LANES, dtype=jnp.int32)
    holder = (places[:, None] == (owner * 3 + 2)[None, :]).astype(jnp.float32)
    named = (lane[None, :] == earlier[:, None]).astype(jnp.float32) * (slot + 1).astype(
        jnp.float32
    )[:, None]
    marks = jnp.dot(holder, named, precision=HIGH)

    copy_sem = pltpu.SemaphoreType.DMA
    state = call(
        run_near,
        (field, field) + held,
        13,
        12,
        in_specs=[smem] + [vmem] * 12,
        out_specs=(hbm,) * 2 + (vmem,) * 5,
        scratch_shapes=[tags, pltpu.VMEM((12, 16, length), jnp.float32), copy_sem((12,))],
        input_output_aliases={1 + k: 2 + k for k in range(5)},
    )(waves, *state, edge_b, edge_a, mid_b, mid_a, corner_l, corner_r, aux_near)
    stage = pltpu.VMEM((12, 8, length), jnp.float32)
    out = call(
        run_far,
        (field, field, (3 * owners, LANES)) + held,
        12,
        8,
        in_specs=[smem] + [vmem] * 5 + [hbm] * 2 + [vmem] * 4,
        out_specs=(hbm,) * 2 + (vmem,) * 6,
        scratch_shapes=[tags, stage, stage, copy_sem((24,))],
        input_output_aliases={6: 0, 7: 1} | {1 + k: 3 + k for k in range(5)},
    )(waves, *state[2:], *state[:2], far_b, far_a, chosen, marks)
    field_e, field_h, packed = out[:3]
    received = lax.all_to_all(
        packed.reshape(owners, 3, LANES), "gy", split_axis=0, concat_axis=0, tiled=True
    )
    (result,) = call(collect, ((DB_DEV, LANES),), 2, 1)(
        received.reshape(3 * owners, LANES), filter_matrix
    )
    return (field_e, field_h, result[None])


def solution(mesh):
    placed = (
        P(None, None, "gx", "gy"),
        P(None, None, "gx", "gy"),
        P("gx", "gy"),
        P(None, "gx", "gy"),
        P(None, "gx"),
        P("gx", "gy", None, None),
        P("gx", "gy", None),
        P(),
    )
    return jax.shard_map(
        per_device,
        mesh=mesh,
        in_specs=placed,
        out_specs=(P(None, None, "gx", "gy"), P(None, None, "gx", "gy"), P("gx", "gy", None)),
        check_vma=False,
    )
```

```python
import functools

import jax
import jax.numpy as jnp
import numpy as np
from jax import lax
from jax.experimental import pallas as pl
from jax.experimental.pallas import tpu as pltpu
from jax.sharding import PartitionSpec as P

NZ = 32
STEPS = 12
BROWS = 2
DB_DEV = 4

time_step = 0.5
omega_source = 1.3

ROWS = 32
TILES = 16
HALO = STEPS
XR = ROWS + 2 * HALO
HT = HALO // 4
YV = 24
PAD = 8
NARR = 14
NEAR = 8
FAR = 4
FARW = TILES + HT + 1
LANES = 128
HIGH = lax.Precision.HIGHEST
PART = NARR // 2
EXTRA = 6 * LANES
CUT = 8


def shifted(array, axis, by):
    count = lax.axis_size(axis)
    return lax.ppermute(array, axis, [(i, (i + by) % count) for i in range(count)])


def dot(a, b):
    return jnp.dot(a, b, precision=HIGH, preferred_element_type=jnp.float32)


def iota(shape, axis):
    return lax.broadcasted_iota(jnp.int32, shape, axis)


def planes(e, h, eps, aux=None):
    out = [e.at[r, c] for r in range(2) for c in range(3)]
    out += [h.at[r, c] for r in range(2) for c in range(3)] + [eps]
    return out + ([] if aux is None else [aux])


def source_tags(profile, plane):
    half = LANES // 2
    c, l = iota((half, LANES), 0), iota((half, LANES), 1)
    strength = dot(profile[0], (l == c).astype(jnp.float32))
    strength = strength + dot(profile[1], (l == c + half).astype(jnp.float32))
    pick = (iota((2, LANES), 0) == iota((2, LANES), 1)).astype(jnp.float32)
    where = lax.dot_general(
        plane[...].astype(jnp.float32), pick, (((0,), (0,)), ((), ())), precision=HIGH, preferred_element_type=jnp.float32
    )
    return strength, where


def source_rows(strength, where):
    length = TILES * LANES
    half = LANES // 2
    c, l = iota((LANES, length), 0), iota((LANES, length), 1)
    spread = ((l // NZ == c % half) & (l % NZ == c // half)).astype(jnp.float32)
    level = iota((strength.shape[0], length), 1) % NZ
    out = dot(strength, spread)
    out = jnp.where(level == 2, where[:, 0:1], out)
    return jnp.where(level == 3, where[:, 1:2], out)


def fetch_tags(profile, plane, pv, lv, sems):
    copies = [
        pltpu.make_async_copy(profile, pv, sems.at[0]),
        pltpu.make_async_copy(plane, lv, sems.at[1]),
    ]
    for copy in copies:
        copy.start()
    return copies


def pack_side(e, h, eps, profile, plane, left_lo, left_hi, right_lo, right_hi, aux, pv, lv, sems):
    edge = HT * LANES
    length = TILES * LANES
    tags = fetch_tags(profile, plane, pv, lv, sems)
    copies = []
    sides = (((left_lo, left_hi), 0), ((right_lo, right_hi), length - edge))
    for parts, begin in sides:
        for a, src in enumerate(planes(e, h, eps)):
            copies.append(
                pltpu.make_async_copy(
                    src.at[:, pl.ds(begin, edge)],
                    parts[a // PART].at[a % PART],
                    sems.at[2 + len(copies)],
                )
            )
            copies[-1].start()
    for copy in tags:
        copy.wait()
    made = source_rows(*source_tags(pv, lv))
    aux[...] = made
    left_hi[PART - 1] = made[:, 0:edge]
    right_hi[PART - 1] = made[:, length - edge : length]
    for copy in copies:
        copy.wait()


def pack_near(e, h, eps, profile, plane, edge_p, edge_n, mid_p, mid_n, pv, lv, sems):
    edge = HT * LANES
    length = TILES * LANES
    inner = length - 2 * edge
    tags = fetch_tags(profile, plane, pv, lv, sems)
    copies = []
    for x, side, middle in ((0, edge_p, mid_p), (ROWS - NEAR, edge_n, mid_n)):
        for a, src in enumerate(planes(e, h, eps)):
            for part, begin, size, to in (
                (side, 0, edge, 2 * a * edge),
                (side, length - edge, edge, (2 * a + 1) * edge),
                (middle, edge, inner, a * inner),
            ):
                copies.append(
                    pltpu.make_async_copy(
                        src.at[pl.ds(x, NEAR), pl.ds(begin, size)],
                        part.at[:, pl.ds(to, size)],
                        sems.at[2 + len(copies)],
                    )
                )
                copies[-1].start()
    for copy in tags:
        copy.wait()
    for k, tag in enumerate(source_tags(pv, lv)):
        cols = pl.ds((NARR - 1) * 2 * edge + k * LANES, LANES)
        edge_p[:, cols] = tag[0:NEAR, :]
        edge_n[:, cols] = tag[ROWS - NEAR : ROWS, :]
    for copy in copies:
        copy.wait()


def near_source(ref):
    base = (NARR - 1) * 2 * HT * LANES
    return source_rows(ref[:, base : base + LANES], ref[:, base + LANES : base + 2 * LANES])


def pack_far(e, h, eps, aux, left_lo, left_hi, right_lo, right_hi, to_prev, to_next):
    edge = HT * LANES
    length = TILES * LANES
    lo, hi = NEAR, ROWS - NEAR - FAR
    for a, src in enumerate(planes(e, h, eps, aux)):
        left, right = ((left_lo, right_lo), (left_hi, right_hi))[a // PART]
        p, q = a // 2, pl.ds(FAR * (a % 2), FAR)
        to_prev[p, q, 0:edge] = left[a % PART, lo : lo + FAR, :]
        to_prev[p, q, edge : edge + length] = src[lo : lo + FAR, :]
        to_prev[p, q, edge + length :] = right[a % PART, lo : lo + FAR, 0:LANES]
        to_next[p, q, 0:LANES] = left[a % PART, hi : hi + FAR, edge - LANES : edge]
        to_next[p, q, LANES : LANES + length] = src[hi : hi + FAR, :]
        to_next[p, q, LANES + length :] = right[a % PART, hi : hi + FAR, :]


def pack_corner(behind, ahead, to_left, to_right, aux):
    edge = HT * LANES
    length = TILES * LANES
    for k, src in enumerate((behind, ahead)):
        made = near_source(src)
        rows = pl.ds(NEAR * k, NEAR)
        aux[rows, :] = made
        to_left[NARR - 1, rows, :] = made[:, 0:edge]
        to_right[NARR - 1, rows, :] = made[:, length - edge : length]
        for a in range(NARR - 1):
            to_left[a, rows, :] = src[:, 2 * a * edge : (2 * a + 1) * edge]
            to_right[a, rows, :] = src[:, (2 * a + 1) * edge : (2 * a + 2) * edge]


def at(a, x, v=0):
    return PAD + (a * XR + x) * YV + v


def place(dst, a, x, v, value):
    dst[pl.ds(at(a, x, v), value.shape[0], stride=YV), :] = value


def row(ref, a, x):
    return ref[pl.ds(pl.multiple_of(at(a, x), 8), YV), :]


def off(ref, a, x, by):
    return ref[pl.ds(at(a, x) + by, YV), :]


def put(ref, a, x, value):
    ref[pl.ds(pl.multiple_of(at(a, x), 8), YV), :] = value


def fill_sources(wa, ws, spans):
    held = jnp.concatenate([wa[pl.ds(at(0, x), n * YV), :] for x, n in spans], axis=0)
    level = iota(held.shape, 1) % NZ
    held = jnp.where(level < 4, held, 0.0)
    i, j = iota((LANES, 4 * LANES), 0), iota((LANES, 4 * LANES), 1)
    spread = dot(held, (i == (j % LANES) // NZ * NZ + j // LANES).astype(jnp.float32))
    for r in range(2):
        strength = spread[:, r * LANES : (r + 1) * LANES]
        where = spread[:, (2 + r) * LANES : (3 + r) * LANES]
        term = jnp.where(level.astype(jnp.float32) == where, strength, 0.0)
        begin = 0
        for x, n in spans:
            ws[pl.ds(at(r, x), n * YV), :] = term[begin : begin + n * YV]
            begin += n * YV


def kinds(we, wh, wc, wa):
    def same(t):
        return t

    out = [(we, a, same) for a in range(6)]
    out += [(wh, a, lambda t: t * 2.0) for a in range(6)]
    return out + [(wc, 0, lambda t: 0.25 / t), (wa, 0, same)]


class Stepper:
    def __init__(self, waves, we, wh, wc, ws, acc):
        self.waves, self.we, self.wh, self.wc, self.ws, self.acc = waves, we, wh, wc, ws, acc
        lane = iota((YV, LANES), 1)
        self.up_keep = lane % NZ != NZ - 1
        self.down_keep = lane % NZ != 0
        self.first = lane < NZ
        self.last = lane >= LANES - NZ

    def up_z(self, t):
        return jnp.where(self.up_keep, pltpu.roll(t, LANES - 1, 1), 0.0)

    def down_z(self, t):
        return jnp.where(self.down_keep, pltpu.roll(t, 1, 1), 0.0)

    def up_y(self, t, after):
        return pltpu.roll(jnp.where(self.first, after, t), LANES - NZ, 1)

    def down_y(self, t, before):
        return pltpu.roll(jnp.where(self.last, before, t), NZ, 1)

    def magnetic_row(self, r, x):
        we, wh = self.we, self.wh
        ex, ey, ez = (row(we, 3 * r + c, x) for c in range(3))
        hx, hy, hz = (row(wh, 3 * r + c, x) for c in range(3))
        ey_x, ez_x = (row(we, 3 * r + c, x + 1) for c in (1, 2))
        ex_y = self.up_y(ex, off(we, 3 * r, x, 1))
        ez_y = self.up_y(ez, off(we, 3 * r + 2, x, 1))
        hx = hx - ((ez_y - ez) - (self.up_z(ey) - ey))
        hy = hy - ((self.up_z(ex) - ex) - (ez_x - ez))
        hz = hz - ((ey_x - ey) - (ex_y - ex))
        return (hx, hy, hz)

    def electric_row(self, r, x, c, wave):
        we, wh = self.we, self.wh
        hx, hy, hz = (row(wh, 3 * r + k, x) for k in range(3))
        hy_x, hz_x = (row(wh, 3 * r + k, x - 1) for k in (1, 2))
        hx_y = self.down_y(hx, off(wh, 3 * r, x, -1))
        hz_y = self.down_y(hz, off(wh, 3 * r + 2, x, -1))
        ex, ey, ez = (row(we, 3 * r + k, x) for k in range(3))
        ex = ex + c * ((hz - hz_y) - (hy - self.down_z(hy))) + wave * row(self.ws, r, x)
        ey = ey + c * ((hx - self.down_z(hx)) - (hz - hz_x))
        ez = ez + c * ((hy - hy_x) - (hx - hx_y))
        return (ex, ey, ez)

    def magnetic(self, x):
        for r in range(2):
            for k, value in enumerate(self.magnetic_row(r, x)):
                put(self.wh, 3 * r + k, x, value)

    def electric(self, x, wave):
        c = row(self.wc, 0, x)
        f = self.electric_row(0, x, c, wave)
        g = self.electric_row(1, x, c, wave)
        put(self.acc, 0, x, row(self.acc, 0, x) + (f[0] * g[0] + f[1] * g[1] + f[2] * g[2]))
        for k in range(3):
            put(self.we, k, x, f[k])
            put(self.we, 3 + k, x, g[k])

    def edges(self, low, high, count):
        def step(n, _):
            wave = self.waves[n]
            for i in range(count):
                self.magnetic(low + n + i)
                self.magnetic(high - n + i)
            for i in range(count):
                self.electric(low + 1 + n + i, wave)
                self.electric(high - n + i, wave)
            return 0

        lax.fori_loop(0, STEPS, step, 0)

    def inside(self, low, high, begin, end):
        def sweep(one, x, count):
            def group(g, _):
                for i in range(8):
                    one(x + g * 8 + i)
                return 0

            lax.fori_loop(0, count // 8, group, 0)
            for size in (4, 2, 1):
                start = x + count // (2 * size) * (2 * size)

                @pl.when(count % (2 * size) >= size)
                def _(size=size, start=start):
                    for i in range(size):
                        one(start + i)

        def step(n, _):
            wave = self.waves[n]
            sweep(self.magnetic, low + n, high - low - 2 * n)
            sweep(lambda x: self.electric(x, wave), low + 1 + n, high - low - 1 - 2 * n)
            return 0

        lax.fori_loop(begin, end, step, 0)


def run_inside(waves, e, h, eps, aux, left_lo, left_hi, right_lo, right_hi, we, wh, wc, ws, acc, wa):
    own = planes(e, h, eps, aux)
    for n, (dst, a, fix) in enumerate(kinds(we, wh, wc, wa)):
        left, right = ((left_lo, right_lo), (left_hi, right_hi))[n // PART]
        for i in range(ROWS // 8):
            rows = pl.ds(8 * i, 8)
            for j in range(TILES):
                place(dst, a, HALO + 8 * i, HT + j, fix(own[n][rows, pl.ds(j * LANES, LANES)]))
            for j in range(HT):
                cols = pl.ds(j * LANES, LANES)
                place(dst, a, HALO + 8 * i, j, fix(left[n % PART, rows, cols]))
                place(dst, a, HALO + 8 * i, HT + TILES + j, fix(right[n % PART, rows, cols]))
    fill_sources(wa, ws, ((HALO, ROWS),))
    acc[...] = jnp.zeros_like(acc)
    Stepper(waves, we, wh, wc, ws, acc).inside(HALO, HALO + ROWS - 1, 0, CUT)


def run_inside_rest(waves, _e, _h, _c, _s, _t, we, wh, wc, ws, acc):
    Stepper(waves, we, wh, wc, ws, acc).inside(HALO, HALO + ROWS - 1, CUT, STEPS)


def store_rows(we, wh, stage, e_out, h_out, sems, x, count):
    copies = []
    for a in range(6):
        for k, (src, out, scale) in enumerate(((we, e_out, None), (wh, h_out, 0.5))):
            for i in range(count // 8):
                for j in range(TILES):
                    value = src[pl.ds(at(a, HALO + x + 8 * i, HT + j), 8, stride=YV), :]
                    value = value if scale is None else value * scale
                    stage[6 * k + a, pl.ds(8 * i, 8), pl.ds(j * LANES, LANES)] = value
            copy = pltpu.make_async_copy(
                stage.at[6 * k + a], out.at[a // 3, a % 3, pl.ds(x, count), :], sems.at[6 * k + a]
            )
            copy.start()
            copies.append(copy)
    return copies


def run_near(waves, _e, _h, _c, _s, _t, edge_b, edge_a, mid_b, mid_a, corner_l, corner_r, aux_near, e_out, h_out, we, wh, wc, ws, acc, wa, stage, sems):
    edge = HT * LANES
    inner = (TILES - 2 * HT) * LANES

    def near_tile(side, middle, n, j, rows):
        if n == NARR - 1:
            return aux_near[rows, pl.ds(j * LANES, LANES)]
        if HT <= j < TILES - HT:
            return middle[:, pl.ds(n * inner + (j - HT) * LANES, LANES)]
        j = j if j < HT else j - (TILES - 2 * HT)
        return side[:, pl.ds(2 * n * edge + j * LANES, LANES)]

    for k, (side, middle, x) in enumerate(
        ((edge_b, mid_b, FAR), (edge_a, mid_a, HALO + ROWS))
    ):
        rows = pl.ds(NEAR * k, NEAR)
        for n, (dst, a, fix) in enumerate(kinds(we, wh, wc, wa)):
            for j in range(TILES):
                place(dst, a, x, HT + j, fix(near_tile(side, middle, n, j, rows)))
            for j in range(HT):
                cols = pl.ds(j * LANES, LANES)
                place(dst, a, x, j, fix(corner_l[n, rows, cols]))
                place(dst, a, x, HT + TILES + j, fix(corner_r[n, rows, cols]))
    fill_sources(wa, ws, ((FAR, NEAR), (HALO + ROWS, NEAR)))
    Stepper(waves, we, wh, wc, ws, acc).edges(FAR, HALO + ROWS - 1, NEAR)
    for copy in store_rows(we, wh, stage, e_out, h_out, sems, 8, 16):
        copy.wait()


def run_far(
    waves, _e, _h, _c, _s, _t, _x, _y, far_b, far_a, select, marks, e_out, h_out, packed, we, wh, wc, ws, acc, wa, stage_lo, stage_hi, sems
):
    for n, (dst, a, fix) in enumerate(kinds(we, wh, wc, wa)):
        q = pl.ds(FAR * (n % 2), FAR)
        for j in range(FARW):
            cols = pl.ds(j * LANES, LANES)
            place(dst, a, 0, HT - 1 + j, fix(far_b[n // 2, q, cols]))
            place(dst, a, XR - FAR, j, fix(far_a[n // 2, q, cols]))
    fill_sources(wa, ws, ((0, FAR), (XR - FAR, FAR)))
    Stepper(waves, we, wh, wc, ws, acc).edges(0, XR - FAR - 1, FAR)

    stores = store_rows(we, wh, stage_lo, e_out, h_out, sems, 0, 8)
    stores += store_rows(we, wh, stage_hi, e_out, h_out, sems.at[pl.ds(12, 12)], 24, 8)

    i, j = iota((LANES, LANES), 0), iota((LANES, LANES), 1)
    sums = dot(acc[pl.ds(at(0, HALO), ROWS * YV), :], (i // NZ == j % 4).astype(jnp.float32))
    per = BROWS * YV
    p, q = iota((per, LANES), 0), iota((per, LANES), 1)
    half = LANES // BROWS
    keep = (p // YV == q // half) & ((q % half) // 4 == p % YV - HT)
    blocks = jnp.sum(
        jnp.where(keep[None], sums.reshape(ROWS // BROWS, per, LANES), 0.0), axis=1
    ) / (STEPS * NZ)
    packed[...] = dot(select[...], blocks) + marks[...]
    for copy in stores:
        copy.wait()


def collect(received, filter_matrix, out):
    rec = received[...]
    places = rec.shape[0]
    p = lax.broadcasted_iota(jnp.int32, (places, places), 0)
    q = lax.broadcasted_iota(jnp.int32, (places, places), 1)
    pick = (q == (p // 3) * 3 + 2).astype(jnp.float32)
    labels = jnp.dot(pick, rec, precision=HIGH, preferred_element_type=jnp.float32)
    pr = lax.broadcasted_iota(jnp.int32, (places, LANES), 0)
    ln = lax.broadcasted_iota(jnp.int32, (places, LANES), 1)
    label = jnp.sum(jnp.where((ln == pr % 3) & (pr % 3 < 2), labels, 0.0), axis=1, keepdims=True)
    want = lax.broadcasted_iota(jnp.int32, (places, 8), 1) + 1
    choose = (label == want.astype(jnp.float32)).astype(jnp.float32)
    design = lax.dot_general(
        choose, rec, (((0,), (0,)), ((), ())), precision=HIGH, preferred_element_type=jnp.float32
    )
    result = jnp.dot(
        design, filter_matrix[...], precision=HIGH, preferred_element_type=jnp.float32
    )
    out[...] = result[0:DB_DEV]


def call(kernel, out_shape, count, micros, limit=32, **kwargs):
    vmem = pl.BlockSpec(memory_space=pltpu.VMEM)
    outs = tuple(jax.ShapeDtypeStruct(shape, jnp.float32) for shape in out_shape)
    return pl.pallas_call(
        kernel,
        in_specs=kwargs.pop("in_specs", [vmem] * count),
        out_specs=kwargs.pop("out_specs", (vmem,) * len(outs)),
        out_shape=outs,
        compiler_params=pltpu.CompilerParams(vmem_limit_bytes=limit * 1024 * 1024),
        name=kernel.__name__,
        cost_estimate=pl.CostEstimate(
            flops=0, transcendentals=0, bytes_accessed=micros * 3_000_000
        ),
        **kwargs,
    )


def per_device(
    electric,
    magnetic,
    permittivity,
    source_profile,
    source_plane,
    block_owner,
    design_slot,
    filter_matrix,
):
    length = TILES * LANES
    edge = HT * LANES
    raw = (electric, magnetic, permittivity, source_profile, source_plane)
    vmem = pl.BlockSpec(memory_space=pltpu.VMEM)
    smem = pl.BlockSpec(memory_space=pltpu.SMEM)
    hbm = pl.BlockSpec(memory_space=pltpu.HBM)
    raw = tuple(pltpu.with_memory_space_constraint(t, pltpu.HBM) for t in raw)

    def packing(copies):
        return dict(
            in_specs=[hbm] * 5,
            scratch_shapes=[
                pltpu.VMEM(source_profile.shape, jnp.float32),
                pltpu.VMEM(source_plane.shape, jnp.int32),
                pltpu.SemaphoreType.DMA((2 + copies,)),
            ],
        )

    x_edge = (NEAR, (NARR - 1) * 2 * edge + 2 * LANES + EXTRA)
    x_mid = (NEAR, (NARR - 1) * (length - 2 * edge))
    edge_prev, edge_next, mid_prev, mid_next = call(
        pack_near, (x_edge, x_edge, x_mid, x_mid), 5, 2, **packing(6 * (NARR - 1))
    )(*raw)
    edge_prev, edge_next, raw = lax.optimization_barrier((edge_prev, edge_next, raw))
    edge_b = shifted(edge_next, "gx", 1)
    edge_a = shifted(edge_prev, "gx", -1)

    y_own = (PART, ROWS, edge)
    *sides, aux = call(
        pack_side, (y_own,) * 4 + ((ROWS, length),), 5, 3, **packing(2 * (NARR - 1))
    )(*raw)
    side = [shifted(t, "gy", 1) for t in sides[2:]] + [shifted(t, "gy", -1) for t in sides[:2]]

    y_corner = (NARR, 2 * NEAR, edge)
    corner_left, corner_right, aux_near = call(
        pack_corner, (y_corner, y_corner, (2 * NEAR, length)), 2, 2
    )(edge_b, edge_a)
    corner_l = shifted(corner_right, "gy", 1)
    corner_r = shifted(corner_left, "gy", -1)
    corner_l, corner_r, side, mid_prev, mid_next = lax.optimization_barrier(
        (corner_l, corner_r, side, mid_prev, mid_next)
    )
    mid_b = shifted(mid_next, "gx", 1)
    mid_a = shifted(mid_prev, "gx", -1)

    own = (electric, magnetic, permittivity, aux)
    x_far = (NARR // 2, 2 * FAR, FARW * LANES)
    far_prev, far_next = call(pack_far, (x_far, x_far), 8, 2)(*own, *side)
    far_prev, far_next, side = lax.optimization_barrier((far_prev, far_next, side))
    waves = jnp.asarray(
        time_step
        * np.sin(np.arange(1, STEPS + 1).astype(np.float32) * np.float32(omega_source * time_step)),
        jnp.float32,
    )
    field = (2, 3, ROWS, length)
    many = XR * YV
    tail = PAD + YV
    held = tuple((k * many + tail, LANES) for k in (6, 6, 1, 2, 1))
    tags = pltpu.VMEM((many + tail, LANES), jnp.float32)
    state = call(run_inside, held, 9, 30, in_specs=[smem] + [vmem] * 8, scratch_shapes=[tags])(
        waves, *own, *side
    )
    far_prev, far_next, state = lax.optimization_barrier((far_prev, far_next, state))
    far_b = shifted(far_next, "gx", 1)
    far_a = shifted(far_prev, "gx", -1)
    keep = {1 + k: k for k in range(5)}
    state = call(
        run_inside_rest,
        held,
        6,
        1,
        in_specs=[smem] + [vmem] * 5,
        input_output_aliases=keep,
    )(waves, *state)

    count = ROWS // BROWS
    owner = block_owner[0, 0, :, 0]
    slot = design_slot[0, 0, :]
    owners = lax.axis_size("gy")
    index = jnp.arange(count, dtype=jnp.int32)
    earlier = (
        ((owner[:, None] == owner[None, :]) & (index[None, :] < index[:, None]))
        .astype(jnp.int32)
        .sum(1)
    )
    places = jnp.arange(3 * owners, dtype=jnp.int32)
    chosen = (places[:, None] == (owner * 3 + earlier)[None, :]).astype(jnp.float32)
    lane = jnp.arange(LANES, dtype=jnp.int32)
    holder = (places[:, None] == (owner * 3 + 2)[None, :]).astype(jnp.float32)
    named = (lane[None, :] == earlier[:, None]).astype(jnp.float32) * (slot + 1).astype(
        jnp.float32
    )[:, None]
    marks = jnp.dot(holder, named, precision=HIGH)

    copy_sem = pltpu.SemaphoreType.DMA
    state = call(
        run_near,
        (field, field) + held,
        13,
        12,
        in_specs=[smem] + [vmem] * 12,
        out_specs=(hbm,) * 2 + (vmem,) * 5,
        scratch_shapes=[tags, pltpu.VMEM((12, 16, length), jnp.float32), copy_sem((12,))],
        input_output_aliases={1 + k: 2 + k for k in range(5)},
    )(waves, *state, edge_b, edge_a, mid_b, mid_a, corner_l, corner_r, aux_near)
    stage = pltpu.VMEM((12, 8, length), jnp.float32)
    out = call(
        run_far,
        (field, field, (3 * owners, LANES)) + held,
        12,
        8,
        in_specs=[smem] + [vmem] * 5 + [hbm] * 2 + [vmem] * 4,
        out_specs=(hbm,) * 2 + (vmem,) * 6,
        scratch_shapes=[tags, stage, stage, copy_sem((24,))],
        input_output_aliases={6: 0, 7: 1} | {1 + k: 3 + k for k in range(5)},
    )(waves, *state[2:], *state[:2], far_b, far_a, chosen, marks)
    field_e, field_h, packed = out[:3]
    received = lax.all_to_all(
        packed.reshape(owners, 3, LANES), "gy", split_axis=0, concat_axis=0, tiled=True
    )
    (result,) = call(collect, ((DB_DEV, LANES),), 2, 1)(
        received.reshape(3 * owners, LANES), filter_matrix
    )
    return (field_e, field_h, result[None])


def solution(mesh):
    placed = (
        P(None, None, "gx", "gy"),
        P(None, None, "gx", "gy"),
        P("gx", "gy"),
        P(None, "gx", "gy"),
        P(None, "gx"),
        P("gx", "gy", None, None),
        P("gx", "gy", None),
        P(),
    )
    return jax.shard_map(
        per_device,
        mesh=mesh,
        in_specs=placed,
        out_specs=(P(None, None, "gx", "gy"), P(None, None, "gx", "gy"), P("gx", "gy", None)),
        check_vma=False,
    )
```

```python
import functools

import jax
import jax.numpy as jnp
import numpy as np
from jax import lax
from jax.experimental import pallas as pl
from jax.experimental.pallas import tpu as pltpu
from jax.sharding import PartitionSpec as P

NZ = 32
STEPS = 12
BROWS = 2
DB_DEV = 4

time_step = 0.5
omega_source = 1.3

ROWS = 32
TILES = 16
HALO = STEPS
XR = ROWS + 2 * HALO
HT = HALO // 4
YV = 24
PAD = 8
NARR = 14
NEAR = 8
FAR = 4
FARW = TILES + HT + 1
LANES = 128
HIGH = lax.Precision.HIGHEST
PART = NARR // 2
EXTRA = 6 * LANES
CUT = 9


def shifted(array, axis, by):
    count = lax.axis_size(axis)
    return lax.ppermute(array, axis, [(i, (i + by) % count) for i in range(count)])


def dot(a, b):
    return jnp.dot(a, b, precision=HIGH, preferred_element_type=jnp.float32)


def iota(shape, axis):
    return lax.broadcasted_iota(jnp.int32, shape, axis)


def planes(e, h, eps, aux=None):
    out = [e.at[r, c] for r in range(2) for c in range(3)]
    out += [h.at[r, c] for r in range(2) for c in range(3)] + [eps]
    return out + ([] if aux is None else [aux])


def source_tags(profile, plane):
    half = LANES // 2
    c, l = iota((half, LANES), 0), iota((half, LANES), 1)
    strength = dot(profile[0], (l == c).astype(jnp.float32))
    strength = strength + dot(profile[1], (l == c + half).astype(jnp.float32))
    pick = (iota((2, LANES), 0) == iota((2, LANES), 1)).astype(jnp.float32)
    where = lax.dot_general(
        plane[...].astype(jnp.float32), pick, (((0,), (0,)), ((), ())), precision=HIGH, preferred_element_type=jnp.float32
    )
    return strength, where


def source_rows(strength, where):
    length = TILES * LANES
    half = LANES // 2
    c, l = iota((LANES, length), 0), iota((LANES, length), 1)
    spread = ((l // NZ == c % half) & (l % NZ == c // half)).astype(jnp.float32)
    level = iota((strength.shape[0], length), 1) % NZ
    out = dot(strength, spread)
    out = jnp.where(level == 2, where[:, 0:1], out)
    return jnp.where(level == 3, where[:, 1:2], out)


def fetch_tags(profile, plane, pv, lv, sems):
    copies = [
        pltpu.make_async_copy(profile, pv, sems.at[0]),
        pltpu.make_async_copy(plane, lv, sems.at[1]),
    ]
    for copy in copies:
        copy.start()
    return copies


def pack_side(e, h, eps, profile, plane, left_lo, left_hi, right_lo, right_hi, aux, pv, lv, sems):
    edge = HT * LANES
    length = TILES * LANES
    tags = fetch_tags(profile, plane, pv, lv, sems)
    copies = []
    sides = (((left_lo, left_hi), 0), ((right_lo, right_hi), length - edge))
    for parts, begin in sides:
        for a, src in enumerate(planes(e, h, eps)):
            copies.append(
                pltpu.make_async_copy(
                    src.at[:, pl.ds(begin, edge)],
                    parts[a // PART].at[a % PART],
                    sems.at[2 + len(copies)],
                )
            )
            copies[-1].start()
    for copy in tags:
        copy.wait()
    made = source_rows(*source_tags(pv, lv))
    aux[...] = made
    left_hi[PART - 1] = made[:, 0:edge]
    right_hi[PART - 1] = made[:, length - edge : length]
    for copy in copies:
        copy.wait()


def pack_near(e, h, eps, profile, plane, edge_p, edge_n, mid_p, mid_n, pv, lv, sems):
    edge = HT * LANES
    length = TILES * LANES
    inner = length - 2 * edge
    tags = fetch_tags(profile, plane, pv, lv, sems)
    copies = []
    for x, side, middle in ((0, edge_p, mid_p), (ROWS - NEAR, edge_n, mid_n)):
        for a, src in enumerate(planes(e, h, eps)):
            for part, begin, size, to in (
                (side, 0, edge, 2 * a * edge),
                (side, length - edge, edge, (2 * a + 1) * edge),
                (middle, edge, inner, a * inner),
            ):
                copies.append(
                    pltpu.make_async_copy(
                        src.at[pl.ds(x, NEAR), pl.ds(begin, size)],
                        part.at[:, pl.ds(to, size)],
                        sems.at[2 + len(copies)],
                    )
                )
                copies[-1].start()
    for copy in tags:
        copy.wait()
    for k, tag in enumerate(source_tags(pv, lv)):
        cols = pl.ds((NARR - 1) * 2 * edge + k * LANES, LANES)
        edge_p[:, cols] = tag[0:NEAR, :]
        edge_n[:, cols] = tag[ROWS - NEAR : ROWS, :]
    for copy in copies:
        copy.wait()


def near_source(ref):
    base = (NARR - 1) * 2 * HT * LANES
    return source_rows(ref[:, base : base + LANES], ref[:, base + LANES : base + 2 * LANES])


def pack_far(e, h, eps, aux, left_lo, left_hi, right_lo, right_hi, to_prev, to_next):
    edge = HT * LANES
    length = TILES * LANES
    lo, hi = NEAR, ROWS - NEAR - FAR
    for a, src in enumerate(planes(e, h, eps, aux)):
        left, right = ((left_lo, right_lo), (left_hi, right_hi))[a // PART]
        p, q = a // 2, pl.ds(FAR * (a % 2), FAR)
        to_prev[p, q, 0:edge] = left[a % PART, lo : lo + FAR, :]
        to_prev[p, q, edge : edge + length] = src[lo : lo + FAR, :]
        to_prev[p, q, edge + length :] = right[a % PART, lo : lo + FAR, 0:LANES]
        to_next[p, q, 0:LANES] = left[a % PART, hi : hi + FAR, edge - LANES : edge]
        to_next[p, q, LANES : LANES + length] = src[hi : hi + FAR, :]
        to_next[p, q, LANES + length :] = right[a % PART, hi : hi + FAR, :]


def pack_corner(behind, ahead, to_left, to_right, aux):
    edge = HT * LANES
    length = TILES * LANES
    for k, src in enumerate((behind, ahead)):
        made = near_source(src)
        rows = pl.ds(NEAR * k, NEAR)
        aux[rows, :] = made
        to_left[NARR - 1, rows, :] = made[:, 0:edge]
        to_right[NARR - 1, rows, :] = made[:, length - edge : length]
        for a in range(NARR - 1):
            to_left[a, rows, :] = src[:, 2 * a * edge : (2 * a + 1) * edge]
            to_right[a, rows, :] = src[:, (2 * a + 1) * edge : (2 * a + 2) * edge]


def at(a, x, v=0):
    return PAD + (a * XR + x) * YV + v


def place(dst, a, x, v, value):
    dst[pl.ds(at(a, x, v), value.shape[0], stride=YV), :] = value


def row(ref, a, x):
    return ref[pl.ds(pl.multiple_of(at(a, x), 8), YV), :]


def off(ref, a, x, by):
    return ref[pl.ds(at(a, x) + by, YV), :]


def put(ref, a, x, value):
    ref[pl.ds(pl.multiple_of(at(a, x), 8), YV), :] = value


def fill_sources(wa, ws, spans):
    held = jnp.concatenate([wa[pl.ds(at(0, x), n * YV), :] for x, n in spans], axis=0)
    level = iota(held.shape, 1) % NZ
    held = jnp.where(level < 4, held, 0.0)
    i, j = iota((LANES, 4 * LANES), 0), iota((LANES, 4 * LANES), 1)
    spread = dot(held, (i == (j % LANES) // NZ * NZ + j // LANES).astype(jnp.float32))
    for r in range(2):
        strength = spread[:, r * LANES : (r + 1) * LANES]
        where = spread[:, (2 + r) * LANES : (3 + r) * LANES]
        term = jnp.where(level.astype(jnp.float32) == where, strength, 0.0)
        begin = 0
        for x, n in spans:
            ws[pl.ds(at(r, x), n * YV), :] = term[begin : begin + n * YV]
            begin += n * YV


def kinds(we, wh, wc, wa):
    def same(t):
        return t

    out = [(we, a, same) for a in range(6)]
    out += [(wh, a, lambda t: t * 2.0) for a in range(6)]
    return out + [(wc, 0, lambda t: 0.25 / t), (wa, 0, same)]


class Stepper:
    def __init__(self, waves, we, wh, wc, ws, acc):
        self.waves, self.we, self.wh, self.wc, self.ws, self.acc = waves, we, wh, wc, ws, acc
        lane = iota((YV, LANES), 1)
        self.up_keep = lane % NZ != NZ - 1
        self.down_keep = lane % NZ != 0
        self.first = lane < NZ
        self.last = lane >= LANES - NZ

    def up_z(self, t):
        return jnp.where(self.up_keep, pltpu.roll(t, LANES - 1, 1), 0.0)

    def down_z(self, t):
        return jnp.where(self.down_keep, pltpu.roll(t, 1, 1), 0.0)

    def up_y(self, t, after):
        return pltpu.roll(jnp.where(self.first, after, t), LANES - NZ, 1)

    def down_y(self, t, before):
        return pltpu.roll(jnp.where(self.last, before, t), NZ, 1)

    def magnetic_row(self, r, x):
        we, wh = self.we, self.wh
        ex, ey, ez = (row(we, 3 * r + c, x) for c in range(3))
        hx, hy, hz = (row(wh, 3 * r + c, x) for c in range(3))
        ey_x, ez_x = (row(we, 3 * r + c, x + 1) for c in (1, 2))
        ex_y = self.up_y(ex, off(we, 3 * r, x, 1))
        ez_y = self.up_y(ez, off(we, 3 * r + 2, x, 1))
        hx = hx - ((ez_y - ez) - (self.up_z(ey) - ey))
        hy = hy - ((self.up_z(ex) - ex) - (ez_x - ez))
        hz = hz - ((ey_x - ey) - (ex_y - ex))
        return (hx, hy, hz)

    def electric_row(self, r, x, c, wave):
        we, wh = self.we, self.wh
        hx, hy, hz = (row(wh, 3 * r + k, x) for k in range(3))
        hy_x, hz_x = (row(wh, 3 * r + k, x - 1) for k in (1, 2))
        hx_y = self.down_y(hx, off(wh, 3 * r, x, -1))
        hz_y = self.down_y(hz, off(wh, 3 * r + 2, x, -1))
        ex, ey, ez = (row(we, 3 * r + k, x) for k in range(3))
        ex = ex + c * ((hz - hz_y) - (hy - self.down_z(hy))) + wave * row(self.ws, r, x)
        ey = ey + c * ((hx - self.down_z(hx)) - (hz - hz_x))
        ez = ez + c * ((hy - hy_x) - (hx - hx_y))
        return (ex, ey, ez)

    def magnetic(self, x):
        for r in range(2):
            for k, value in enumerate(self.magnetic_row(r, x)):
                put(self.wh, 3 * r + k, x, value)

    def electric(self, x, wave):
        c = row(self.wc, 0, x)
        f = self.electric_row(0, x, c, wave)
        g = self.electric_row(1, x, c, wave)
        put(self.acc, 0, x, row(self.acc, 0, x) + (f[0] * g[0] + f[1] * g[1] + f[2] * g[2]))
        for k in range(3):
            put(self.we, k, x, f[k])
            put(self.we, 3 + k, x, g[k])

    def edges(self, low, high, count):
        def step(n, _):
            wave = self.waves[n]
            for i in range(count):
                self.magnetic(low + n + i)
                self.magnetic(high - n + i)
            for i in range(count):
                self.electric(low + 1 + n + i, wave)
                self.electric(high - n + i, wave)
            return 0

        lax.fori_loop(0, STEPS, step, 0)

    def inside(self, low, high, begin, end):
        def sweep(one, x, count):
            def group(g, _):
                for i in range(8):
                    one(x + g * 8 + i)
                return 0

            lax.fori_loop(0, count // 8, group, 0)
            start = x + count // 8 * 8
            for size in range(1, 8):

                @pl.when(count % 8 == size)
                def _(size=size):
                    for i in range(size):
                        one(start + i)

        def step(n, _):
            wave = self.waves[n]
            sweep(self.magnetic, low + n, high - low - 2 * n)
            sweep(lambda x: self.electric(x, wave), low + 1 + n, high - low - 1 - 2 * n)
            return 0

        lax.fori_loop(begin, end, step, 0)


def run_inside(waves, e, h, eps, aux, left_lo, left_hi, right_lo, right_hi, we, wh, wc, ws, acc, wa):
    own = planes(e, h, eps, aux)
    for n, (dst, a, fix) in enumerate(kinds(we, wh, wc, wa)):
        left, right = ((left_lo, right_lo), (left_hi, right_hi))[n // PART]
        for i in range(ROWS // 8):
            rows = pl.ds(8 * i, 8)
            for j in range(TILES):
                place(dst, a, HALO + 8 * i, HT + j, fix(own[n][rows, pl.ds(j * LANES, LANES)]))
            for j in range(HT):
                cols = pl.ds(j * LANES, LANES)
                place(dst, a, HALO + 8 * i, j, fix(left[n % PART, rows, cols]))
                place(dst, a, HALO + 8 * i, HT + TILES + j, fix(right[n % PART, rows, cols]))
    fill_sources(wa, ws, ((HALO, ROWS),))
    acc[...] = jnp.zeros_like(acc)
    Stepper(waves, we, wh, wc, ws, acc).inside(HALO, HALO + ROWS - 1, 0, CUT)


def run_inside_rest(waves, _e, _h, _c, _s, _t, we, wh, wc, ws, acc):
    Stepper(waves, we, wh, wc, ws, acc).inside(HALO, HALO + ROWS - 1, CUT, STEPS)


def store_rows(we, wh, stage, e_out, h_out, sems, x, count):
    copies = []
    for a in range(6):
        for k, (src, out, scale) in enumerate(((we, e_out, None), (wh, h_out, 0.5))):
            for i in range(count // 8):
                for j in range(TILES):
                    value = src[pl.ds(at(a, HALO + x + 8 * i, HT + j), 8, stride=YV), :]
                    value = value if scale is None else value * scale
                    stage[6 * k + a, pl.ds(8 * i, 8), pl.ds(j * LANES, LANES)] = value
            copy = pltpu.make_async_copy(
                stage.at[6 * k + a], out.at[a // 3, a % 3, pl.ds(x, count), :], sems.at[6 * k + a]
            )
            copy.start()
            copies.append(copy)
    return copies


def run_near(waves, _e, _h, _c, _s, _t, edge_b, edge_a, mid_b, mid_a, corner_l, corner_r, aux_near, e_out, h_out, we, wh, wc, ws, acc, wa, stage, sems):
    edge = HT * LANES
    inner = (TILES - 2 * HT) * LANES

    def near_tile(side, middle, n, j, rows):
        if n == NARR - 1:
            return aux_near[rows, pl.ds(j * LANES, LANES)]
        if HT <= j < TILES - HT:
            return middle[:, pl.ds(n * inner + (j - HT) * LANES, LANES)]
        j = j if j < HT else j - (TILES - 2 * HT)
        return side[:, pl.ds(2 * n * edge + j * LANES, LANES)]

    for k, (side, middle, x) in enumerate(
        ((edge_b, mid_b, FAR), (edge_a, mid_a, HALO + ROWS))
    ):
        rows = pl.ds(NEAR * k, NEAR)
        for n, (dst, a, fix) in enumerate(kinds(we, wh, wc, wa)):
            for j in range(TILES):
                place(dst, a, x, HT + j, fix(near_tile(side, middle, n, j, rows)))
            for j in range(HT):
                cols = pl.ds(j * LANES, LANES)
                place(dst, a, x, j, fix(corner_l[n, rows, cols]))
                place(dst, a, x, HT + TILES + j, fix(corner_r[n, rows, cols]))
    fill_sources(wa, ws, ((FAR, NEAR), (HALO + ROWS, NEAR)))
    Stepper(waves, we, wh, wc, ws, acc).edges(FAR, HALO + ROWS - 1, NEAR)
    for copy in store_rows(we, wh, stage, e_out, h_out, sems, 8, 16):
        copy.wait()


def run_far(
    waves, _e, _h, _c, _s, _t, _x, _y, far_b, far_a, select, marks, e_out, h_out, packed, we, wh, wc, ws, acc, wa, stage_lo, stage_hi, sems
):
    for n, (dst, a, fix) in enumerate(kinds(we, wh, wc, wa)):
        q = pl.ds(FAR * (n % 2), FAR)
        for j in range(FARW):
            cols = pl.ds(j * LANES, LANES)
            place(dst, a, 0, HT - 1 + j, fix(far_b[n // 2, q, cols]))
            place(dst, a, XR - FAR, j, fix(far_a[n // 2, q, cols]))
    fill_sources(wa, ws, ((0, FAR), (XR - FAR, FAR)))
    Stepper(waves, we, wh, wc, ws, acc).edges(0, XR - FAR - 1, FAR)

    stores = store_rows(we, wh, stage_lo, e_out, h_out, sems, 0, 8)
    stores += store_rows(we, wh, stage_hi, e_out, h_out, sems.at[pl.ds(12, 12)], 24, 8)

    i, j = iota((LANES, LANES), 0), iota((LANES, LANES), 1)
    sums = dot(acc[pl.ds(at(0, HALO), ROWS * YV), :], (i // NZ == j % 4).astype(jnp.float32))
    per = BROWS * YV
    p, q = iota((per, LANES), 0), iota((per, LANES), 1)
    half = LANES // BROWS
    keep = (p // YV == q // half) & ((q % half) // 4 == p % YV - HT)
    blocks = jnp.sum(
        jnp.where(keep[None], sums.reshape(ROWS // BROWS, per, LANES), 0.0), axis=1
    ) / (STEPS * NZ)
    packed[...] = dot(select[...], blocks) + marks[...]
    for copy in stores:
        copy.wait()


def collect(received, filter_matrix, out):
    rec = received[...]
    places = rec.shape[0]
    p = lax.broadcasted_iota(jnp.int32, (places, places), 0)
    q = lax.broadcasted_iota(jnp.int32, (places, places), 1)
    pick = (q == (p // 3) * 3 + 2).astype(jnp.float32)
    labels = jnp.dot(pick, rec, precision=HIGH, preferred_element_type=jnp.float32)
    pr = lax.broadcasted_iota(jnp.int32, (places, LANES), 0)
    ln = lax.broadcasted_iota(jnp.int32, (places, LANES), 1)
    label = jnp.sum(jnp.where((ln == pr % 3) & (pr % 3 < 2), labels, 0.0), axis=1, keepdims=True)
    want = lax.broadcasted_iota(jnp.int32, (places, 8), 1) + 1
    choose = (label == want.astype(jnp.float32)).astype(jnp.float32)
    design = lax.dot_general(
        choose, rec, (((0,), (0,)), ((), ())), precision=HIGH, preferred_element_type=jnp.float32
    )
    result = jnp.dot(
        design, filter_matrix[...], precision=HIGH, preferred_element_type=jnp.float32
    )
    out[...] = result[0:DB_DEV]


def call(kernel, out_shape, count, micros, limit=32, **kwargs):
    vmem = pl.BlockSpec(memory_space=pltpu.VMEM)
    outs = tuple(jax.ShapeDtypeStruct(shape, jnp.float32) for shape in out_shape)
    return pl.pallas_call(
        kernel,
        in_specs=kwargs.pop("in_specs", [vmem] * count),
        out_specs=kwargs.pop("out_specs", (vmem,) * len(outs)),
        out_shape=outs,
        compiler_params=pltpu.CompilerParams(vmem_limit_bytes=limit * 1024 * 1024),
        name=kernel.__name__,
        cost_estimate=pl.CostEstimate(
            flops=0, transcendentals=0, bytes_accessed=micros * 3_000_000
        ),
        **kwargs,
    )


def per_device(
    electric,
    magnetic,
    permittivity,
    source_profile,
    source_plane,
    block_owner,
    design_slot,
    filter_matrix,
):
    length = TILES * LANES
    edge = HT * LANES
    raw = (electric, magnetic, permittivity, source_profile, source_plane)
    vmem = pl.BlockSpec(memory_space=pltpu.VMEM)
    smem = pl.BlockSpec(memory_space=pltpu.SMEM)
    hbm = pl.BlockSpec(memory_space=pltpu.HBM)
    raw = tuple(pltpu.with_memory_space_constraint(t, pltpu.HBM) for t in raw)

    def packing(copies):
        return dict(
            in_specs=[hbm] * 5,
            scratch_shapes=[
                pltpu.VMEM(source_profile.shape, jnp.float32),
                pltpu.VMEM(source_plane.shape, jnp.int32),
                pltpu.SemaphoreType.DMA((2 + copies,)),
            ],
        )

    x_edge = (NEAR, (NARR - 1) * 2 * edge + 2 * LANES + EXTRA)
    x_mid = (NEAR, (NARR - 1) * (length - 2 * edge))
    edge_prev, edge_next, mid_prev, mid_next = call(
        pack_near, (x_edge, x_edge, x_mid, x_mid), 5, 2, **packing(6 * (NARR - 1))
    )(*raw)
    edge_prev, edge_next, raw = lax.optimization_barrier((edge_prev, edge_next, raw))
    edge_b = shifted(edge_next, "gx", 1)
    edge_a = shifted(edge_prev, "gx", -1)

    y_own = (PART, ROWS, edge)
    *sides, aux = call(
        pack_side, (y_own,) * 4 + ((ROWS, length),), 5, 3, **packing(2 * (NARR - 1))
    )(*raw)
    side = [shifted(t, "gy", 1) for t in sides[2:]] + [shifted(t, "gy", -1) for t in sides[:2]]

    y_corner = (NARR, 2 * NEAR, edge)
    corner_left, corner_right, aux_near = call(
        pack_corner, (y_corner, y_corner, (2 * NEAR, length)), 2, 2
    )(edge_b, edge_a)
    corner_l = shifted(corner_right, "gy", 1)
    corner_r = shifted(corner_left, "gy", -1)
    corner_l, corner_r, side, mid_prev, mid_next = lax.optimization_barrier(
        (corner_l, corner_r, side, mid_prev, mid_next)
    )
    mid_b = shifted(mid_next, "gx", 1)
    mid_a = shifted(mid_prev, "gx", -1)

    own = (electric, magnetic, permittivity, aux)
    x_far = (NARR // 2, 2 * FAR, FARW * LANES)
    far_prev, far_next = call(pack_far, (x_far, x_far), 8, 2)(*own, *side)
    far_prev, far_next, side = lax.optimization_barrier((far_prev, far_next, side))
    waves = jnp.asarray(
        time_step
        * np.sin(np.arange(1, STEPS + 1).astype(np.float32) * np.float32(omega_source * time_step)),
        jnp.float32,
    )
    field = (2, 3, ROWS, length)
    many = XR * YV
    tail = PAD + YV
    held = tuple((k * many + tail, LANES) for k in (6, 6, 1, 2, 1))
    tags = pltpu.VMEM((many + tail, LANES), jnp.float32)
    state = call(run_inside, held, 9, 30, in_specs=[smem] + [vmem] * 8, scratch_shapes=[tags])(
        waves, *own, *side
    )
    far_prev, far_next, state = lax.optimization_barrier((far_prev, far_next, state))
    far_b = shifted(far_next, "gx", 1)
    far_a = shifted(far_prev, "gx", -1)
    keep = {1 + k: k for k in range(5)}
    state = call(
        run_inside_rest,
        held,
        6,
        1,
        in_specs=[smem] + [vmem] * 5,
        input_output_aliases=keep,
    )(waves, *state)

    count = ROWS // BROWS
    owner = block_owner[0, 0, :, 0]
    slot = design_slot[0, 0, :]
    owners = lax.axis_size("gy")
    index = jnp.arange(count, dtype=jnp.int32)
    earlier = (
        ((owner[:, None] == owner[None, :]) & (index[None, :] < index[:, None]))
        .astype(jnp.int32)
        .sum(1)
    )
    places = jnp.arange(3 * owners, dtype=jnp.int32)
    chosen = (places[:, None] == (owner * 3 + earlier)[None, :]).astype(jnp.float32)
    lane = jnp.arange(LANES, dtype=jnp.int32)
    holder = (places[:, None] == (owner * 3 + 2)[None, :]).astype(jnp.float32)
    named = (lane[None, :] == earlier[:, None]).astype(jnp.float32) * (slot + 1).astype(
        jnp.float32
    )[:, None]
    marks = jnp.dot(holder, named, precision=HIGH)

    copy_sem = pltpu.SemaphoreType.DMA
    state = call(
        run_near,
        (field, field) + held,
        13,
        12,
        in_specs=[smem] + [vmem] * 12,
        out_specs=(hbm,) * 2 + (vmem,) * 5,
        scratch_shapes=[tags, pltpu.VMEM((12, 16, length), jnp.float32), copy_sem((12,))],
        input_output_aliases={1 + k: 2 + k for k in range(5)},
    )(waves, *state, edge_b, edge_a, mid_b, mid_a, corner_l, corner_r, aux_near)
    stage = pltpu.VMEM((12, 8, length), jnp.float32)
    out = call(
        run_far,
        (field, field, (3 * owners, LANES)) + held,
        12,
        8,
        in_specs=[smem] + [vmem] * 5 + [hbm] * 2 + [vmem] * 4,
        out_specs=(hbm,) * 2 + (vmem,) * 6,
        scratch_shapes=[tags, stage, stage, copy_sem((24,))],
        input_output_aliases={6: 0, 7: 1} | {1 + k: 3 + k for k in range(5)},
    )(waves, *state[2:], *state[:2], far_b, far_a, chosen, marks)
    field_e, field_h, packed = out[:3]
    received = lax.all_to_all(
        packed.reshape(owners, 3, LANES), "gy", split_axis=0, concat_axis=0, tiled=True
    )
    (result,) = call(collect, ((DB_DEV, LANES),), 2, 1)(
        received.reshape(3 * owners, LANES), filter_matrix
    )
    return (field_e, field_h, result[None])


def solution(mesh):
    placed = (
        P(None, None, "gx", "gy"),
        P(None, None, "gx", "gy"),
        P("gx", "gy"),
        P(None, "gx", "gy"),
        P(None, "gx"),
        P("gx", "gy", None, None),
        P("gx", "gy", None),
        P(),
    )
    return jax.shard_map(
        per_device,
        mesh=mesh,
        in_specs=placed,
        out_specs=(P(None, None, "gx", "gy"), P(None, None, "gx", "gy"), P("gx", "gy", None)),
        check_vma=False,
    )
```
